32 devices in a mesh: shard: 8 (over y, x, core), rep: 4 (over z).
Axes of the slice: x: 2, y: 2, z: 4, core: 2. Of those that a mesh axis runs over, the one named last changes fastest.
Arguments:
- inputs: bfloat16 [32, 1024, 768], P(('shard', 'rep')), may hold values from -6 to 6
- seq_lens: int32 [32], P(('shard', 'rep')), may hold values from 1 to 1024, 20480 in all
- pass_idx: int32 [32], P(('shard', 'rep')), may hold values from 0 to 4
- pass_table: bfloat16 [5, 768], P(None, 'shard'), may hold values from -3 to 3
- gain_attn: bfloat16 [768], P('shard'), may hold values from 0.099609375 to 1.8984375
- w_qkv: bfloat16 [768, 2304], P('shard'), may hold values from -0.21875 to 0.21875
- w_out: bfloat16 [768, 768], P('shard'), may hold values from -1.75 to 1.75
- gain_mlp: bfloat16 [768], P('shard'), may hold values from 0.099609375 to 1.8984375
- w_up: bfloat16 [768, 3072], P('shard'), may hold values from -0.21875 to 0.21875
- w_down: bfloat16 [3072, 768], P('shard'), may hold values from -0.109375 to 0.109375
- cotangent: bfloat16 [32, 1024, 768], P(('shard', 'rep')), may hold values from -6 to 6
Outputs:
- outputs: bfloat16 [32, 1024, 768], P(('shard', 'rep'))
- grad_input: float32 [32, 1024, 768], P(('shard', 'rep'))
- grad_table: float32 [5, 768], P(None, 'shard')
- grad_gain_attn: float32 [768], P('shard')
- grad_qkv: float32 [768, 2304], P('shard')
- grad_out: float32 [768, 768], P('shard')
- grad_gain_mlp: float32 [768], P('shard')
- grad_up: float32 [768, 3072], P('shard')
- grad_down: float32 [3072, 768], P('shard')
The draws below stay inside these ranges and needn't reach their ends.
Inputs may be any that keep to these rules, and one draw needn't show every extreme that they name: Tokens from position seq_lens of a slot on are padding; in every draw some slot holds exactly 1024 real tokens. `pass_idx`: the repetition of the block that a slot is in.
All inputs are finite; a program needn't handle non-finite values. No bound on the sum of `seq_lens` on one device may be relied on, other than what follows from the above.
Results may differ from the reference program's by a relative error of at most 0.011.
Values may be sent and summed in bfloat16 or wider, within the bound.
A program may use at most 192 MiB of HBM per device.

```python
import math
import jax
import jax.numpy as jnp
import numpy as np
from jax import lax

D = 768
HEADS = 12
HEAD_DIM = 64
FF = 3072
PASSES = 5
LEN = 1024
SEQS = 32


def plant(values, stream_key, least, largest):
    index_at = [jax.random.randint(jax.random.fold_in(stream_key, axis), (), 0, length) for axis, length in enumerate(values.shape)]
    widest = values.shape.index(max(values.shape))
    beside = index_at[:widest] + [(index_at[widest] + 1) % values.shape[widest]] + index_at[widest + 1:]
    return values.at[tuple(index_at)].set(least).at[tuple(beside)].set(largest)


def levels(own_key, dims, cuts, least, largest):
    def one(dim, parts):
        draws = jax.random.uniform(jax.random.fold_in(jax.random.fold_in(own_key, 6), dim), (parts,), jnp.float32, least / len(cuts), largest / len(cuts))
        return jnp.repeat(jnp.exp(draws), dims[dim] // parts).reshape((-1,) + (1,) * (len(dims) - dim - 1))

    gain = one(*cuts[0])
    for cut in cuts[1:]:
        gain = gain * one(*cut)
    return gain


def split_up(number_of, total, most, lean):
    weights = [(1 << 20) // math.isqrt(rank ** lean) + 1 for rank in range(2, number_of + 1)]
    rest, holding = total - most - (number_of - 1), [1] * (number_of - 1)
    while rest > 0:
        free = [i for i in range(number_of - 1) if holding[i] < most]
        mass, left = sum([weights[i] for i in free]), rest
        for i in free:
            addition = min(most - holding[i], max(1, left * weights[i] // mass), rest)
            holding[i] = holding[i] + addition
            rest = rest - addition
    return np.array([most] + holding)


def uneven_parts(rng, number_of, total, reach, lean):
    if number_of == 2:
        one = jax.random.randint(rng, (), max(1, total - reach), min(reach, total - 1) + 1)
        return jnp.stack([one, total - one])
    sizes = jnp.asarray(split_up(number_of, total, reach, lean), jnp.int32)
    couples = (number_of - 1) // 2
    giver, taker = sizes[1:1 + 2 * couples:2], sizes[2:2 + 2 * couples:2]
    room = jnp.minimum(giver - 1, reach - taker)
    shifted = jax.random.randint(jax.random.fold_in(rng, 1), (couples,), 0, 1 << 20) % (room + 1)
    sizes = sizes.at[1:1 + 2 * couples:2].set(giver - shifted).at[2:2 + 2 * couples:2].set(taker + shifted)
    return sizes[jax.random.permutation(jax.random.fold_in(rng, 2), number_of)]


def bell_draw(stream_key, dims, deviation, reach, cuts=(), kind=jnp.bfloat16):
    values = deviation * jax.random.normal(stream_key, dims, jnp.float32)
    if cuts:
        values = values * levels(stream_key, dims, cuts, -0.22, 0.18)
    return jnp.clip(values, -reach, reach).astype(kind)


def setup_inputs(seed: int = 0) -> dict:
    key_of = jax.random.split(jax.random.key(seed), 12)
    inputs = bell_draw(key_of[0], (SEQS, LEN, D), 1.0, 6.0, ((0, 32),))
    seq_lens = uneven_parts(key_of[1], SEQS, SEQS * LEN * 5 // 8, LEN, 2).astype(jnp.int32)
    pass_idx = plant(jax.random.randint(key_of[2], (SEQS,), 0, PASSES), jax.random.fold_in(key_of[2], 1), 0, PASSES - 1).astype(jnp.int32)
    pass_table = bell_draw(key_of[3], (PASSES, D), 0.5, 3.0, ((1, 8),))
    gain_attn = jnp.clip(1.0 + 0.18 * jax.random.normal(key_of[4], (D,), jnp.float32), 0.099609375, 1.8984375).astype(jnp.bfloat16)
    w_qkv = bell_draw(key_of[5], (D, 3 * D), D ** -0.5, 0.21875, ((0, 8),))
    w_out = bell_draw(key_of[6], (D, D), (max(D * 16 // LEN, 1)) ** -0.5, 1.75, ((0, 8),))
    gain_mlp = jnp.clip(1.0 + 0.18 * jax.random.normal(key_of[7], (D,), jnp.float32), 0.099609375, 1.8984375).astype(jnp.bfloat16)
    w_up = bell_draw(key_of[8], (D, FF), D ** -0.5, 0.21875, ((0, 8),))
    w_down = bell_draw(key_of[9], (FF, D), FF ** -0.5, 0.109375, ((0, 8),))
    cotangent = bell_draw(key_of[10], (SEQS, LEN, D), 1.0, 6.0, ((0, 32),))
    return dict(inputs=inputs, seq_lens=seq_lens, pass_idx=pass_idx, pass_table=pass_table, gain_attn=gain_attn, w_qkv=w_qkv, w_out=w_out, gain_mlp=gain_mlp, w_up=w_up, w_down=w_down, cotangent=cotangent)


EPSILON = 1e-05
MASKED = -1e+30
HIGHEST = lax.Precision.HIGHEST

@jax.custom_vjp
def low(v):
    return lax.optimization_barrier(v.astype(jnp.bfloat16)).astype(jnp.float32)

@jax.custom_vjp
def low_back(v):
    return v

def low_keep(v):
    return (low(v), None)

def low_pass(kept, grad):
    return (grad,)

def back_keep(v):
    return (v, None)

def back_low(kept, grad):
    return (low(grad),)
low.defvjp(low_keep, low_pass)
low_back.defvjp(back_keep, back_low)

def layer_norm(values, scaling):
    average = lax.optimization_barrier(jnp.mean(values, axis=-1, keepdims=True))
    centred = values - average
    variance = lax.optimization_barrier(jnp.mean(centred * centred, axis=-1, keepdims=True))
    return centred * lax.rsqrt(variance + EPSILON) * scaling

def gelu_curve(values):
    inside_term = math.sqrt(2.0 / math.pi) * (values + 0.044715 * values * values * values)
    return 0.5 * values * (1.0 + jnp.tanh(inside_term))

def attend(queries, all_keys, all_values, seq_length):
    block_rows = min(512, LEN)
    score_scale = HEAD_DIM ** (-0.5)
    key_places = jnp.arange(LEN, dtype=jnp.int32)

    def one_block(block_index):
        first_row = (block_index * block_rows).astype(jnp.int32)
        query_block = lax.dynamic_slice_in_dim(queries, first_row, block_rows, 0)
        scores = jnp.einsum('qhd,khd->hqk', query_block, all_keys, precision=HIGHEST) * score_scale
        scores = low_back(scores)
        query_places = first_row + jnp.arange(block_rows, dtype=jnp.int32)
        allowed = (key_places[None, :] <= query_places[:, None]) & (key_places[None, :] < seq_length)
        scores = jnp.where(allowed[None], scores, MASKED)
        row_top = lax.optimization_barrier(jnp.max(scores, axis=-1, keepdims=True))
        weights = jnp.exp(scores - row_top)
        shares = low(weights / lax.optimization_barrier(jnp.sum(weights, axis=-1, keepdims=True)))
        return jnp.einsum('hqk,khd->qhd', shares, all_values, precision=HIGHEST)
    blocks = lax.map(jax.checkpoint(one_block), jnp.arange(LEN // block_rows, dtype=jnp.int32))
    return blocks.reshape(LEN, HEADS * HEAD_DIM)

def forward(inputs, pass_rows, gain_attn, w_qkv, w_out, gain_mlp, w_up, w_down, passes, lengths):
    members = inputs.shape[0]
    chosen = (passes[:, None] == jnp.arange(PASSES, dtype=jnp.int32)[None, :]).astype(jnp.float32)
    entered = inputs + jnp.dot(chosen, pass_rows, precision=HIGHEST)[:, None, :]
    normed = low(layer_norm(entered, gain_attn))
    joined = jnp.einsum('gtd,de->gte', normed, w_qkv, precision=HIGHEST)
    joined = low(low_back(joined)).reshape(members, LEN, 3, HEADS, HEAD_DIM)
    attended = jax.vmap(attend)(joined[:, :, 0], joined[:, :, 1], joined[:, :, 2], lengths)
    attended = low(low_back(attended))
    branch = low_back(jnp.einsum('gte,ed->gtd', attended, w_out, precision=HIGHEST))
    hidden = entered + branch
    second = low(layer_norm(hidden, gain_mlp))
    rising = low_back(jnp.einsum('gtd,df->gtf', second, w_up, precision=HIGHEST))
    active = low(gelu_curve(rising))
    return hidden + jnp.einsum('gtf,fd->gtd', active, w_down, precision=HIGHEST)

def reference(inputs, seq_lens, pass_idx, pass_table, gain_attn, w_qkv, w_out, gain_mlp, w_up, w_down, cotangent):
    floats = tuple((element.astype(jnp.float32) for element in (pass_table, gain_attn, w_qkv, w_out, gain_mlp, w_up, w_down)))
    members = math.gcd(SEQS, max(1, 4096 // LEN))
    steps_count = SEQS // members

    def regroup(array):
        return array.reshape((steps_count, members) + array.shape[1:])

    def advance(running, pieces):
        block_in, block_lens, block_passes, block_cot = pieces

        def locally(inputs_now, *weights):
            return forward(inputs_now, *weights, block_passes, block_lens)
        result, pullback = jax.vjp(locally, block_in.astype(jnp.float32), *floats)
        gradients = pullback(block_cot.astype(jnp.float32))
        running = tuple((running_sum + gradient for running_sum, gradient in zip(running, gradients[1:])))
        return (running, (result.astype(jnp.bfloat16), gradients[0]))
    starting = tuple((jnp.zeros(element.shape, jnp.float32) for element in floats))
    running, (outputs, grad_input) = lax.scan(advance, starting, (regroup(inputs), regroup(seq_lens), regroup(pass_idx), regroup(cotangent)))
    return (outputs.reshape(SEQS, LEN, D), grad_input.reshape(SEQS, LEN, D), running[0], running[1], running[2], running[3], running[4], running[5], running[6])
```

```python
import functools
import math

import jax
import jax.numpy as jnp
from jax import lax
from jax.experimental import pallas as pl
from jax.experimental.pallas import tpu as pltpu
from jax.sharding import PartitionSpec as P

HEADS = 12
HEAD_DIM = 64
PAIR = 2 * HEAD_DIM
EPSILON = 1e-05
MASKED = -1e30
BF16 = jnp.bfloat16
F32 = jnp.float32
VMEM_LIMIT = 64 * 1024 * 1024 - 65536

NN = (((1,), (0,)), ((), ()))
NT = (((1,), (1,)), ((), ()))
TN = (((0,), (0,)), ((), ()))


def mm(a, b, dims=NN):
    return lax.dot_general(a, b, dims, preferred_element_type=F32)


def norm_parts(values):
    average = jnp.mean(values, axis=-1, keepdims=True)
    centred = values - average
    variance = jnp.mean(centred * centred, axis=-1, keepdims=True)
    scale = lax.rsqrt(variance + EPSILON)
    return centred * scale, scale


def norm_back(unit, scale, grad, gain):
    scaled = grad * gain
    part = scaled - jnp.mean(scaled, axis=-1, keepdims=True)
    return scale * (part - unit * jnp.mean(scaled * unit, axis=-1, keepdims=True))


def lanes_of(shape):
    return lax.broadcasted_iota(jnp.int32, shape, len(shape) - 1)


def head_only(values, head, zero_at=None):
    lanes = lanes_of(values.shape)
    own = (lanes < HEAD_DIM) if head == 0 else (lanes >= HEAD_DIM)
    return jnp.where(own, values, jnp.zeros_like(values)), own, lanes


def query_with_bias(query, head):
    kept, own, lanes = head_only(query * BF16(HEAD_DIM**-0.5), head)
    spot = HEAD_DIM if head == 0 else 0
    return jnp.where(lanes == spot, jnp.ones_like(kept), kept), kept


def key_with_bias(keys, bias, head):
    kept, own, lanes = head_only(keys, head)
    spot = HEAD_DIM if head == 0 else 0
    return jnp.where(lanes == spot, bias, kept), kept


def attention_front(length, joined, attended, log_sums, key_bias, pair, block):
    rows = attended.shape[0]
    width = attended.shape[1]
    at = pl.multiple_of(pair * PAIR, PAIR)
    keys = joined[:, pl.ds(width + at, PAIR)]
    values = joined[:, pl.ds(2 * width + at, PAIR)]
    bias = key_bias[...]
    biased = [key_with_bias(keys, bias, head)[0] for head in range(2)]
    for first in range(0, rows, block):
        live = first + block
        query = joined[pl.ds(first, block), pl.ds(at, PAIR)]
        mixed = []
        sums = []
        for head in range(2):
            asked, _ = query_with_bias(query, head)
            scores = mm(asked, biased[head][:live], NT)
            row_at = lax.broadcasted_iota(jnp.int32, (block, block), 0)
            key_at = lax.broadcasted_iota(jnp.int32, (block, block), 1)
            last = jnp.where(key_at <= row_at, scores[:, first:], MASKED)
            scores = last if first == 0 else jnp.concatenate([scores[:, :first], last], axis=1)
            top = jnp.max(scores, axis=-1, keepdims=True)
            weights = jnp.exp(scores - top)
            total = jnp.sum(weights, axis=-1, keepdims=True)
            mixed.append(mm(weights.astype(BF16), values[:live]) / total)
            sums.append(top + jnp.log(total))
        lanes = lanes_of(mixed[0].shape)
        attended[pl.ds(first, block), pl.ds(at, PAIR)] = jnp.where(
            lanes < HEAD_DIM, mixed[0], mixed[1]
        ).astype(BF16)
        log_sums[pair, pl.ds(first, block), :] = jnp.where(lanes < HEAD_DIM, sums[0], sums[1])


def fill_bias(length, key_bias):
    rows = key_bias.shape[0]
    places = lax.broadcasted_iota(jnp.int32, key_bias.shape, 0)
    key_bias[...] = jnp.where(places < length, 0.0, MASKED).astype(BF16)


def front_kernel(
    block, tile, length_ref, inputs, pass_row, gain, w_qkv, w_out,
    joined_out, attended_out, sums_out, hidden_out, normed, key_bias,
):
    rows, width = inputs.shape
    length = length_ref[0]
    fill_bias(length, key_bias)

    @pl.loop(0, rows // 256)
    def _(step):
        at = pl.ds(step * 256, 256)
        entered = inputs[at, :].astype(F32) + pass_row[0:1, :]
        normed[at, :] = (norm_parts(entered)[0] * gain[0:1, :]).astype(BF16)

    @pl.loop(0, 3)
    def _(part):
        columns = pl.ds(pl.multiple_of(part * width, width), width)

        @pl.loop(0, rows // tile)
        def _(step):
            at = pl.ds(step * tile, tile)
            joined_out[at, columns] = mm(normed[at, :], w_qkv[:, columns]).astype(BF16)

    @pl.loop(0, HEADS // 2)
    def _(pair):
        attention_front(length, joined_out, attended_out, sums_out, key_bias, pair, block)

    @pl.loop(0, rows // tile)
    def _(step):
        at = pl.ds(step * tile, tile)
        entered = inputs[at, :].astype(F32) + pass_row[0:1, :]
        hidden_out[at, :] = entered + mm(attended_out[at, :], w_out[...])


def gelu_both(values):
    outer = math.sqrt(2.0 / math.pi)
    square = values * values
    bent = jnp.tanh(outer * values * (1.0 + 0.044715 * square))
    half = 0.5 * (1.0 + bent)
    slope = half + 0.5 * values * (1.0 - bent * bent) * (outer * (1.0 + 3 * 0.044715 * square))
    return values * half, slope


def mlp_kernel(
    tile, chunk, hidden, cotangent, gain, w_up, w_down,
    outputs, hidden_grad, gain_grad, up_grad, down_grad,
    second, mixed, second_grad, active, rising_grad,
):
    rows, width = hidden.shape
    chunks = w_down.shape[0] // chunk

    @pl.loop(0, rows // 256)
    def _(step):
        at = pl.ds(step * 256, 256)
        second[at, :] = (norm_parts(hidden[at, :])[0] * gain[0:1, :]).astype(BF16)
        mixed[at, :] = hidden[at, :]
        second_grad[at, :] = jnp.zeros((256, width), F32)

    @pl.loop(0, chunks)
    def _(part):
        units = pl.ds(pl.multiple_of(part * chunk, chunk), chunk)

        @pl.loop(0, rows // tile)
        def _(step):
            at = pl.ds(step * tile, tile)
            rising = mm(second[at, :], w_up[:, units])
            active_grad = mm(cotangent[at, :], w_down[units, :], NT)
            bent, slope = gelu_both(rising)
            shown = bent.astype(BF16)
            moved = (slope * active_grad).astype(BF16)
            active[at, :] = shown
            rising_grad[at, :] = moved
            mixed[at, :] += mm(shown, w_down[units, :])
            second_grad[at, :] += mm(moved, w_up[:, units], NT)

        down_grad[units, :] = mm(active[...], cotangent[...], TN).astype(BF16)
        up_grad[:, units] = mm(second[...], rising_grad[...], TN).astype(BF16)

    gain_grad[...] = jnp.zeros_like(gain_grad)

    @pl.loop(0, rows // 256)
    def _(step):
        at = pl.ds(step * 256, 256)
        outputs[at, :] = mixed[at, :].astype(BF16)
        unit, scale = norm_parts(hidden[at, :])
        grad = second_grad[at, :]
        hidden_grad[at, :] = cotangent[at, :].astype(F32) + norm_back(unit, scale, grad, gain[0:1, :])
        gain_grad[0:1, :] += jnp.sum(grad * unit, axis=0, keepdims=True)


def attention_back(joined, log_rows, grads, joined_grad, key_bias, key_total, value_total, pair, block):
    rows = grads.shape[0]
    width = grads.shape[1]
    at = pl.multiple_of(pair * PAIR, PAIR)
    keys = joined[:, pl.ds(width + at, PAIR)]
    values = joined[:, pl.ds(2 * width + at, PAIR)]
    bias = key_bias[...]
    biased = [key_with_bias(keys, bias, head) for head in range(2)]
    key_total[...] = jnp.zeros_like(key_total)
    value_total[...] = jnp.zeros_like(value_total)
    for first in range(0, rows, block):
        live = first + block
        query = joined[pl.ds(first, block), pl.ds(at, PAIR)]
        grad = grads[pl.ds(first, block), pl.ds(at, PAIR)]
        query_grad = None
        for head in range(2):
            asked, asked_only = query_with_bias(query, head)
            grad_only = head_only(grad, head)[0]
            scores = mm(biased[head][0][:live], asked, NT)
            share_grad = mm(values[:live], grad_only, NT)
            log_sum = log_rows[pl.ds(pair * 2 + head, 1), pl.ds(first, block)]
            shares = jnp.exp(scores - log_sum)
            key_at = lax.broadcasted_iota(jnp.int32, (block, block), 0)
            row_at = lax.broadcasted_iota(jnp.int32, (block, block), 1)
            last = jnp.where(key_at <= row_at, shares[first:], 0.0)
            shares = last if first == 0 else jnp.concatenate([shares[:first], last], axis=0)
            inner = jnp.sum(share_grad * shares, axis=0, keepdims=True)
            score_grad = (shares * (share_grad - inner)).astype(BF16)
            value_total[:live, :] += mm(shares.astype(BF16), grad_only)
            key_total[:live, :] += mm(score_grad, asked_only)
            part = mm(score_grad, biased[head][1][:live], TN)
            query_grad = part if query_grad is None else query_grad + part
        joined_grad[pl.ds(first, block), pl.ds(at, PAIR)] = (
            query_grad * HEAD_DIM**-0.5
        ).astype(BF16)
    joined_grad[:, pl.ds(width + at, PAIR)] = key_total[...].astype(BF16)
    joined_grad[:, pl.ds(2 * width + at, PAIR)] = value_total[...].astype(BF16)


def back_kernel(
    block, tile, length_ref, inputs, pass_row, gain, w_qkv, w_out, joined, log_rows, attended, hidden_grad,
    grad_input, gain_grad, table_grad, qkv_grad, out_grad,
    branch_grad, attended_grad, normed, joined_grad, key_bias, key_total, value_total,
):
    rows, width = inputs.shape
    length = length_ref[0]
    fill_bias(length, key_bias)

    @pl.loop(0, rows // 256)
    def _(step):
        at = pl.ds(step * 256, 256)
        branch_grad[at, :] = hidden_grad[at, :].astype(BF16)
        entered = inputs[at, :].astype(F32) + pass_row[0:1, :]
        normed[at, :] = (norm_parts(entered)[0] * gain[0:1, :]).astype(BF16)

    @pl.loop(0, rows // tile)
    def _(step):
        at = pl.ds(step * tile, tile)
        attended_grad[at, :] = mm(branch_grad[at, :], w_out[...], NT).astype(BF16)

    out_grad[...] = mm(attended[...], branch_grad[...], TN).astype(BF16)

    @pl.loop(0, HEADS // 2)
    def _(pair):
        attention_back(
            joined, log_rows, attended_grad, joined_grad, key_bias, key_total, value_total, pair, block
        )

    @pl.loop(0, 3)
    def _(part):
        columns = pl.ds(pl.multiple_of(part * width, width), width)
        qkv_grad[:, columns] = mm(normed[...], joined_grad[:, columns], TN).astype(BF16)

    gain_grad[...] = jnp.zeros_like(gain_grad)
    table_grad[...] = jnp.zeros_like(table_grad)

    @pl.loop(0, rows // 256)
    def _(step):
        at = pl.ds(step * 256, 256)
        grad = mm(joined_grad[at, :], w_qkv[...], NT)
        unit, scale = norm_parts(inputs[at, :].astype(F32) + pass_row[0:1, :])
        total = hidden_grad[at, :] + norm_back(unit, scale, grad, gain[0:1, :])
        grad_input[at, :] = total
        gain_grad[0:1, :] += jnp.sum(grad * unit, axis=0, keepdims=True)
        table_grad[0:1, :] += jnp.sum(total, axis=0, keepdims=True)


def whole(count):
    return [pl.BlockSpec(memory_space=pltpu.VMEM)] * count


def call(kernel, outs, scratch, *args, scalars=0):
    specs = [pl.BlockSpec(memory_space=pltpu.SMEM)] * scalars + whole(len(args) - scalars)
    return pl.pallas_call(
        kernel,
        out_shape=[jax.ShapeDtypeStruct(shape, kind) for shape, kind in outs],
        in_specs=specs,
        out_specs=whole(len(outs)),
        scratch_shapes=[pltpu.VMEM(shape, kind) for shape, kind in scratch],
        compiler_params=pltpu.CompilerParams(vmem_limit_bytes=VMEM_LIMIT),
    )(*args)


def body(
    inputs, seq_lens, pass_idx, pass_table, gain_attn, w_qkv, w_out, gain_mlp, w_up, w_down, cotangent,
):
    _, rows, width = inputs.shape
    inputs2 = inputs[0]
    out_cot = cotangent[0]
    gather = functools.partial(lax.all_gather, axis_name="shard", tiled=True)
    table = gather(pass_table, axis=1)
    attn_gain = jnp.broadcast_to(gather(gain_attn, axis=0).astype(F32)[None, :], (8, width))
    mlp_gain = jnp.broadcast_to(gather(gain_mlp, axis=0).astype(F32)[None, :], (8, width))
    qkv_w = gather(w_qkv, axis=0)
    out_w = gather(w_out, axis=0)
    up_w = gather(w_up, axis=0)
    down_w = gather(w_down, axis=0)
    chosen = (pass_idx[:, None] == jnp.arange(table.shape[0], dtype=jnp.int32)[None, :]).astype(F32)
    pass_row = jnp.broadcast_to(
        jnp.sum(chosen[0][:, None] * table.astype(F32), axis=0, keepdims=True), (8, width)
    )
    block = 256
    tile = 512
    joined, attended, sums, hidden = call(
        functools.partial(front_kernel, block, tile),
        [((rows, 3 * width), BF16), ((rows, width), BF16), ((HEADS // 2, rows, PAIR), F32), ((rows, width), F32)],
        [((rows, width), BF16), ((rows, PAIR), BF16)],
        seq_lens, inputs2, pass_row, attn_gain, qkv_w, out_w, scalars=1,
    )
    chunk = 1024
    outputs, hidden_grad, mlp_gain_grad, up_grad, down_grad = call(
        functools.partial(mlp_kernel, tile, chunk),
        [((rows, width), BF16), ((rows, width), F32), ((8, width), F32), (up_w.shape, BF16), (down_w.shape, BF16)],
        [((rows, width), BF16), ((rows, width), F32), ((rows, width), F32), ((rows, chunk), BF16), ((rows, chunk), BF16)],
        hidden, out_cot, mlp_gain, up_w, down_w,
    )
    log_rows = jnp.stack([sums[:, :, 0], sums[:, :, HEAD_DIM]], axis=1).reshape(HEADS, rows)
    grad_input, attn_gain_grad, table_row, qkv_grad, out_grad = call(
        functools.partial(back_kernel, block, tile),
        [((rows, width), F32), ((8, width), F32), ((8, width), F32), (qkv_w.shape, BF16), (out_w.shape, BF16)],
        [((rows, width), BF16), ((rows, width), BF16), ((rows, width), BF16), ((rows, 3 * width), BF16),
         ((rows, PAIR), BF16), ((rows, PAIR), F32), ((rows, PAIR), F32)],
        seq_lens, inputs2, pass_row, attn_gain, qkv_w, out_w, joined, log_rows, attended, hidden_grad, scalars=1,
    )
    scatter = lambda grad, dim=0: lax.psum_scatter(grad, "shard", scatter_dimension=dim, tiled=True)
    up_part, down_part = scatter(up_grad), scatter(down_grad)
    out_part, qkv_part = scatter(out_grad), scatter(qkv_grad)
    small = jnp.concatenate(
        [chosen[0][:, None] * table_row[0:1], attn_gain_grad[0:1], mlp_gain_grad[0:1]], axis=0
    )
    small = lax.psum(scatter(small, 1), "rep")
    up_sum, down_sum, out_sum, qkv_sum = lax.psum((up_part, down_part, out_part, qkv_part), "rep")
    count = table.shape[0]
    return (
        outputs[None], grad_input[None], small[:count], small[count], qkv_sum.astype(F32), out_sum.astype(F32),
        small[count + 1], up_sum.astype(F32), down_sum.astype(F32),
    )


def solution(mesh):
    part = P(("shard", "rep"), None, None)
    return jax.shard_map(
        body,
        mesh=mesh,
        in_specs=(
            part, P(("shard", "rep")), P(("shard", "rep")), P(None, "shard"), P("shard"), P("shard", None),
            P("shard", None), P("shard"), P("shard", None), P("shard", None), part,
        ),
        out_specs=(
            part, part, P(None, "shard"), P("shard"), P("shard", None), P("shard", None), P("shard"),
            P("shard", None), P("shard", None),
        ),
        check_vma=False,
    )
```

```python
import functools
import math

import jax
import jax.numpy as jnp
from jax import lax
from jax.experimental import pallas as pl
from jax.experimental.pallas import tpu as pltpu
from jax.sharding import PartitionSpec as P

HEADS = 12
HEAD_DIM = 64
PAIR = 2 * HEAD_DIM
EPSILON = 1e-05
MASKED = -1e30
BF16 = jnp.bfloat16
F32 = jnp.float32
VMEM_LIMIT = 64 * 1024 * 1024 - 65536

NN = (((1,), (0,)), ((), ()))
NT = (((1,), (1,)), ((), ()))
TN = (((0,), (0,)), ((), ()))


def mm(a, b, dims=NN):
    return lax.dot_general(a, b, dims, preferred_element_type=F32)


def norm_parts(values):
    average = jnp.mean(values, axis=-1, keepdims=True)
    centred = values - average
    variance = jnp.mean(centred * centred, axis=-1, keepdims=True)
    scale = lax.rsqrt(variance + EPSILON)
    return centred * scale, scale


def norm_back(unit, scale, grad, gain):
    scaled = grad * gain
    part = scaled - jnp.mean(scaled, axis=-1, keepdims=True)
    return scale * (part - unit * jnp.mean(scaled * unit, axis=-1, keepdims=True))


def lanes_of(shape):
    return lax.broadcasted_iota(jnp.int32, shape, len(shape) - 1)


def head_only(values, head, zero_at=None):
    lanes = lanes_of(values.shape)
    own = (lanes < HEAD_DIM) if head == 0 else (lanes >= HEAD_DIM)
    return jnp.where(own, values, jnp.zeros_like(values)), own, lanes


def query_with_bias(query, head):
    kept, own, lanes = head_only(query * BF16(HEAD_DIM**-0.5), head)
    spot = HEAD_DIM if head == 0 else 0
    return jnp.where(lanes == spot, jnp.ones_like(kept), kept), kept


def key_with_bias(keys, bias, head):
    kept, own, lanes = head_only(keys, head)
    spot = HEAD_DIM if head == 0 else 0
    return jnp.where(lanes == spot, bias, kept), kept


def attention_front(length, joined, attended, log_sums, key_bias, pair, block):
    rows = attended.shape[0]
    width = attended.shape[1]
    at = pl.multiple_of(pair * PAIR, PAIR)
    keys = joined[:, pl.ds(width + at, PAIR)]
    values = joined[:, pl.ds(2 * width + at, PAIR)]
    bias = key_bias[...]
    biased = [key_with_bias(keys, bias, head)[0] for head in range(2)]
    for first in range(0, rows, block):
        live = first + block
        query = joined[pl.ds(first, block), pl.ds(at, PAIR)]
        mixed = []
        sums = []
        for head in range(2):
            asked, _ = query_with_bias(query, head)
            scores = mm(asked, biased[head][:live], NT)
            row_at = lax.broadcasted_iota(jnp.int32, (block, block), 0)
            key_at = lax.broadcasted_iota(jnp.int32, (block, block), 1)
            last = jnp.where(key_at <= row_at, scores[:, first:], MASKED)
            scores = last if first == 0 else jnp.concatenate([scores[:, :first], last], axis=1)
            top = jnp.max(scores, axis=-1, keepdims=True)
            weights = jnp.exp(scores - top)
            total = jnp.sum(weights, axis=-1, keepdims=True)
            mixed.append(mm(weights.astype(BF16), values[:live]) / total)
            sums.append(top + jnp.log(total))
        lanes = lanes_of(mixed[0].shape)
        attended[pl.ds(first, block), pl.ds(at, PAIR)] = jnp.where(
            lanes < HEAD_DIM, mixed[0], mixed[1]
        ).astype(BF16)
        log_sums[pair, pl.ds(first, block), :] = jnp.where(lanes < HEAD_DIM, sums[0], sums[1])


def fill_bias(length, key_bias):
    rows = key_bias.shape[0]
    places = lax.broadcasted_iota(jnp.int32, key_bias.shape, 0)
    key_bias[...] = jnp.where(places < length, 0.0, MASKED).astype(BF16)


def front_kernel(
    block, tile, length_ref, inputs, pass_row, gain, w_qkv, w_out,
    joined_out, attended_out, sums_out, hidden_out, normed, key_bias,
):
    rows, width = inputs.shape
    length = length_ref[0]
    fill_bias(length, key_bias)

    @pl.loop(0, rows // 256)
    def _(step):
        at = pl.ds(step * 256, 256)
        entered = inputs[at, :].astype(F32) + pass_row[0:1, :]
        normed[at, :] = (norm_parts(entered)[0] * gain[0:1, :]).astype(BF16)

    @pl.loop(0, 3)
    def _(part):
        columns = pl.ds(pl.multiple_of(part * width, width), width)

        @pl.loop(0, rows // tile)
        def _(step):
            at = pl.ds(step * tile, tile)
            joined_out[at, columns] = mm(normed[at, :], w_qkv[:, columns]).astype(BF16)

    @pl.loop(0, HEADS // 2)
    def _(pair):
        attention_front(length, joined_out, attended_out, sums_out, key_bias, pair, block)

    @pl.loop(0, rows // tile)
    def _(step):
        at = pl.ds(step * tile, tile)
        entered = inputs[at, :].astype(F32) + pass_row[0:1, :]
        hidden_out[at, :] = entered + mm(attended_out[at, :], w_out[...])


def gelu_both(values):
    outer = math.sqrt(2.0 / math.pi)
    square = values * values
    bent = jnp.tanh(outer * values * (1.0 + 0.044715 * square))
    half = 0.5 * (1.0 + bent)
    slope = half + 0.5 * values * (1.0 - bent * bent) * (outer * (1.0 + 3 * 0.044715 * square))
    return values * half, slope


def mlp_kernel(
    tile, chunk, hidden, cotangent, gain, w_up, w_down,
    outputs, hidden_grad, gain_grad, up_grad, down_grad,
    second, mixed, second_grad, active, rising_grad,
):
    rows, width = hidden.shape
    chunks = w_down.shape[0] // chunk

    @pl.loop(0, rows // 256)
    def _(step):
        at = pl.ds(step * 256, 256)
        second[at, :] = (norm_parts(hidden[at, :])[0] * gain[0:1, :]).astype(BF16)
        mixed[at, :] = hidden[at, :]
        second_grad[at, :] = jnp.zeros((256, width), F32)

    @pl.loop(0, chunks)
    def _(part):
        units = pl.ds(pl.multiple_of(part * chunk, chunk), chunk)

        @pl.loop(0, rows // tile)
        def _(step):
            at = pl.ds(step * tile, tile)
            rising = mm(second[at, :], w_up[:, units])
            active_grad = mm(cotangent[at, :], w_down[units, :], NT)
            bent, slope = gelu_both(rising)
            shown = bent.astype(BF16)
            moved = (slope * active_grad).astype(BF16)
            active[at, :] = shown
            rising_grad[at, :] = moved
            mixed[at, :] += mm(shown, w_down[units, :])
            second_grad[at, :] += mm(moved, w_up[:, units], NT)

        down_grad[units, :] = mm(active[...], cotangent[...], TN).astype(BF16)
        up_grad[:, units] = mm(second[...], rising_grad[...], TN).astype(BF16)

    gain_grad[...] = jnp.zeros_like(gain_grad)

    @pl.loop(0, rows // 256)
    def _(step):
        at = pl.ds(step * 256, 256)
        outputs[at, :] = mixed[at, :].astype(BF16)
        unit, scale = norm_parts(hidden[at, :])
        grad = second_grad[at, :]
        hidden_grad[at, :] = cotangent[at, :].astype(F32) + norm_back(unit, scale, grad, gain[0:1, :])
        gain_grad[0:1, :] += jnp.sum(grad * unit, axis=0, keepdims=True)


def attention_back(joined, log_rows, grads, joined_grad, key_bias, key_total, value_total, pair, block):
    rows = grads.shape[0]
    width = grads.shape[1]
    at = pl.multiple_of(pair * PAIR, PAIR)
    keys = joined[:, pl.ds(width + at, PAIR)]
    values = joined[:, pl.ds(2 * width + at, PAIR)]
    bias = key_bias[...]
    biased = [key_with_bias(keys, bias, head) for head in range(2)]
    key_total[...] = jnp.zeros_like(key_total)
    value_total[...] = jnp.zeros_like(value_total)
    for first in range(0, rows, block):
        live = first + block
        query = joined[pl.ds(first, block), pl.ds(at, PAIR)]
        grad = grads[pl.ds(first, block), pl.ds(at, PAIR)]
        query_grad = None
        for head in range(2):
            asked, asked_only = query_with_bias(query, head)
            grad_only = head_only(grad, head)[0]
            scores = mm(biased[head][0][:live], asked, NT)
            share_grad = mm(values[:live], grad_only, NT)
            log_sum = log_rows[pl.ds(pair * 2 + head, 1), pl.ds(first, block)]
            shares = jnp.exp(scores - log_sum)
            key_at = lax.broadcasted_iota(jnp.int32, (block, block), 0)
            row_at = lax.broadcasted_iota(jnp.int32, (block, block), 1)
            last = jnp.where(key_at <= row_at, shares[first:], 0.0)
            shares = last if first == 0 else jnp.concatenate([shares[:first], last], axis=0)
            inner = jnp.sum(share_grad * shares, axis=0, keepdims=True)
            score_grad = (shares * (share_grad - inner)).astype(BF16)
            value_total[:live, :] += mm(shares.astype(BF16), grad_only)
            key_total[:live, :] += mm(score_grad, asked_only)
            part = mm(score_grad, biased[head][1][:live], TN)
            query_grad = part if query_grad is None else query_grad + part
        joined_grad[pl.ds(first, block), pl.ds(at, PAIR)] = (
            query_grad * HEAD_DIM**-0.5
        ).astype(BF16)
    joined_grad[:, pl.ds(width + at, PAIR)] = key_total[...].astype(BF16)
    joined_grad[:, pl.ds(2 * width + at, PAIR)] = value_total[...].astype(BF16)


def back_kernel(
    block, tile, length_ref, inputs, pass_row, gain, w_qkv, w_out, joined, log_rows, attended, hidden_grad,
    grad_input, gain_grad, table_grad, qkv_grad, out_grad,
    branch_grad, attended_grad, normed, joined_grad, key_bias, key_total, value_total,
):
    rows, width = inputs.shape
    length = length_ref[0]
    fill_bias(length, key_bias)

    @pl.loop(0, rows // 256)
    def _(step):
        at = pl.ds(step * 256, 256)
        branch_grad[at, :] = hidden_grad[at, :].astype(BF16)
        entered = inputs[at, :].astype(F32) + pass_row[0:1, :]
        normed[at, :] = (norm_parts(entered)[0] * gain[0:1, :]).astype(BF16)

    @pl.loop(0, rows // tile)
    def _(step):
        at = pl.ds(step * tile, tile)
        attended_grad[at, :] = mm(branch_grad[at, :], w_out[...], NT).astype(BF16)

    out_grad[...] = mm(attended[...], branch_grad[...], TN).astype(BF16)

    @pl.loop(0, HEADS // 2)
    def _(pair):
        attention_back(
            joined, log_rows, attended_grad, joined_grad, key_bias, key_total, value_total, pair, block
        )

    @pl.loop(0, 3)
    def _(part):
        columns = pl.ds(pl.multiple_of(part * width, width), width)
        qkv_grad[:, columns] = mm(normed[...], joined_grad[:, columns], TN).astype(BF16)

    gain_grad[...] = jnp.zeros_like(gain_grad)
    table_grad[...] = jnp.zeros_like(table_grad)

    @pl.loop(0, rows // 256)
    def _(step):
        at = pl.ds(step * 256, 256)
        grad = mm(joined_grad[at, :], w_qkv[...], NT)
        unit, scale = norm_parts(inputs[at, :].astype(F32) + pass_row[0:1, :])
        total = hidden_grad[at, :] + norm_back(unit, scale, grad, gain[0:1, :])
        grad_input[at, :] = total
        gain_grad[0:1, :] += jnp.sum(grad * unit, axis=0, keepdims=True)
        table_grad[0:1, :] += jnp.sum(total, axis=0, keepdims=True)


def whole(count):
    return [pl.BlockSpec(memory_space=pltpu.VMEM)] * count


def call(kernel, outs, scratch, *args, scalars=0):
    specs = [pl.BlockSpec(memory_space=pltpu.SMEM)] * scalars + whole(len(args) - scalars)
    return pl.pallas_call(
        kernel,
        out_shape=[jax.ShapeDtypeStruct(shape, kind) for shape, kind in outs],
        in_specs=specs,
        out_specs=whole(len(outs)),
        scratch_shapes=[pltpu.VMEM(shape, kind) for shape, kind in scratch],
        compiler_params=pltpu.CompilerParams(vmem_limit_bytes=VMEM_LIMIT),
    )(*args)


def body(
    inputs, seq_lens, pass_idx, pass_table, gain_attn, w_qkv, w_out, gain_mlp, w_up, w_down, cotangent,
):
    _, rows, width = inputs.shape
    inputs2 = inputs[0]
    out_cot = cotangent[0]
    gather = functools.partial(lax.all_gather, axis_name="shard", tiled=True)
    table = gather(pass_table, axis=1)
    attn_gain = jnp.broadcast_to(gather(gain_attn, axis=0).astype(F32)[None, :], (8, width))
    mlp_gain = jnp.broadcast_to(gather(gain_mlp, axis=0).astype(F32)[None, :], (8, width))
    qkv_w = gather(w_qkv, axis=0)
    out_w = gather(w_out, axis=0)
    up_w = gather(w_up, axis=0)
    down_w = gather(w_down, axis=0)
    chosen = (pass_idx[:, None] == jnp.arange(table.shape[0], dtype=jnp.int32)[None, :]).astype(F32)
    pass_row = jnp.broadcast_to(
        jnp.sum(chosen[0][:, None] * table.astype(F32), axis=0, keepdims=True), (8, width)
    )
    block = 256
    tile = 512
    joined, attended, sums, hidden = call(
        functools.partial(front_kernel, block, tile),
        [((rows, 3 * width), BF16), ((rows, width), BF16), ((HEADS // 2, rows, PAIR), F32), ((rows, width), F32)],
        [((rows, width), BF16), ((rows, PAIR), BF16)],
        seq_lens, inputs2, pass_row, attn_gain, qkv_w, out_w, scalars=1,
    )
    chunk = 1024
    outputs, hidden_grad, mlp_gain_grad, up_grad, down_grad = call(
        functools.partial(mlp_kernel, tile, chunk),
        [((rows, width), BF16), ((rows, width), F32), ((8, width), F32), (up_w.shape, BF16), (down_w.shape, BF16)],
        [((rows, width), BF16), ((rows, width), F32), ((rows, width), F32), ((rows, chunk), BF16), ((rows, chunk), BF16)],
        hidden, out_cot, mlp_gain, up_w, down_w,
    )
    log_rows = jnp.stack([sums[:, :, 0], sums[:, :, HEAD_DIM]], axis=1).reshape(HEADS, rows)
    grad_input, attn_gain_grad, table_row, qkv_grad, out_grad = call(
        functools.partial(back_kernel, block, tile),
        [((rows, width), F32), ((8, width), F32), ((8, width), F32), (qkv_w.shape, BF16), (out_w.shape, BF16)],
        [((rows, width), BF16), ((rows, width), BF16), ((rows, width), BF16), ((rows, 3 * width), BF16),
         ((rows, PAIR), BF16), ((rows, PAIR), F32), ((rows, PAIR), F32)],
        seq_lens, inputs2, pass_row, attn_gain, qkv_w, out_w, joined, log_rows, attended, hidden_grad, scalars=1,
    )
    scatter = lambda grad, dim=0: lax.psum_scatter(grad, "shard", scatter_dimension=dim, tiled=True)
    up_part, down_part = scatter(up_grad), scatter(down_grad)
    out_part, qkv_part = scatter(out_grad), scatter(qkv_grad)
    small = jnp.concatenate(
        [chosen[0][:, None] * table_row[0:1], attn_gain_grad[0:1], mlp_gain_grad[0:1]], axis=0
    )
    small = lax.psum(scatter(small, 1), "rep")
    up_sum, down_sum, out_sum, qkv_sum = lax.psum((up_part, down_part, out_part, qkv_part), "rep")
    count = table.shape[0]
    return (
        outputs[None], grad_input[None], small[:count], small[count], qkv_sum.astype(F32), out_sum.astype(F32),
        small[count + 1], up_sum.astype(F32), down_sum.astype(F32),
    )


MESH = pl.DeviceIdType.MESH


class Place:
    def __init__(self):
        self.me = lax.axis_index("shard")
        self.z = lax.axis_index("rep")
        self.core = lax.rem(self.me, 2)
        self.x = lax.rem(self.me // 2, 2)
        self.y = self.me // 4
        self.by_x = self.me + 2 - 4 * self.x
        self.by_y = self.me + 4 - 8 * self.y
        self.by_core = self.me + 1 - 2 * self.core
        self.by_both = self.by_x + 4 - 8 * self.y

    def at(self, shard):
        return (shard, self.z)


def remote(src, dst, sends, recvs, index, device):
    return pltpu.make_async_remote_copy(
        src_ref=src, dst_ref=dst, send_sem=sends.at[index], recv_sem=recvs.at[index],
        device_id=device, device_id_type=MESH,
    )


class Gather:
    def __init__(self, place, own, block_of, half_of, sends, recvs, local, row):
        self.place, self.own, self.block, self.half = place, own, block_of, half_of
        self.sends, self.recvs, self.local, self.row = sends, recvs, local, row

    def copy(self, slot, src, dst, shard):
        return remote(src, dst, self.sends, self.recvs, (self.row, slot), self.place.at(shard))

    def same(self, slot, ref, shard):
        return self.copy(slot, ref, ref, shard)

    def make(self, slot):
        p, block, half = self.place, self.block, self.half
        if slot < 3:
            return self.copy(slot, self.own, block(p.me), (p.by_x, p.by_y, p.by_core)[slot])
        if slot == 3:
            return self.same(slot, half(p.by_x, 0), p.by_y)
        if slot == 4:
            return self.same(slot, half(p.by_y, 1), p.by_x)
        if slot < 7:
            return self.same(slot, block(p.by_x if slot == 5 else p.by_y), p.by_core)
        return self.same(slot, half(p.by_both, slot - 7), p.by_core)

    def here(self):
        return pltpu.make_async_copy(self.own, self.block(self.place.me), self.local.at[self.row])

    def start(self):
        for slot in range(3):
            self.make(slot).start()
        self.here().start()

    def relay(self):
        self.make(0).wait_recv()
        self.make(3).start()
        self.make(5).start()
        self.make(1).wait_recv()
        self.make(4).start()
        self.make(6).start()

    def finish(self):
        self.make(3).wait_recv()
        self.make(7).start()
        self.make(4).wait_recv()
        self.make(8).start()

    def ready(self):
        for slot in (2, 5, 6, 7, 8):
            self.make(slot).wait_recv()
        self.here().wait()

    def drain(self):
        for slot in range(9):
            self.make(slot).wait_send()


def enter(place, shards, reps=()):
    barrier = pltpu.get_barrier_semaphore()
    for shard in shards:
        pl.semaphore_signal(barrier, inc=1, device_id=(shard, place.z), device_id_type=MESH)
    for rep in reps:
        pl.semaphore_signal(barrier, inc=1, device_id=(place.me, rep), device_id_type=MESH)
    pl.semaphore_wait(barrier, len(shards) + len(reps))


def rows_block(ref, rows, lead=(), columns=slice(None)):
    def block(shard):
        return ref.at[lead + (pl.ds(pl.multiple_of(shard * rows, rows), rows), columns)]

    def half(shard, part):
        start = pl.multiple_of(shard * rows + part * (rows // 2), rows // 2)
        return ref.at[lead + (pl.ds(start, rows // 2), columns)]

    return block, half


def attention_rows(joined, attended, log_rows, key_bias, pair, block):
    rows = attended.shape[0]
    columns = pl.ds(pl.multiple_of(pair * PAIR, PAIR), PAIR)
    keys = joined[1, :, columns]
    values = joined[2, :, columns]
    bias = key_bias[...]
    biased = [key_with_bias(keys, bias, head)[0] for head in range(2)]
    for first in range(0, rows, block):
        live = first + block
        query = joined[0, pl.ds(first, block), columns]
        mixed = []
        sums = []
        for head in range(2):
            asked, _ = query_with_bias(query, head)
            scores = mm(asked, biased[head][:live], NT)
            row_at = lax.broadcasted_iota(jnp.int32, (block, block), 0)
            key_at = lax.broadcasted_iota(jnp.int32, (block, block), 1)
            last = jnp.where(key_at <= row_at, scores[:, first:], MASKED)
            scores = last if first == 0 else jnp.concatenate([scores[:, :first], last], axis=1)
            top = jnp.max(scores, axis=-1, keepdims=True)
            weights = jnp.exp(scores - top)
            total = jnp.sum(weights, axis=-1, keepdims=True)
            mixed.append(mm(weights.astype(BF16), values[:live]) / total)
            sums.append(top + jnp.log(total))
        lanes = lanes_of(mixed[0].shape)
        attended[pl.ds(first, block), columns] = jnp.where(lanes < HEAD_DIM, mixed[0], mixed[1]).astype(BF16)
        turned = jnp.transpose(jnp.where(lanes < HEAD_DIM, sums[0], sums[1]))
        log_rows[pl.ds(pair * 2, 1), pl.ds(first, block)] = turned[0:1]
        log_rows[pl.ds(pair * 2 + 1, 1), pl.ds(first, block)] = turned[HEAD_DIM : HEAD_DIM + 1]


def norm_rows(inputs, pass_row, gain, normed):
    @pl.loop(0, inputs.shape[0] // 256)
    def _(step):
        at = pl.ds(step * 256, 256)
        entered = inputs[at, :].astype(F32) + pass_row
        normed[at, :] = (norm_parts(entered)[0] * gain).astype(BF16)


def front_comm_kernel(
    ahead, block, tile, group,
    length_ref, pass_ref, inputs, small_own, qkv_own, out_own, up_own, down_own,
    rows_out, log_out, joined_out, attended_out, hidden_out, qkv_out, out_out, up_out, down_out,
    slots, normed, joined, attended, hidden, qkv_w, out_w, key_bias,
    sends, recvs, local, small_sends, small_recvs, saves,
):
    place = Place()
    rows, width = inputs.shape
    shards = slots.shape[0]
    part = qkv_own.shape[1]
    groups = width // group
    others = [lax.rem(place.me + shift, shards) for shift in range(1, shards)]
    enter(place, others)

    smalls = [
        remote(small_own, slots.at[place.me], small_sends, small_recvs, shift, place.at(other))
        for shift, other in enumerate(others)
    ]
    for copy in smalls:
        copy.start()
    mine = pltpu.make_async_copy(small_own, slots.at[place.me], small_sends.at[shards - 1])
    mine.start()

    pieces = []

    def add(own, block_of, half_of):
        pieces.append(Gather(place, own, block_of, half_of, sends, recvs, local, len(pieces)))

    for index in range(groups):
        columns = pl.ds(index * group, group)
        add(qkv_own.at[:, :, columns], *rows_block(qkv_w, part, (slice(None),), columns))
    add(out_own, *rows_block(out_w, part))
    for index in range(ahead):
        add(up_own.at[index], *rows_block(up_out, part, (index,)))
        add(down_own.at[index], *rows_block(down_out, down_own.shape[1], (index,)))
    count = len(pieces)

    def tick(index):
        if index + 2 < count:
            pieces[index + 2].start()
        if index < count:
            pieces[index].relay()
        if 0 <= index - 1 < count:
            pieces[index - 1].finish()

    pieces[0].start()
    pieces[1].start()
    fill_bias(length_ref[0], key_bias)
    mine.wait()
    for copy in smalls:
        copy.wait_recv()
    total = slots[0].astype(F32)
    for shard in range(1, shards):
        total = total + slots[shard].astype(F32)
    places = lax.broadcasted_iota(jnp.int32, total.shape, 0)
    pass_row = jnp.sum(jnp.where(places == pass_ref[0], total, 0.0), axis=0, keepdims=True)
    rows_out[0:1, :] = pass_row
    rows_out[1:3, :] = total[8:10]
    rows_out[3:8, :] = jnp.zeros((5, width), F32)

    tick(0)
    norm_rows(inputs, rows_out[0:1, :], rows_out[1:2, :], normed)
    tick(1)

    def save(source, target, index):
        return pltpu.make_async_copy(source, target, saves.at[index])

    pairs = width // PAIR
    per_group = group // PAIR

    @pl.loop(0, pairs)
    def _(pair):
        for index in range(groups):
            @pl.when(pair == index * per_group)
            def _(index=index):
                pieces[index].ready()

        @pl.when(lax.rem(pair, per_group) == 0)
        def _():
            columns = pl.ds(pl.multiple_of(pair * PAIR, group), group)

            @pl.loop(0, 3)
            def _(plane):
                joined[plane, :, columns] = mm(normed[...], qkv_w[plane, :, columns]).astype(BF16)

        attention_rows(joined, attended, log_out, key_bias, pair, block)
        for index in range(pairs):
            @pl.when(pair == index)
            def _(index=index):
                tick(index + 2)

    keep = [
        save(joined, joined_out, 0), save(attended, attended_out, 1), save(qkv_w, qkv_out, 2),
    ]
    for copy in keep:
        copy.start()
    pieces[groups].ready()
    keep.append(save(out_w, out_out, 3))
    keep[-1].start()

    @pl.loop(0, rows // tile)
    def _(step):
        at = pl.ds(step * tile, tile)
        entered = inputs[at, :].astype(F32) + rows_out[0:1, :]
        hidden[at, :] = entered + mm(attended[at, :], out_w[...])

    keep.append(save(hidden, hidden_out, 4))
    keep[-1].start()
    for index in range(pairs + 2, count + 1):
        tick(index)
    for piece in pieces[groups + 1 :]:
        piece.ready()
    for piece in pieces:
        piece.drain()
    for copy in smalls:
        copy.wait_send()
    for copy in keep:
        copy.wait()


def any_spec(count):
    return [pl.BlockSpec(memory_space=pl.ANY)] * count


def smem_spec(count):
    return [pl.BlockSpec(memory_space=pltpu.SMEM)] * count


def vmem_spec(count):
    return [pl.BlockSpec(memory_space=pltpu.VMEM)] * count


def shaped(shape, kind):
    return jax.ShapeDtypeStruct(shape, kind)


def front_comm(ahead, seq_lens, pass_idx, inputs, small, qkv, out, up, down):
    rows, width = inputs.shape
    shards = width // out.shape[0]
    chunk = up.shape[2]
    group = 4 * HEAD_DIM
    count = width // group + 1 + 2 * ahead
    return pl.pallas_call(
        functools.partial(front_comm_kernel, ahead, 256, 512, group),
        out_shape=[
            shaped((8, width), F32), shaped((16, rows), F32), shaped((3, rows, width), BF16),
            shaped((rows, width), BF16), shaped((rows, width), F32), shaped((3, width, width), BF16),
            shaped((width, width), BF16), shaped((ahead, width, chunk), BF16), shaped((ahead, chunk, width), BF16),
        ],
        in_specs=smem_spec(2) + vmem_spec(1) + any_spec(5),
        out_specs=vmem_spec(2) + any_spec(7),
        scratch_shapes=[
            pltpu.VMEM((shards,) + small.shape, BF16), pltpu.VMEM((rows, width), BF16),
            pltpu.VMEM((3, rows, width), BF16), pltpu.VMEM((rows, width), BF16), pltpu.VMEM((rows, width), F32),
            pltpu.VMEM((3, width, width), BF16), pltpu.VMEM((width, width), BF16), pltpu.VMEM((rows, PAIR), BF16),
            pltpu.SemaphoreType.DMA((count, 9)), pltpu.SemaphoreType.DMA((count, 9)), pltpu.SemaphoreType.DMA((count,)),
            pltpu.SemaphoreType.DMA((shards,)), pltpu.SemaphoreType.DMA((shards,)), pltpu.SemaphoreType.DMA((5,)),
        ],
        compiler_params=pltpu.CompilerParams(
            vmem_limit_bytes=VMEM_LIMIT, collective_id=1, has_side_effects=True
        ),
    )(seq_lens, pass_idx, inputs, small, qkv, out, up, down)


class Scatter:
    def __init__(self, place, grads, first, by_x, by_y, last, sends, recvs, row):
        self.place, self.grads, self.first = place, grads, first
        self.in_x, self.in_y, self.last = by_x, by_y, last
        self.sends, self.recvs, self.row = sends, recvs, row
        half = first.shape[-1] // 2
        self.left, self.right = pl.ds(0, half), pl.ds(half, half)

    def copy(self, slot, src, dst, shard):
        return remote(src, dst, self.sends, self.recvs, (self.row, slot), self.place.at(shard))

    def swap_copy(self):
        p = self.place
        return self.copy(0, self.grads.at[:, :, 1 - p.core], self.first, p.by_core)

    def spread_copies(self):
        p = self.place
        return [
            self.copy(1, self.first.at[:, 1 - p.x, :, self.left], self.in_x, p.by_x),
            self.copy(2, self.first.at[1 - p.y, :, :, self.right], self.in_y, p.by_y),
        ]

    def fold_copies(self):
        p = self.place
        return [
            self.copy(3, self.in_x.at[1 - p.y], self.last.at[:, self.left], p.by_y),
            self.copy(4, self.in_y.at[1 - p.x], self.last.at[:, self.right], p.by_x),
        ]

    def swap(self):
        self.swap_copy().start()

    def merge(self, target=None):
        p = self.place
        target = self.first if target is None else target
        self.swap_copy().wait_recv()
        for y in range(2):
            for x in range(2):
                total = self.grads[y, x, p.core].astype(F32) + self.first[y, x].astype(F32)
                target[y, x] = total.astype(BF16)

    def spread(self):
        for copy in self.spread_copies():
            copy.start()

    def fold(self):
        p = self.place
        for copy in self.spread_copies():
            copy.wait_recv()
        for other in range(2):
            total = self.first[other, p.x, :, self.left].astype(F32) + self.in_x[other].astype(F32)
            self.in_x[other] = total.astype(BF16)
            total = self.first[p.y, other, :, self.right].astype(F32) + self.in_y[other].astype(F32)
            self.in_y[other] = total.astype(BF16)
        for copy in self.fold_copies():
            copy.start()

    def close(self, target):
        p = self.place
        for copy in self.fold_copies():
            copy.wait_recv()
        target[:, self.left] = (self.last[:, self.left].astype(F32) + self.in_x[p.y].astype(F32)).astype(BF16)
        target[:, self.right] = (self.last[:, self.right].astype(F32) + self.in_y[p.x].astype(F32)).astype(BF16)

    def drain(self, swapped=True, spread=True):
        if swapped:
            self.swap_copy().wait_send()
        if spread:
            for copy in self.spread_copies() + self.fold_copies():
                copy.wait_send()


def mlp_comm_kernel(
    ahead, tile,
    hidden, cotangent, rows_in, up_have, down_have, up_own, down_own,
    outputs, hidden_grad, gain_grad, up_done, down_done, up_half, down_half,
    up_w, down_w, second, mixed, active, rising_grad,
    up_grads, up_first, up_x, up_y, up_last, down_grads, down_first, down_x, down_y, down_last,
    gather_sends, gather_recvs, gather_local, up_sends, up_recvs, down_sends, down_recvs, loads,
):
    place = Place()
    rows, width = hidden.shape
    chunks, chunk = down_w.shape[0], down_w.shape[1]
    enter(place, [place.by_x, place.by_y, place.by_core])
    gain = rows_in[2:3, :]

    pieces = []
    for index in range(ahead, chunks):
        for own, ref in ((up_own, up_w), (down_own, down_w)):
            block, half = rows_block(ref, own.shape[1], (index,))
            pieces.append(
                Gather(place, own.at[index], block, half, gather_sends, gather_recvs, gather_local, len(pieces))
            )
    for piece in pieces:
        piece.start()
    have = []
    for index in range(ahead):
        for ref, weights in ((up_have, up_w), (down_have, down_w)):
            have.append(pltpu.make_async_copy(ref.at[index], weights.at[index], loads.at[len(have)]))
    for copy in have:
        copy.start()

    def up_message(index):
        return Scatter(
            place, up_grads.at[index], up_first.at[index], up_x.at[index], up_y.at[index], up_last.at[index],
            up_sends, up_recvs, index,
        )

    def down_message(index):
        return Scatter(
            place, down_grads.at[index], down_first.at[index], down_x.at[index], down_y.at[index], down_last.at[index],
            down_sends, down_recvs, index,
        )

    @pl.loop(0, rows // 256)
    def _(step):
        at = pl.ds(step * 256, 256)
        second[at, :] = (norm_parts(hidden[at, :])[0] * gain).astype(BF16)
        mixed[at, :] = hidden[at, :]
        hidden_grad[at, :] = jnp.zeros((256, width), F32)

    @pl.loop(0, chunks)
    def _(part):
        for index in range(ahead):
            @pl.when(part == index)
            def _(index=index):
                have[2 * index].wait()
                have[2 * index + 1].wait()
        for index in range(ahead, chunks):
            @pl.when(part == index)
            def _(index=index):
                pieces[2 * (index - ahead)].ready()
                pieces[2 * (index - ahead) + 1].ready()

        @pl.loop(0, rows // tile)
        def _(step):
            at = pl.ds(step * tile, tile)
            rising = mm(second[at, :], up_w[part])
            active_grad = mm(cotangent[at, :], down_w[part], NT)
            bent, slope = gelu_both(rising)
            shown = bent.astype(BF16)
            moved = (slope * active_grad).astype(BF16)
            active[at, :] = shown
            rising_grad[at, :] = moved
            mixed[at, :] += mm(shown, down_w[part])
            hidden_grad[at, :] += mm(moved, up_w[part], NT)

            @pl.when((part == 0) & (step == 0))
            def _():
                for piece in pieces[:2]:
                    piece.relay()

            @pl.when((part == 0) & (step == 1))
            def _():
                for piece in pieces[:2]:
                    piece.finish()
                for piece in pieces[2:]:
                    piece.relay()

            @pl.when((part > 0) & (step == 0))
            def _():
                message = up_message(part - 1)
                message.merge()
                message.spread()

            @pl.when((part > 0) & (step == 1))
            def _():
                down_message(part - 1).fold()

        down_grads[part] = mm(active[...], cotangent[...], TN).astype(BF16).reshape(down_grads.shape[1:])
        down_message(part).swap()

        @pl.when(part == 0)
        def _():
            for piece in pieces[2:]:
                piece.finish()

        @pl.when(part > 0)
        def _():
            up_message(part - 1).fold()

        up_grads[part] = mm(second[...], rising_grad[...], TN).astype(BF16).reshape(up_grads.shape[1:])
        up_message(part).swap()

        @pl.when(part < chunks - 1)
        def _():
            message = down_message(part)
            message.merge()
            message.spread()

        @pl.when(part > 0)
        def _():
            down_message(part - 1).close(down_done.at[part - 1])
            up_message(part - 1).close(up_done.at[part - 1])

    down_message(chunks - 1).merge(down_half)
    gain_grad[...] = jnp.zeros_like(gain_grad)

    @pl.loop(0, rows // 256)
    def _(step):
        at = pl.ds(step * 256, 256)
        outputs[at, :] = mixed[at, :].astype(BF16)
        unit, scale = norm_parts(hidden[at, :])
        grad = hidden_grad[at, :]
        hidden_grad[at, :] = cotangent[at, :].astype(F32) + norm_back(unit, scale, grad, gain)
        gain_grad[0:1, :] += jnp.sum(grad * unit, axis=0, keepdims=True)

    up_message(chunks - 1).merge(up_half)
    for piece in pieces:
        piece.drain()
    for index in range(chunks):
        up_message(index).drain(True, index < chunks - 1)
        down_message(index).drain(True, index < chunks - 1)


def scatter_scratch(count, part, columns):
    return [
        pltpu.VMEM((count, 2, 2, 2, part, columns), BF16), pltpu.VMEM((count, 2, 2, part, columns), BF16),
        pltpu.VMEM((count, 2, part, columns // 2), BF16), pltpu.VMEM((count, 2, part, columns // 2), BF16),
        pltpu.VMEM((count, part, columns), BF16),
    ]


def dma(*shapes):
    return [pltpu.SemaphoreType.DMA(shape) for shape in shapes]


def mlp_comm(ahead, hidden, cotangent, rows_in, up_have, down_have, up, down):
    rows, width = hidden.shape
    chunks, up_part, chunk = up.shape
    down_part = down.shape[1]
    late = 2 * (chunks - ahead)
    return pl.pallas_call(
        functools.partial(mlp_comm_kernel, ahead, 512),
        out_shape=[
            shaped((rows, width), BF16), shaped((rows, width), F32), shaped((8, width), F32),
            shaped((chunks - 1, up_part, chunk), BF16), shaped((chunks - 1, down_part, width), BF16),
            shaped((2, 2, up_part, chunk), BF16), shaped((2, 2, down_part, width), BF16),
        ],
        in_specs=vmem_spec(3) + any_spec(4),
        out_specs=vmem_spec(7),
        scratch_shapes=[
            pltpu.VMEM((chunks, width, chunk), BF16), pltpu.VMEM((chunks, chunk, width), BF16),
            pltpu.VMEM((rows, width), BF16), pltpu.VMEM((rows, width), F32),
            pltpu.VMEM((rows, chunk), BF16), pltpu.VMEM((rows, chunk), BF16),
        ]
        + scatter_scratch(chunks, up_part, chunk)
        + scatter_scratch(chunks, down_part, width)
        + dma((late, 9), (late, 9), (late,), (chunks, 5), (chunks, 5), (chunks, 5), (chunks, 5), (2 * ahead,)),
        compiler_params=pltpu.CompilerParams(
            vmem_limit_bytes=VMEM_LIMIT, collective_id=2, has_side_effects=True
        ),
    )(hidden, cotangent, rows_in, up_have, down_have, up, down)


class Column:
    def __init__(self, place, block, inward, middle, outward, total, sends, recvs, row):
        self.place, self.block, self.inward, self.middle = place, block, inward, middle
        self.outward, self.total = outward, total
        self.sends, self.recvs, self.row = sends, recvs, row
        self.end = (place.z == 0) | (place.z == 3)

    def copy(self, slot, src, dst, rep):
        return remote(src, dst, self.sends, self.recvs, (self.row, slot), (self.place.me, rep))

    def in_copy(self):
        return self.copy(0, self.block, self.inward, 1 + self.place.z // 3)

    def across_copy(self):
        return self.copy(1, self.middle, self.outward, 3 - self.place.z)

    def out_copy(self):
        return self.copy(2, self.total, self.outward, 3 * (self.place.z - 1))

    def begin(self):
        @pl.when(self.end)
        def _():
            self.in_copy().start()

    def cross(self):
        @pl.when(jnp.logical_not(self.end))
        def _():
            self.in_copy().wait_recv()
            self.middle[...] = (self.block[...].astype(F32) + self.inward[...].astype(F32)).astype(BF16)
            self.across_copy().start()

    def settle(self):
        @pl.when(jnp.logical_not(self.end))
        def _():
            self.across_copy().wait_recv()
            self.total[...] = (self.middle[...].astype(F32) + self.outward[...].astype(F32)).astype(BF16)
            self.out_copy().start()

    def finish(self):
        @pl.when(self.end)
        def _():
            self.out_copy().wait_recv()
            self.total[...] = self.outward[...]
            self.in_copy().wait_send()

        @pl.when(jnp.logical_not(self.end))
        def _():
            self.across_copy().wait_send()
            self.out_copy().wait_send()


def attention_columns(joined, log_rows, grads, joined_grad, key_bias, key_total, value_total, pair, block):
    rows = grads.shape[0]
    columns = pl.ds(pl.multiple_of(pair * PAIR, PAIR), PAIR)
    keys = joined[1, :, columns]
    values = joined[2, :, columns]
    bias = key_bias[...]
    biased = [key_with_bias(keys, bias, head) for head in range(2)]
    key_total[...] = jnp.zeros_like(key_total)
    value_total[...] = jnp.zeros_like(value_total)
    for first in range(0, rows, block):
        live = first + block
        query = joined[0, pl.ds(first, block), columns]
        grad = grads[pl.ds(first, block), columns]
        query_grad = None
        for head in range(2):
            asked, asked_only = query_with_bias(query, head)
            grad_only = head_only(grad, head)[0]
            scores = mm(biased[head][0][:live], asked, NT)
            share_grad = mm(values[:live], grad_only, NT)
            log_sum = log_rows[pl.ds(pair * 2 + head, 1), pl.ds(first, block)]
            shares = jnp.exp(scores - log_sum)
            key_at = lax.broadcasted_iota(jnp.int32, (block, block), 0)
            row_at = lax.broadcasted_iota(jnp.int32, (block, block), 1)
            last = jnp.where(key_at <= row_at, shares[first:], 0.0)
            shares = last if first == 0 else jnp.concatenate([shares[:first], last], axis=0)
            inner = jnp.sum(share_grad * shares, axis=0, keepdims=True)
            score_grad = (shares * (share_grad - inner)).astype(BF16)
            value_total[:live, :] += mm(shares.astype(BF16), grad_only)
            key_total[:live, :] += mm(score_grad, asked_only)
            part = mm(score_grad, biased[head][1][:live], TN)
            query_grad = part if query_grad is None else query_grad + part
        joined_grad[0, pl.ds(first, block), columns] = (query_grad * HEAD_DIM**-0.5).astype(BF16)
    joined_grad[1, :, columns] = key_total[...].astype(BF16)
    joined_grad[2, :, columns] = value_total[...].astype(BF16)


def back_comm_kernel(
    block, tile, group,
    length_ref, pass_ref, inputs, rows_in, out_w, log_rows, attended, hidden_grad, mlp_gain_grad,
    up_done, down_done, up_half, down_half, qkv_in, joined_in,
    grad_input, small_sum, up_total, down_total, attn_total,
    qkv_w, joined, branch_grad, attended_grad, normed, joined_grad, key_bias, key_total, value_total,
    grads, first, in_x, in_y, last, block_sum,
    up_x, up_y, up_last, up_block, down_x, down_y, down_last, down_block,
    up_in, up_mid, up_out, down_in, down_mid, down_out, attn_in, attn_mid, attn_out,
    small_own, small_slots, small_plane, small_reps,
    sends, recvs, up_sends, up_recvs, down_sends, down_recvs, z_sends, z_recvs,
    plane_sends, plane_recvs, rep_sends, rep_recvs, loads,
):
    place = Place()
    rows, width = inputs.shape
    shards = small_slots.shape[0]
    reps = small_reps.shape[0]
    chunks = up_total.shape[0]
    groups = width // group
    pairs = width // PAIR
    per_group = group // PAIR
    others = [lax.rem(place.me + shift, shards) for shift in range(1, shards)]
    others_z = [lax.rem(place.z + shift, reps) for shift in range(1, reps)]
    enter(place, others, others_z)
    take = [
        pltpu.make_async_copy(joined_in, joined, loads.at[0]),
        pltpu.make_async_copy(qkv_in, qkv_w, loads.at[1]),
    ]
    for copy in take:
        copy.start()

    up_late = Scatter(place, None, up_half, up_x, up_y, up_last, up_sends, up_recvs, 0)
    down_late = Scatter(place, None, down_half, down_x, down_y, down_last, down_sends, down_recvs, 0)

    def message(index):
        return Scatter(
            place, grads.at[index], first.at[index], in_x.at[index], in_y.at[index], last.at[index],
            sends, recvs, index,
        )

    out_msg = message(0)
    qkv_msg = [message(1 + index) for index in range(groups)]

    lines = {}

    def line(key, source, inward, middle, outward, total):
        lines[key] = Column(place, source, inward, middle, outward, total, z_sends, z_recvs, len(lines))

    for index in range(chunks):
        final = index == chunks - 1
        line(("d", index), down_block if final else down_done.at[index],
             down_in.at[index], down_mid.at[index], down_out.at[index], down_total.at[index])
        line(("u", index), up_block if final else up_done.at[index],
             up_in.at[index], up_mid.at[index], up_out.at[index], up_total.at[index])
    for index in range(1 + groups):
        line(("a", index), block_sum.at[index], attn_in.at[index], attn_mid.at[index], attn_out.at[index],
             attn_total.at[index])

    down_late.spread()
    up_late.spread()
    for index in range(chunks - 1):
        lines["d", index].begin()
        lines["u", index].begin()

    fill_bias(length_ref[0], key_bias)
    norm_rows(inputs, rows_in[0:1, :], rows_in[1:2, :], normed)

    @pl.loop(0, rows // tile)
    def _(step):
        at = pl.ds(step * tile, tile)
        shown = hidden_grad[at, :].astype(BF16)
        branch_grad[at, :] = shown
        attended_grad[at, :] = mm(shown, out_w[...], NT).astype(BF16)

    lines["d", 0].cross()
    down_late.fold()
    grads[0] = mm(attended[...], branch_grad[...], TN).astype(BF16).reshape(grads.shape[1:])
    out_msg.swap()
    for copy in take:
        copy.wait()

    def late_close(message, target, key):
        message.close(target)
        lines[key].begin()

    def close(index):
        message(index).close(block_sum.at[index])
        lines["a", index].begin()

    def send(index):
        message(index).merge()
        message(index).spread()

    after_pair = [
        lambda: (lines["u", 0].cross(), send(0), up_late.fold(), lines["d", 1].cross()),
        lambda: (late_close(down_late, down_block, ("d", 2)), lines["u", 1].cross(), lines["d", 0].settle(),
                 lines["u", 0].settle(), out_msg.fold()),
        lambda: (send(1), late_close(up_late, up_block, ("u", 2)), lines["d", 2].cross(), lines["d", 1].settle(),
                 lines["u", 1].settle(), lines["d", 0].finish(), lines["u", 0].finish()),
        lambda: (close(0), qkv_msg[0].fold(), lines["u", 2].cross(), lines["d", 2].settle(),
                 lines["d", 1].finish(), lines["u", 1].finish()),
        lambda: (send(2), close(1), lines["a", 0].cross(), lines["u", 2].settle()),
        lambda: (qkv_msg[1].fold(), lines["a", 1].cross(), lines["a", 0].settle(), lines["d", 2].finish(),
                 lines["u", 2].finish()),
    ]

    @pl.loop(0, pairs)
    def _(pair):
        attention_columns(
            joined, log_rows, attended_grad, joined_grad, key_bias, key_total, value_total, pair, block
        )

        @pl.when(lax.rem(pair, per_group) == per_group - 1)
        def _():
            index = pair // per_group
            columns = pl.ds(pl.multiple_of(index * group, group), group)
            for plane in range(3):
                part = mm(normed[...], joined_grad[plane, :, columns], TN).astype(BF16)
                grads[1 + index, :, :, :, :, pl.ds(plane * group, group)] = part.reshape(
                    grads.shape[1:5] + (group,)
                )
            message(1 + index).swap()

        for index in range(pairs):
            @pl.when(pair == index)
            def _(index=index):
                after_pair[index]()

    small_own[...] = jnp.zeros_like(small_own)

    def after_rows(step):
        @pl.when(step == 0)
        def _():
            send(3)
            close(2)

        @pl.when(step == 1)
        def _():
            lines["a", 1].settle()

        @pl.when(step == 2)
        def _():
            qkv_msg[2].fold()
            lines["a", 2].cross()

    @pl.loop(0, rows // 256)
    def _(step):
        at = pl.ds(step * 256, 256)
        grad = mm(joined_grad[0, at, :], qkv_w[0], NT)
        grad = grad + mm(joined_grad[1, at, :], qkv_w[1], NT)
        grad = grad + mm(joined_grad[2, at, :], qkv_w[2], NT)
        unit, scale = norm_parts(inputs[at, :].astype(F32) + rows_in[0:1, :])
        total = hidden_grad[at, :] + norm_back(unit, scale, grad, rows_in[1:2, :])
        grad_input[at, :] = total
        small_own[5:6, :] += jnp.sum(grad * unit, axis=0, keepdims=True)
        small_own[0:1, :] += jnp.sum(total, axis=0, keepdims=True)
        after_rows(step)

    close(3)
    places = lax.broadcasted_iota(jnp.int32, small_own.shape, 0)
    own = small_own[...]
    table = jnp.where((places == pass_ref[0]) & (places < 5), own[0:1], 0.0)
    own = jnp.where(places == 5, own, table)
    small_own[...] = jnp.where(places == 6, mlp_gain_grad[0:1], own)
    small_slots[place.me] = small_own[...]
    plane_copies = [
        remote(small_own, small_slots.at[place.me], plane_sends, plane_recvs, shift, place.at(other))
        for shift, other in enumerate(others)
    ]
    for copy in plane_copies:
        copy.start()
    lines["a", 2].settle()
    lines["a", 3].cross()
    for copy in plane_copies:
        copy.wait_recv()
    total = small_slots[0]
    for shard in range(1, shards):
        total = total + small_slots[shard]
    small_plane[...] = total
    small_reps[place.z] = total
    rep_copies = [
        remote(small_plane, small_reps.at[place.z], rep_sends, rep_recvs, shift, (place.me, other))
        for shift, other in enumerate(others_z)
    ]
    for copy in rep_copies:
        copy.start()
    lines["a", 3].settle()
    for copy in rep_copies:
        copy.wait_recv()
    total = small_reps[0]
    for rep in range(1, reps):
        total = total + small_reps[rep]
    small_sum[...] = total
    for index in range(1 + groups):
        lines["a", index].finish()
    for index in range(1 + groups):
        message(index).drain()
    up_late.drain(swapped=False)
    down_late.drain(swapped=False)
    for copy in plane_copies + rep_copies:
        copy.wait_send()


def back_comm(reps, seq_lens, pass_idx, inputs, rows_in, out_w, log_rows, attended, hidden_grad, mlp_gain_grad,
              up_done, down_done, up_half, down_half, qkv_w, joined):
    rows, width = inputs.shape
    _, _, up_part, chunk = up_half.shape
    down_part = down_half.shape[2]
    chunks = up_done.shape[0] + 1
    shards = width // up_part
    group = 4 * HEAD_DIM
    count = 1 + width // group
    wide = 3 * group
    vm = lambda *shape: pltpu.VMEM(shape, BF16)
    return pl.pallas_call(
        functools.partial(back_comm_kernel, 256, 512, group),
        out_shape=[
            shaped((rows, width), F32), shaped((8, width), F32), shaped((chunks, up_part, chunk), BF16),
            shaped((chunks, down_part, width), BF16), shaped((count, up_part, wide), BF16),
        ],
        in_specs=smem_spec(2) + vmem_spec(11) + any_spec(2),
        out_specs=vmem_spec(5),
        scratch_shapes=[
            vm(3, width, width), vm(3, rows, width), vm(rows, width), vm(rows, width), vm(rows, width),
            vm(3, rows, width), vm(rows, PAIR), pltpu.VMEM((rows, PAIR), F32), pltpu.VMEM((rows, PAIR), F32),
        ]
        + scatter_scratch(count, up_part, wide)
        + [
            vm(count, up_part, wide),
            vm(2, up_part, chunk // 2), vm(2, up_part, chunk // 2), vm(up_part, chunk), vm(up_part, chunk),
            vm(2, down_part, width // 2), vm(2, down_part, width // 2), vm(down_part, width), vm(down_part, width),
        ]
        + [vm(chunks, up_part, chunk)] * 3
        + [vm(chunks, down_part, width)] * 3
        + [vm(count, up_part, wide)] * 3
        + [
            pltpu.VMEM((8, width), F32), pltpu.VMEM((shards, 8, width), F32), pltpu.VMEM((8, width), F32),
            pltpu.VMEM((reps, 8, width), F32),
        ]
        + dma((count, 5), (count, 5), (1, 5), (1, 5), (1, 5), (1, 5), (2 * chunks + count, 3), (2 * chunks + count, 3),
              (shards - 1,), (shards - 1,), (reps - 1,), (reps - 1,), (2,)),
        compiler_params=pltpu.CompilerParams(
            vmem_limit_bytes=VMEM_LIMIT, collective_id=3, has_side_effects=True
        ),
    )(seq_lens, pass_idx, inputs, rows_in, out_w, log_rows, attended, hidden_grad, mlp_gain_grad,
      up_done, down_done, up_half, down_half, qkv_w, joined)


def direct(reps, inputs, seq_lens, pass_idx, pass_table, gain_attn, w_qkv, w_out, gain_mlp, w_up, w_down, cotangent):
    _, rows, width = inputs.shape
    me = lax.axis_index("shard")
    part = w_out.shape[0]
    shards = width // part
    slices = 3
    passes = pass_table.shape[0]
    lanes = w_up.shape[1] // (slices * shards)
    own = jnp.concatenate(
        [pass_table, jnp.zeros((8 - passes, part), BF16), gain_attn[None], gain_mlp[None], jnp.zeros((6, part), BF16)]
    )
    small = jnp.where(jnp.arange(width)[None, :] // part == me, jnp.tile(own, (1, shards)), BF16(0))
    qkv = w_qkv.reshape(part, 3, width).transpose(1, 0, 2)
    up = w_up.reshape(part, shards, slices, lanes).transpose(2, 0, 1, 3).reshape(slices, part, shards * lanes)
    down = w_down.reshape(slices, w_down.shape[0] // slices, width)
    ahead = 2
    rows_in, log_rows, joined, attended, hidden, qkv_w, out_w, up_have, down_have = front_comm(
        ahead, seq_lens, pass_idx, inputs[0], small, qkv, w_out, up, down
    )
    outputs, hidden_grad, mlp_gain_grad, up_done, down_done, up_half, down_half = mlp_comm(
        ahead, hidden, cotangent[0], rows_in, up_have, down_have, up, down
    )
    grad_input, small_sum, up_total, down_total, attn_total = back_comm(
        reps, seq_lens, pass_idx, inputs[0], rows_in, out_w, log_rows, attended, hidden_grad, mlp_gain_grad,
        up_done, down_done, up_half, down_half, qkv_w, joined,
    )
    small_own = lax.dynamic_slice(small_sum, (0, me * part), (8, part))
    up_grad = up_total.reshape(slices, part, shards, lanes).transpose(1, 2, 0, 3).reshape(w_up.shape)
    down_grad = down_total.reshape(w_down.shape)
    group = attn_total.shape[2] // 3
    qkv_grad = attn_total[1:].reshape(width // group, part, 3, group).transpose(1, 2, 0, 3).reshape(w_qkv.shape)
    return (
        outputs[None], grad_input[None], small_own[:passes], small_own[5], qkv_grad.astype(F32),
        attn_total[0].astype(F32), small_own[6], up_grad.astype(F32), down_grad.astype(F32),
    )


def solution(mesh):
    shards, reps = mesh.shape["shard"], mesh.shape["rep"]
    run = functools.partial(direct, reps) if (shards, reps) == (8, 4) else body
    part = P(("shard", "rep"), None, None)
    return jax.shard_map(
        run,
        mesh=mesh,
        in_specs=(
            part, P(("shard", "rep")), P(("shard", "rep")), P(None, "shard"), P("shard"), P("shard", None),
            P("shard", None), P("shard"), P("shard", None), P("shard", None), part,
        ),
        out_specs=(
            part, part, P(None, "shard"), P("shard"), P("shard", None), P("shard", None), P("shard"),
            P("shard", None), P("shard", None),
        ),
        check_vma=False,
    )
```

```python
import functools
import math

import jax
import jax.numpy as jnp
from jax import lax
from jax.experimental import pallas as pl
from jax.experimental.pallas import tpu as pltpu
from jax.sharding import PartitionSpec as P

HEADS = 12
HEAD_DIM = 64
PAIR = 2 * HEAD_DIM
EPSILON = 1e-05
MASKED = -1e30
BF16 = jnp.bfloat16
F32 = jnp.float32
VMEM_LIMIT = 64 * 1024 * 1024 - 65536

NN = (((1,), (0,)), ((), ()))
NT = (((1,), (1,)), ((), ()))
TN = (((0,), (0,)), ((), ()))


def mm(a, b, dims=NN):
    return lax.dot_general(a, b, dims, preferred_element_type=F32)


def norm_parts(values):
    average = jnp.mean(values, axis=-1, keepdims=True)
    centred = values - average
    variance = jnp.mean(centred * centred, axis=-1, keepdims=True)
    scale = lax.rsqrt(variance + EPSILON)
    return centred * scale, scale


def norm_back(unit, scale, grad, gain):
    scaled = grad * gain
    part = scaled - jnp.mean(scaled, axis=-1, keepdims=True)
    return scale * (part - unit * jnp.mean(scaled * unit, axis=-1, keepdims=True))


def lanes_of(shape):
    return lax.broadcasted_iota(jnp.int32, shape, len(shape) - 1)


def head_only(values, head, zero_at=None):
    lanes = lanes_of(values.shape)
    own = (lanes < HEAD_DIM) if head == 0 else (lanes >= HEAD_DIM)
    return jnp.where(own, values, jnp.zeros_like(values)), own, lanes


def query_with_bias(query, head):
    kept, own, lanes = head_only(query * BF16(HEAD_DIM**-0.5), head)
    spot = HEAD_DIM if head == 0 else 0
    return jnp.where(lanes == spot, jnp.ones_like(kept), kept), kept


def key_with_bias(keys, bias, head):
    kept, own, lanes = head_only(keys, head)
    spot = HEAD_DIM if head == 0 else 0
    return jnp.where(lanes == spot, bias, kept), kept


def attention_front(length, joined, attended, log_sums, key_bias, pair, block):
    rows = attended.shape[0]
    width = attended.shape[1]
    at = pl.multiple_of(pair * PAIR, PAIR)
    keys = joined[:, pl.ds(width + at, PAIR)]
    values = joined[:, pl.ds(2 * width + at, PAIR)]
    bias = key_bias[...]
    biased = [key_with_bias(keys, bias, head)[0] for head in range(2)]
    for first in range(0, rows, block):
        live = first + block
        query = joined[pl.ds(first, block), pl.ds(at, PAIR)]
        mixed = []
        sums = []
        for head in range(2):
            asked, _ = query_with_bias(query, head)
            scores = mm(asked, biased[head][:live], NT)
            row_at = lax.broadcasted_iota(jnp.int32, (block, block), 0)
            key_at = lax.broadcasted_iota(jnp.int32, (block, block), 1)
            last = jnp.where(key_at <= row_at, scores[:, first:], MASKED)
            scores = last if first == 0 else jnp.concatenate([scores[:, :first], last], axis=1)
            top = jnp.max(scores, axis=-1, keepdims=True)
            weights = jnp.exp(scores - top)
            total = jnp.sum(weights, axis=-1, keepdims=True)
            mixed.append(mm(weights.astype(BF16), values[:live]) / total)
            sums.append(top + jnp.log(total))
        lanes = lanes_of(mixed[0].shape)
        attended[pl.ds(first, block), pl.ds(at, PAIR)] = jnp.where(
            lanes < HEAD_DIM, mixed[0], mixed[1]
        ).astype(BF16)
        log_sums[pair, pl.ds(first, block), :] = jnp.where(lanes < HEAD_DIM, sums[0], sums[1])


def fill_bias(length, key_bias):
    rows = key_bias.shape[0]
    places = lax.broadcasted_iota(jnp.int32, key_bias.shape, 0)
    key_bias[...] = jnp.where(places < length, 0.0, MASKED).astype(BF16)


def front_kernel(
    block, tile, length_ref, inputs, pass_row, gain, w_qkv, w_out,
    joined_out, attended_out, sums_out, hidden_out, normed, key_bias,
):
    rows, width = inputs.shape
    length = length_ref[0]
    fill_bias(length, key_bias)

    @pl.loop(0, rows // 256)
    def _(step):
        at = pl.ds(step * 256, 256)
        entered = inputs[at, :].astype(F32) + pass_row[0:1, :]
        normed[at, :] = (norm_parts(entered)[0] * gain[0:1, :]).astype(BF16)

    @pl.loop(0, 3)
    def _(part):
        columns = pl.ds(pl.multiple_of(part * width, width), width)

        @pl.loop(0, rows // tile)
        def _(step):
            at = pl.ds(step * tile, tile)
            joined_out[at, columns] = mm(normed[at, :], w_qkv[:, columns]).astype(BF16)

    @pl.loop(0, HEADS // 2)
    def _(pair):
        attention_front(length, joined_out, attended_out, sums_out, key_bias, pair, block)

    @pl.loop(0, rows // tile)
    def _(step):
        at = pl.ds(step * tile, tile)
        entered = inputs[at, :].astype(F32) + pass_row[0:1, :]
        hidden_out[at, :] = entered + mm(attended_out[at, :], w_out[...])


def gelu_both(values):
    outer = math.sqrt(2.0 / math.pi)
    square = values * values
    bent = jnp.tanh(outer * values * (1.0 + 0.044715 * square))
    half = 0.5 * (1.0 + bent)
    slope = half + 0.5 * values * (1.0 - bent * bent) * (outer * (1.0 + 3 * 0.044715 * square))
    return values * half, slope


def mlp_kernel(
    tile, chunk, hidden, cotangent, gain, w_up, w_down,
    outputs, hidden_grad, gain_grad, up_grad, down_grad,
    second, mixed, second_grad, active, rising_grad,
):
    rows, width = hidden.shape
    chunks = w_down.shape[0] // chunk

    @pl.loop(0, rows // 256)
    def _(step):
        at = pl.ds(step * 256, 256)
        second[at, :] = (norm_parts(hidden[at, :])[0] * gain[0:1, :]).astype(BF16)
        mixed[at, :] = hidden[at, :]
        second_grad[at, :] = jnp.zeros((256, width), F32)

    @pl.loop(0, chunks)
    def _(part):
        units = pl.ds(pl.multiple_of(part * chunk, chunk), chunk)

        @pl.loop(0, rows // tile)
        def _(step):
            at = pl.ds(step * tile, tile)
            rising = mm(second[at, :], w_up[:, units])
            active_grad = mm(cotangent[at, :], w_down[units, :], NT)
            bent, slope = gelu_both(rising)
            shown = bent.astype(BF16)
            moved = (slope * active_grad).astype(BF16)
            active[at, :] = shown
            rising_grad[at, :] = moved
            mixed[at, :] += mm(shown, w_down[units, :])
            second_grad[at, :] += mm(moved, w_up[:, units], NT)

        down_grad[units, :] = mm(active[...], cotangent[...], TN).astype(BF16)
        up_grad[:, units] = mm(second[...], rising_grad[...], TN).astype(BF16)

    gain_grad[...] = jnp.zeros_like(gain_grad)

    @pl.loop(0, rows // 256)
    def _(step):
        at = pl.ds(step * 256, 256)
        outputs[at, :] = mixed[at, :].astype(BF16)
        unit, scale = norm_parts(hidden[at, :])
        grad = second_grad[at, :]
        hidden_grad[at, :] = cotangent[at, :].astype(F32) + norm_back(unit, scale, grad, gain[0:1, :])
        gain_grad[0:1, :] += jnp.sum(grad * unit, axis=0, keepdims=True)


def attention_back(joined, log_rows, grads, joined_grad, key_bias, key_total, value_total, pair, block):
    rows = grads.shape[0]
    width = grads.shape[1]
    at = pl.multiple_of(pair * PAIR, PAIR)
    keys = joined[:, pl.ds(width + at, PAIR)]
    values = joined[:, pl.ds(2 * width + at, PAIR)]
    bias = key_bias[...]
    biased = [key_with_bias(keys, bias, head) for head in range(2)]
    key_total[...] = jnp.zeros_like(key_total)
    value_total[...] = jnp.zeros_like(value_total)
    for first in range(0, rows, block):
        live = first + block
        query = joined[pl.ds(first, block), pl.ds(at, PAIR)]
        grad = grads[pl.ds(first, block), pl.ds(at, PAIR)]
        query_grad = None
        for head in range(2):
            asked, asked_only = query_with_bias(query, head)
            grad_only = head_only(grad, head)[0]
            scores = mm(biased[head][0][:live], asked, NT)
            share_grad = mm(values[:live], grad_only, NT)
            log_sum = log_rows[pl.ds(pair * 2 + head, 1), pl.ds(first, block)]
            shares = jnp.exp(scores - log_sum)
            key_at = lax.broadcasted_iota(jnp.int32, (block, block), 0)
            row_at = lax.broadcasted_iota(jnp.int32, (block, block), 1)
            last = jnp.where(key_at <= row_at, shares[first:], 0.0)
            shares = last if first == 0 else jnp.concatenate([shares[:first], last], axis=0)
            inner = jnp.sum(share_grad * shares, axis=0, keepdims=True)
            score_grad = (shares * (share_grad - inner)).astype(BF16)
            value_total[:live, :] += mm(shares.astype(BF16), grad_only)
            key_total[:live, :] += mm(score_grad, asked_only)
            part = mm(score_grad, biased[head][1][:live], TN)
            query_grad = part if query_grad is None else query_grad + part
        joined_grad[pl.ds(first, block), pl.ds(at, PAIR)] = (
            query_grad * HEAD_DIM**-0.5
        ).astype(BF16)
    joined_grad[:, pl.ds(width + at, PAIR)] = key_total[...].astype(BF16)
    joined_grad[:, pl.ds(2 * width + at, PAIR)] = value_total[...].astype(BF16)


def back_kernel(
    block, tile, length_ref, inputs, pass_row, gain, w_qkv, w_out, joined, log_rows, attended, hidden_grad,
    grad_input, gain_grad, table_grad, qkv_grad, out_grad,
    branch_grad, attended_grad, normed, joined_grad, key_bias, key_total, value_total,
):
    rows, width = inputs.shape
    length = length_ref[0]
    fill_bias(length, key_bias)

    @pl.loop(0, rows // 256)
    def _(step):
        at = pl.ds(step * 256, 256)
        branch_grad[at, :] = hidden_grad[at, :].astype(BF16)
        entered = inputs[at, :].astype(F32) + pass_row[0:1, :]
        normed[at, :] = (norm_parts(entered)[0] * gain[0:1, :]).astype(BF16)

    @pl.loop(0, rows // tile)
    def _(step):
        at = pl.ds(step * tile, tile)
        attended_grad[at, :] = mm(branch_grad[at, :], w_out[...], NT).astype(BF16)

    out_grad[...] = mm(attended[...], branch_grad[...], TN).astype(BF16)

    @pl.loop(0, HEADS // 2)
    def _(pair):
        attention_back(
            joined, log_rows, attended_grad, joined_grad, key_bias, key_total, value_total, pair, block
        )

    @pl.loop(0, 3)
    def _(part):
        columns = pl.ds(pl.multiple_of(part * width, width), width)
        qkv_grad[:, columns] = mm(normed[...], joined_grad[:, columns], TN).astype(BF16)

    gain_grad[...] = jnp.zeros_like(gain_grad)
    table_grad[...] = jnp.zeros_like(table_grad)

    @pl.loop(0, rows // 256)
    def _(step):
        at = pl.ds(step * 256, 256)
        grad = mm(joined_grad[at, :], w_qkv[...], NT)
        unit, scale = norm_parts(inputs[at, :].astype(F32) + pass_row[0:1, :])
        total = hidden_grad[at, :] + norm_back(unit, scale, grad, gain[0:1, :])
        grad_input[at, :] = total
        gain_grad[0:1, :] += jnp.sum(grad * unit, axis=0, keepdims=True)
        table_grad[0:1, :] += jnp.sum(total, axis=0, keepdims=True)


def whole(count):
    return [pl.BlockSpec(memory_space=pltpu.VMEM)] * count


def call(kernel, outs, scratch, *args, scalars=0):
    specs = [pl.BlockSpec(memory_space=pltpu.SMEM)] * scalars + whole(len(args) - scalars)
    return pl.pallas_call(
        kernel,
        out_shape=[jax.ShapeDtypeStruct(shape, kind) for shape, kind in outs],
        in_specs=specs,
        out_specs=whole(len(outs)),
        scratch_shapes=[pltpu.VMEM(shape, kind) for shape, kind in scratch],
        compiler_params=pltpu.CompilerParams(vmem_limit_bytes=VMEM_LIMIT),
    )(*args)


def body(
    inputs, seq_lens, pass_idx, pass_table, gain_attn, w_qkv, w_out, gain_mlp, w_up, w_down, cotangent,
):
    _, rows, width = inputs.shape
    inputs2 = inputs[0]
    out_cot = cotangent[0]
    gather = functools.partial(lax.all_gather, axis_name="shard", tiled=True)
    table = gather(pass_table, axis=1)
    attn_gain = jnp.broadcast_to(gather(gain_attn, axis=0).astype(F32)[None, :], (8, width))
    mlp_gain = jnp.broadcast_to(gather(gain_mlp, axis=0).astype(F32)[None, :], (8, width))
    qkv_w = gather(w_qkv, axis=0)
    out_w = gather(w_out, axis=0)
    up_w = gather(w_up, axis=0)
    down_w = gather(w_down, axis=0)
    chosen = (pass_idx[:, None] == jnp.arange(table.shape[0], dtype=jnp.int32)[None, :]).astype(F32)
    pass_row = jnp.broadcast_to(
        jnp.sum(chosen[0][:, None] * table.astype(F32), axis=0, keepdims=True), (8, width)
    )
    block = 256
    tile = 512
    joined, attended, sums, hidden = call(
        functools.partial(front_kernel, block, tile),
        [((rows, 3 * width), BF16), ((rows, width), BF16), ((HEADS // 2, rows, PAIR), F32), ((rows, width), F32)],
        [((rows, width), BF16), ((rows, PAIR), BF16)],
        seq_lens, inputs2, pass_row, attn_gain, qkv_w, out_w, scalars=1,
    )
    chunk = 1024
    outputs, hidden_grad, mlp_gain_grad, up_grad, down_grad = call(
        functools.partial(mlp_kernel, tile, chunk),
        [((rows, width), BF16), ((rows, width), F32), ((8, width), F32), (up_w.shape, BF16), (down_w.shape, BF16)],
        [((rows, width), BF16), ((rows, width), F32), ((rows, width), F32), ((rows, chunk), BF16), ((rows, chunk), BF16)],
        hidden, out_cot, mlp_gain, up_w, down_w,
    )
    log_rows = jnp.stack([sums[:, :, 0], sums[:, :, HEAD_DIM]], axis=1).reshape(HEADS, rows)
    grad_input, attn_gain_grad, table_row, qkv_grad, out_grad = call(
        functools.partial(back_kernel, block, tile),
        [((rows, width), F32), ((8, width), F32), ((8, width), F32), (qkv_w.shape, BF16), (out_w.shape, BF16)],
        [((rows, width), BF16), ((rows, width), BF16), ((rows, width), BF16), ((rows, 3 * width), BF16),
         ((rows, PAIR), BF16), ((rows, PAIR), F32), ((rows, PAIR), F32)],
        seq_lens, inputs2, pass_row, attn_gain, qkv_w, out_w, joined, log_rows, attended, hidden_grad, scalars=1,
    )
    scatter = lambda grad, dim=0: lax.psum_scatter(grad, "shard", scatter_dimension=dim, tiled=True)
    up_part, down_part = scatter(up_grad), scatter(down_grad)
    out_part, qkv_part = scatter(out_grad), scatter(qkv_grad)
    small = jnp.concatenate(
        [chosen[0][:, None] * table_row[0:1], attn_gain_grad[0:1], mlp_gain_grad[0:1]], axis=0
    )
    small = lax.psum(scatter(small, 1), "rep")
    up_sum, down_sum, out_sum, qkv_sum = lax.psum((up_part, down_part, out_part, qkv_part), "rep")
    count = table.shape[0]
    return (
        outputs[None], grad_input[None], small[:count], small[count], qkv_sum.astype(F32), out_sum.astype(F32),
        small[count + 1], up_sum.astype(F32), down_sum.astype(F32),
    )


MESH = pl.DeviceIdType.MESH


class Place:
    def __init__(self):
        self.me = lax.axis_index("shard")
        self.z = lax.axis_index("rep")
        self.core = lax.rem(self.me, 2)
        self.x = lax.rem(self.me // 2, 2)
        self.y = self.me // 4
        self.by_x = self.me + 2 - 4 * self.x
        self.by_y = self.me + 4 - 8 * self.y
        self.by_core = self.me + 1 - 2 * self.core
        self.by_both = self.by_x + 4 - 8 * self.y
        self.side = lax.rem(self.z, 2)
        self.by_z = self.z + 1 - 2 * self.side

    def at(self, shard):
        return (shard, self.z)


def remote(src, dst, sends, recvs, index, device):
    return pltpu.make_async_remote_copy(
        src_ref=src, dst_ref=dst, send_sem=sends.at[index], recv_sem=recvs.at[index],
        device_id=device, device_id_type=MESH,
    )


class Gather:
    def __init__(self, place, part, fills, sends, recvs, local, row, shared):
        self.place, self.part, self.fills, self.shared = place, part, fills, shared
        self.sends, self.recvs, self.local, self.row = sends, recvs, local, row
        self.slots = 17 if shared else 9

    def piece(self, shard, columns=None, other=False):
        if not self.shared:
            return self.part(shard, None, columns)
        side = 1 - self.place.side if other else self.place.side
        return self.part(shard, side, columns)

    def make(self, slot):
        p = self.place
        rep = p.z
        if slot < 2:
            ref, shard = self.piece(p.me), (p.by_x, p.by_y)[slot]
        elif slot == 2:
            ref, shard = self.part(p.me, None, None), p.by_core
        elif slot == 3:
            ref, shard = self.piece(p.by_x, 0), p.by_y
        elif slot == 4:
            ref, shard = self.piece(p.by_y, 1), p.by_x
        else:
            kind = (slot - 5) % 4
            source = (p.by_x, p.by_y, p.by_both, p.by_both)[kind]
            ref = self.piece(source, None if kind < 2 else kind - 2, slot >= 13)
            shard = p.by_core
            if 9 <= slot < 13:
                shard, rep = p.me, p.by_z
        return remote(ref, ref, self.sends, self.recvs, (self.row, slot), (shard, rep))

    def fill(self):
        for source, target in self.fills:
            pltpu.make_async_copy(source, target, self.local.at[self.row]).start()

    def start(self):
        own = self.part(self.place.me, None, None)
        pltpu.make_async_copy(own, own, self.local.at[self.row]).wait()
        for slot in range(3):
            self.make(slot).start()

    def pass_on(self, slot, *targets):
        self.make(slot).wait_recv()
        for target in targets:
            if target < self.slots:
                self.make(target).start()

    def relay(self):
        self.pass_on(0, 3, 5, 9)
        self.pass_on(1, 4, 6, 10)

    def finish(self):
        self.pass_on(3, 7, 11)
        self.pass_on(4, 8, 12)

    def across(self):
        if self.shared:
            for slot in range(9, 13):
                self.pass_on(slot, slot + 4)

    def ready(self):
        for slot in (2, 5, 6, 7, 8) + ((13, 14, 15, 16) if self.shared else ()):
            self.make(slot).wait_recv()

    def drain(self):
        for slot in range(self.slots):
            self.make(slot).wait_send()


def enter(place, shards, reps=()):
    barrier = pltpu.get_barrier_semaphore()
    for shard in shards:
        pl.semaphore_signal(barrier, inc=1, device_id=(shard, place.z), device_id_type=MESH)
    for rep in reps:
        pl.semaphore_signal(barrier, inc=1, device_id=(place.me, rep), device_id_type=MESH)
    pl.semaphore_wait(barrier, len(shards) + len(reps))


def part_of(ref, rows, lead, start, width):
    def part(shard, side, half):
        count = rows if side is None else rows // 2
        first = shard * rows if side is None else shard * rows + side * count
        left, wide = (start, width) if half is None else (start + half * (width // 2), width // 2)
        return ref.at[lead + (pl.ds(pl.multiple_of(first, count), count), pl.ds(left, wide))]

    return part


def up_fills(own, ref, index, place, shards):
    part, chunk = own.shape[0], ref.shape[2]
    lanes = chunk // shards
    slices = own.shape[1] // chunk
    rows = pl.ds(pl.multiple_of(place.me * part, part), part)
    return [
        (own.at[:, pl.ds((slices * shard + index) * lanes, lanes)], ref.at[index, rows, pl.ds(shard * lanes, lanes)])
        for shard in range(shards)
    ]


def down_fills(own, ref, index, place, shards):
    count = ref.shape[1] // shards
    rows = pl.ds(pl.multiple_of(place.me * count, count), count)
    return [(own.at[pl.ds(index * count, count), :], ref.at[index, rows, :])]


def attention_rows(joined, attended, log_rows, key_bias, pair, block):
    rows = attended.shape[0]
    columns = pl.ds(pl.multiple_of(pair * PAIR, PAIR), PAIR)
    keys = joined[1, :, columns]
    values = joined[2, :, columns]
    bias = key_bias[...]
    biased = [key_with_bias(keys, bias, head)[0] for head in range(2)]
    for first in range(0, rows, block):
        live = first + block
        query = joined[0, pl.ds(first, block), columns]
        mixed = []
        sums = []
        for head in range(2):
            asked, _ = query_with_bias(query, head)
            scores = mm(asked, biased[head][:live], NT)
            row_at = lax.broadcasted_iota(jnp.int32, (block, block), 0)
            key_at = lax.broadcasted_iota(jnp.int32, (block, block), 1)
            last = jnp.where(key_at <= row_at, scores[:, first:], MASKED)
            scores = last if first == 0 else jnp.concatenate([scores[:, :first], last], axis=1)
            top = jnp.max(scores, axis=-1, keepdims=True)
            weights = jnp.exp(scores - top)
            total = jnp.sum(weights, axis=-1, keepdims=True)
            mixed.append(mm(weights.astype(BF16), values[:live]) / total)
            sums.append(top + jnp.log(total))
        lanes = lanes_of(mixed[0].shape)
        attended[pl.ds(first, block), columns] = jnp.where(lanes < HEAD_DIM, mixed[0], mixed[1]).astype(BF16)
        turned = jnp.transpose(jnp.where(lanes < HEAD_DIM, sums[0], sums[1]))
        log_rows[pl.ds(pair * 2, 1), pl.ds(first, block)] = turned[0:1]
        log_rows[pl.ds(pair * 2 + 1, 1), pl.ds(first, block)] = turned[HEAD_DIM : HEAD_DIM + 1]


def norm_rows(inputs, pass_row, gain, normed):
    @pl.loop(0, inputs.shape[0] // 256)
    def _(step):
        at = pl.ds(step * 256, 256)
        entered = inputs[at, :].astype(F32) + pass_row
        normed[at, :] = (norm_parts(entered)[0] * gain).astype(BF16)


def select_lanes(place, part, width):
    rows = lax.broadcasted_iota(jnp.int32, (part, width), 0)
    lanes = lax.broadcasted_iota(jnp.int32, (part, width), 1)
    return lanes == rows + place.me * part


SHARED = (False, True, True, False, True, True, False, True, True, False)


def front_comm_kernel(
    ahead, block, tile, group,
    length_ref, pass_ref, inputs, table_own, attn_gain_own, mlp_gain_own, qkv_own, out_own, up_own, down_own,
    rows_out, log_out, normed_out, joined_out, attended_out, hidden_out, qkv_out, out_out, up_out, down_out,
    slots, small_wide, small_own, normed, joined, attended, hidden, qkv_w, out_w, up_w, down_w, key_bias,
    sends, recvs, local, small_sends, small_recvs, saves,
):
    place = Place()
    rows, width = inputs.shape
    shards = slots.shape[0]
    part = qkv_own.shape[0]
    groups = width // group

    pieces = []

    def add(part_at, fills):
        row = len(pieces)
        pieces.append(Gather(place, part_at, fills, sends, recvs, local, row, SHARED[row]))

    own_rows = pl.ds(pl.multiple_of(place.me * part, part), part)
    for index in range(groups):
        columns = pl.ds(index * group, group)
        fills = [
            (qkv_own.at[:, pl.ds(plane * width + index * group, group)], qkv_w.at[plane, own_rows, columns])
            for plane in range(3)
        ]
        add(part_of(qkv_w, part, (slice(None),), index * group, group), fills)
    add(part_of(out_w, part, (), 0, width), [(out_own, out_w.at[own_rows, :])])
    for index in range(ahead):
        add(part_of(up_w, part, (index,), 0, up_w.shape[2]), up_fills(up_own, up_w, index, place, shards))
        add(part_of(down_w, down_w.shape[1] // shards, (index,), 0, width),
            down_fills(down_own, down_w, index, place, shards))
    count = len(pieces)
    for piece in pieces:
        piece.fill()

    chosen = select_lanes(place, part, width).astype(BF16)
    small_wide[...] = jnp.zeros_like(small_wide)
    small_wide[0 : table_own.shape[0], :] = mm(table_own[...], chosen)
    small_wide[8:9, :] = mm(attn_gain_own[...], chosen)
    small_wide[9:10, :] = mm(mlp_gain_own[...], chosen)
    small_own[...] = small_wide[...].astype(BF16)
    slots[place.me] = small_own[...]

    others = [lax.rem(place.me + shift, shards) for shift in range(1, shards)]
    enter(place, others, [place.by_z])
    smalls = [
        remote(small_own, slots.at[place.me], small_sends, small_recvs, shift, place.at(other))
        for shift, other in enumerate(others)
    ]
    pieces[0].start()
    for copy in smalls:
        copy.start()
    pieces[1].start()

    def tick(index):
        if index < count:
            pieces[index].relay()
        if index + 2 < count:
            pieces[index + 2].start()
        if 0 <= index - 1 < count:
            pieces[index - 1].finish()
        if 0 <= index - 2 < count:
            pieces[index - 2].across()

    fill_bias(length_ref[0], key_bias)
    for copy in smalls:
        copy.wait_recv()
    total = slots[0].astype(F32)
    for shard in range(1, shards):
        total = total + slots[shard].astype(F32)
    places = lax.broadcasted_iota(jnp.int32, total.shape, 0)
    rows_out[0:1, :] = jnp.sum(jnp.where(places == pass_ref[0], total, 0.0), axis=0, keepdims=True)
    rows_out[1:3, :] = total[8:10]
    rows_out[3:8, :] = jnp.zeros((5, width), F32)

    tick(0)
    norm_rows(inputs, rows_out[0:1, :], rows_out[1:2, :], normed)
    tick(1)

    keep = []

    def save(source, target):
        keep.append(pltpu.make_async_copy(source, target, saves.at[len(keep)]))
        return keep[-1]

    save(normed, normed_out).start()
    pairs = width // PAIR
    per_group = group // PAIR
    joined_saves = [
        save(joined.at[:, :, pl.ds(index * group, group)], joined_out.at[:, :, pl.ds(index * group, group)])
        for index in range(groups)
    ]
    qkv_save = save(qkv_w, qkv_out)

    @pl.loop(0, pairs)
    def _(pair):
        for index in range(groups):
            @pl.when(pair == index * per_group)
            def _(index=index):
                pieces[index].ready()
                if index == groups - 1:
                    qkv_save.start()

        @pl.when(lax.rem(pair, per_group) == 0)
        def _():
            columns = pl.ds(pl.multiple_of(pair * PAIR, group), group)

            @pl.loop(0, 3)
            def _(plane):
                joined[plane, :, columns] = mm(normed[...], qkv_w[plane, :, columns]).astype(BF16)

        attention_rows(joined, attended, log_out, key_bias, pair, block)
        for index in range(pairs):
            @pl.when(pair == index)
            def _(index=index):
                if index % per_group == 0:
                    joined_saves[index // per_group].start()
                tick(index + 2)

    save(attended, attended_out).start()
    pieces[groups].ready()
    save(out_w, out_out).start()
    for step in range(rows // tile):
        at = pl.ds(step * tile, tile)
        entered = inputs[at, :].astype(F32) + rows_out[0:1, :]
        hidden[at, :] = entered + mm(attended[at, :], out_w[...])
        save(hidden.at[at, :], hidden_out.at[at, :]).start()
        tick(pairs + 2 + step)
    for index in range(pairs + 2 + rows // tile, count + 2):
        tick(index)
    late = [(ref.at[index], target.at[index]) for index in range(ahead) for ref, target in ((up_w, up_out), (down_w, down_out))]
    for piece, (source, target) in zip(pieces[groups + 1 :], late):
        piece.ready()
        save(source, target).start()
    for piece in pieces:
        piece.drain()
    for copy in smalls:
        copy.wait_send()
    for copy in keep:
        copy.wait()


def any_spec(count):
    return [pl.BlockSpec(memory_space=pl.ANY)] * count


def smem_spec(count):
    return [pl.BlockSpec(memory_space=pltpu.SMEM)] * count


def vmem_spec(count):
    return [pl.BlockSpec(memory_space=pltpu.VMEM)] * count


def shaped(shape, kind):
    return jax.ShapeDtypeStruct(shape, kind)


def front_comm(ahead, slices, seq_lens, pass_idx, inputs, table, attn_gain, mlp_gain, qkv, out, up, down):
    rows, width = inputs.shape
    shards = width // out.shape[0]
    chunk = up.shape[1] // slices
    group = 4 * HEAD_DIM
    count = width // group + 1 + 2 * ahead
    vm = lambda *shape: pltpu.VMEM(shape, BF16)
    return pl.pallas_call(
        functools.partial(front_comm_kernel, ahead, 256, 512, group),
        out_shape=[
            shaped((8, width), F32), shaped((16, rows), F32), shaped((rows, width), BF16),
            shaped((3, rows, width), BF16), shaped((rows, width), BF16), shaped((rows, width), F32),
            shaped((3, width, width), BF16), shaped((width, width), BF16), shaped((ahead, width, chunk), BF16),
            shaped((ahead, chunk, width), BF16),
        ],
        in_specs=smem_spec(2) + vmem_spec(4) + any_spec(4),
        out_specs=vmem_spec(2) + any_spec(8),
        scratch_shapes=[
            vm(shards, 16, width), pltpu.VMEM((16, width), F32), vm(16, width), vm(rows, width), vm(3, rows, width),
            vm(rows, width), pltpu.VMEM((rows, width), F32), vm(3, width, width), vm(width, width),
            vm(ahead, width, chunk), vm(ahead, chunk, width), vm(rows, PAIR),
        ]
        + dma((count, 17), (count, 17), (count,), (shards,), (shards,), (9 + width // group + 2 * ahead,)),
        compiler_params=pltpu.CompilerParams(
            vmem_limit_bytes=VMEM_LIMIT, collective_id=1, has_side_effects=True
        ),
    )(seq_lens, pass_idx, inputs, table, attn_gain, mlp_gain, qkv, out, up, down)


class Scatter:
    def __init__(self, place, grads, first, by_x, by_y, last, sends, recvs, row):
        self.place, self.grads, self.first = place, grads, first
        self.in_x, self.in_y, self.last = by_x, by_y, last
        self.sends, self.recvs, self.row = sends, recvs, row
        half = first.shape[-1] // 2
        self.left, self.right = pl.ds(0, half), pl.ds(half, half)

    def copy(self, slot, src, dst, shard):
        return remote(src, dst, self.sends, self.recvs, (self.row, slot), self.place.at(shard))

    def swap_copy(self):
        p = self.place
        return self.copy(0, self.grads.at[:, :, 1 - p.core], self.first, p.by_core)

    def spread_copies(self):
        p = self.place
        return [
            self.copy(1, self.first.at[:, 1 - p.x, :, self.left], self.in_x, p.by_x),
            self.copy(2, self.first.at[1 - p.y, :, :, self.right], self.in_y, p.by_y),
        ]

    def fold_copies(self):
        p = self.place
        return [
            self.copy(3, self.in_x.at[1 - p.y], self.last.at[:, self.left], p.by_y),
            self.copy(4, self.in_y.at[1 - p.x], self.last.at[:, self.right], p.by_x),
        ]

    def swap(self):
        self.swap_copy().start()

    def merge(self, target=None):
        p = self.place
        target = self.first if target is None else target
        self.swap_copy().wait_recv()
        for y in range(2):
            for x in range(2):
                total = self.grads[y, x, p.core].astype(F32) + self.first[y, x].astype(F32)
                target[y, x] = total.astype(BF16)

    def spread(self):
        for copy in self.spread_copies():
            copy.start()

    def fold(self):
        p = self.place
        for copy in self.spread_copies():
            copy.wait_recv()
        for other in range(2):
            total = self.first[other, p.x, :, self.left].astype(F32) + self.in_x[other].astype(F32)
            self.in_x[other] = total.astype(BF16)
            total = self.first[p.y, other, :, self.right].astype(F32) + self.in_y[other].astype(F32)
            self.in_y[other] = total.astype(BF16)
        for copy in self.fold_copies():
            copy.start()

    def close(self, target):
        p = self.place
        for copy in self.fold_copies():
            copy.wait_recv()
        target[:, self.left] = (self.last[:, self.left].astype(F32) + self.in_x[p.y].astype(F32)).astype(BF16)
        target[:, self.right] = (self.last[:, self.right].astype(F32) + self.in_y[p.x].astype(F32)).astype(BF16)

    def drain(self, swapped=True, spread=True):
        if swapped:
            self.swap_copy().wait_send()
        if spread:
            for copy in self.spread_copies() + self.fold_copies():
                copy.wait_send()


def mlp_comm_kernel(
    ahead, tile, shards,
    hidden, cotangent, rows_in, up_have, down_have, up_own, down_own,
    outputs_out, hidden_grad_out, gain_grad, up_done_out, down_done_out, up_half, down_half,
    outputs, hidden_grad, up_done, down_done, up_w, down_w, second, mixed, active, rising_grad,
    up_grads, up_first, up_x, up_y, up_last, down_grads, down_first, down_x, down_y, down_last,
    gather_sends, gather_recvs, gather_local, up_sends, up_recvs, down_sends, down_recvs, loads, saves,
):
    place = Place()
    rows, width = hidden.shape
    chunks, chunk = down_w.shape[0], down_w.shape[1]
    gain = rows_in[2:3, :]

    pieces = []
    for index in range(ahead, chunks):
        for kind in range(2):
            row = len(pieces)
            if kind == 0:
                part_at = part_of(up_w, width // shards, (index,), 0, chunk)
                fills = up_fills(up_own, up_w, index, place, shards)
            else:
                part_at = part_of(down_w, chunk // shards, (index,), 0, width)
                fills = down_fills(down_own, down_w, index, place, shards)
            pieces.append(
                Gather(place, part_at, fills, gather_sends, gather_recvs, gather_local, row, SHARED[row + 4 + 2 * ahead])
            )
    for piece in pieces:
        piece.fill()
    have = []
    for index in range(ahead):
        for ref, weights in ((up_have, up_w), (down_have, down_w)):
            have.append(pltpu.make_async_copy(ref.at[index], weights.at[index], loads.at[len(have)]))
    for copy in have:
        copy.start()
    enter(place, [place.by_x, place.by_y, place.by_core], [place.by_z])
    for piece in pieces:
        piece.start()
    keep = []

    def save(source, target):
        keep.append(pltpu.make_async_copy(source, target, saves.at[len(keep)]))
        return keep[-1]

    def up_message(index):
        return Scatter(
            place, up_grads.at[index], up_first.at[index], up_x.at[index], up_y.at[index], up_last.at[index],
            up_sends, up_recvs, index,
        )

    def down_message(index):
        return Scatter(
            place, down_grads.at[index], down_first.at[index], down_x.at[index], down_y.at[index], down_last.at[index],
            down_sends, down_recvs, index,
        )

    @pl.loop(0, rows // 256)
    def _(step):
        at = pl.ds(step * 256, 256)
        second[at, :] = (norm_parts(hidden[at, :])[0] * gain).astype(BF16)
        mixed[at, :] = hidden[at, :]
        hidden_grad[at, :] = jnp.zeros((256, width), F32)

    @pl.loop(0, chunks)
    def _(part):
        for index in range(ahead):
            @pl.when(part == index)
            def _(index=index):
                have[2 * index].wait()
                have[2 * index + 1].wait()
        for index in range(ahead, chunks):
            @pl.when(part == index)
            def _(index=index):
                pieces[2 * (index - ahead)].ready()
                pieces[2 * (index - ahead) + 1].ready()

        @pl.loop(0, rows // tile)
        def _(step):
            at = pl.ds(step * tile, tile)
            rising = mm(second[at, :], up_w[part])
            active_grad = mm(cotangent[at, :], down_w[part], NT)
            bent, slope = gelu_both(rising)
            shown = bent.astype(BF16)
            moved = (slope * active_grad).astype(BF16)
            active[at, :] = shown
            rising_grad[at, :] = moved
            mixed[at, :] += mm(shown, down_w[part])
            hidden_grad[at, :] += mm(moved, up_w[part], NT)

            @pl.when((part == 0) & (step == 0))
            def _():
                for piece in pieces[:2]:
                    piece.relay()

            @pl.when((part == 0) & (step == 1))
            def _():
                for piece in pieces[:2]:
                    piece.finish()
                for piece in pieces[2:]:
                    piece.relay()

            @pl.when((part == 1) & (step == 0))
            def _():
                for piece in pieces[2:]:
                    piece.across()

            @pl.when((part > 0) & (step == 0))
            def _():
                message = up_message(part - 1)
                message.merge()
                message.spread()

            @pl.when((part > 0) & (step == 1))
            def _():
                down_message(part - 1).fold()

        down_grads[part] = mm(active[...], cotangent[...], TN).astype(BF16).reshape(down_grads.shape[1:])
        down_message(part).swap()

        @pl.when(part == 0)
        def _():
            for piece in pieces[:2]:
                piece.across()
            for piece in pieces[2:]:
                piece.finish()

        @pl.when(part > 0)
        def _():
            up_message(part - 1).fold()

        up_grads[part] = mm(second[...], rising_grad[...], TN).astype(BF16).reshape(up_grads.shape[1:])
        up_message(part).swap()

        @pl.when(part < chunks - 1)
        def _():
            message = down_message(part)
            message.merge()
            message.spread()

        @pl.when(part > 0)
        def _():
            down_message(part - 1).close(down_done.at[part - 1])
            up_message(part - 1).close(up_done.at[part - 1])

    down_message(chunks - 1).merge(down_half)
    save(up_done, up_done_out).start()
    save(down_done, down_done_out).start()
    gain_grad[...] = jnp.zeros_like(gain_grad)

    @pl.loop(0, rows // 256)
    def _(step):
        at = pl.ds(step * 256, 256)
        outputs[at, :] = mixed[at, :].astype(BF16)
        unit, scale = norm_parts(hidden[at, :])
        grad = hidden_grad[at, :]
        hidden_grad[at, :] = cotangent[at, :].astype(F32) + norm_back(unit, scale, grad, gain)
        gain_grad[0:1, :] += jnp.sum(grad * unit, axis=0, keepdims=True)
        pltpu.make_async_copy(hidden_grad.at[at, :], hidden_grad_out.at[at, :], saves.at[4 + step]).start()

    save(outputs, outputs_out).start()
    for step in range(rows // 256):
        at = pl.ds(step * 256, 256)
        pltpu.make_async_copy(hidden_grad.at[at, :], hidden_grad_out.at[at, :], saves.at[4 + step]).wait()

    up_message(chunks - 1).merge(up_half)
    for piece in pieces:
        piece.drain()
    for index in range(chunks):
        up_message(index).drain(True, index < chunks - 1)
        down_message(index).drain(True, index < chunks - 1)
    for copy in keep:
        copy.wait()


def scatter_scratch(count, part, columns):
    return [
        pltpu.VMEM((count, 2, 2, 2, part, columns), BF16), pltpu.VMEM((count, 2, 2, part, columns), BF16),
        pltpu.VMEM((count, 2, part, columns // 2), BF16), pltpu.VMEM((count, 2, part, columns // 2), BF16),
        pltpu.VMEM((count, part, columns), BF16),
    ]


def dma(*shapes):
    return [pltpu.SemaphoreType.DMA(shape) for shape in shapes]


def mlp_comm(ahead, slices, hidden, cotangent, rows_in, up_have, down_have, up, down):
    rows, width = hidden.shape
    up_part, chunk = up.shape[0], up.shape[1] // slices
    down_part = down.shape[0] // slices
    shards = width // up_part
    late = max(1, 2 * (slices - ahead))
    vm = lambda *shape: pltpu.VMEM(shape, BF16)
    return pl.pallas_call(
        functools.partial(mlp_comm_kernel, ahead, 512, shards),
        out_shape=[
            shaped((rows, width), BF16), shaped((rows, width), F32), shaped((8, width), F32),
            shaped((slices - 1, up_part, chunk), BF16), shaped((slices - 1, down_part, width), BF16),
            shaped((2, 2, up_part, chunk), BF16), shaped((2, 2, down_part, width), BF16),
        ],
        in_specs=vmem_spec(3) + any_spec(4),
        out_specs=any_spec(2) + vmem_spec(1) + any_spec(2) + vmem_spec(2),
        scratch_shapes=[
            vm(rows, width), pltpu.VMEM((rows, width), F32),
            vm(slices - 1, up_part, chunk), vm(slices - 1, down_part, width),
            vm(slices, width, chunk), vm(slices, chunk, width),
            vm(rows, width), pltpu.VMEM((rows, width), F32), vm(rows, chunk), vm(rows, chunk),
        ]
        + scatter_scratch(slices, up_part, chunk)
        + scatter_scratch(slices, down_part, width)
        + dma((late, 17), (late, 17), (late,), (slices, 5), (slices, 5), (slices, 5), (slices, 5), (2 * ahead,),
              (4 + rows // 256,)),
        compiler_params=pltpu.CompilerParams(
            vmem_limit_bytes=VMEM_LIMIT, collective_id=2, has_side_effects=True
        ),
    )(hidden, cotangent, rows_in, up_have, down_have, up, down)


class Column:
    def __init__(self, place, block, inward, middle, outward, total, sends, recvs, row):
        self.place, self.block, self.inward, self.middle = place, block, inward, middle
        self.outward, self.total = outward, total
        self.sends, self.recvs, self.row = sends, recvs, row
        self.end = (place.z == 0) | (place.z == 3)

    def copy(self, slot, src, dst, rep):
        return remote(src, dst, self.sends, self.recvs, (self.row, slot), (self.place.me, rep))

    def in_copy(self):
        return self.copy(0, self.block, self.inward, 1 + self.place.z // 3)

    def across_copy(self):
        return self.copy(1, self.middle, self.outward, 3 - self.place.z)

    def out_copy(self):
        return self.copy(2, self.total, self.outward, 3 * (self.place.z - 1))

    def begin(self):
        @pl.when(self.end)
        def _():
            self.in_copy().start()

    def cross(self):
        @pl.when(jnp.logical_not(self.end))
        def _():
            self.in_copy().wait_recv()
            self.middle[...] = (self.block[...].astype(F32) + self.inward[...].astype(F32)).astype(BF16)
            self.across_copy().start()

    def settle(self):
        @pl.when(jnp.logical_not(self.end))
        def _():
            self.across_copy().wait_recv()
            self.total[...] = (self.middle[...].astype(F32) + self.outward[...].astype(F32)).astype(BF16)
            self.out_copy().start()

    def finish(self):
        @pl.when(self.end)
        def _():
            self.out_copy().wait_recv()
            self.total[...] = self.outward[...]
            self.in_copy().wait_send()

        @pl.when(jnp.logical_not(self.end))
        def _():
            self.across_copy().wait_send()
            self.out_copy().wait_send()


def attention_columns(joined, log_rows, grads, joined_grad, key_bias, key_total, value_total, pair, block):
    rows = grads.shape[0]
    columns = pl.ds(pl.multiple_of(pair * PAIR, PAIR), PAIR)
    keys = joined[1, :, columns]
    values = joined[2, :, columns]
    bias = key_bias[...]
    biased = [key_with_bias(keys, bias, head) for head in range(2)]
    key_total[...] = jnp.zeros_like(key_total)
    value_total[...] = jnp.zeros_like(value_total)
    for first in range(0, rows, block):
        live = first + block
        query = joined[0, pl.ds(first, block), columns]
        grad = grads[pl.ds(first, block), columns]
        query_grad = None
        for head in range(2):
            asked, asked_only = query_with_bias(query, head)
            grad_only = head_only(grad, head)[0]
            scores = mm(biased[head][0][:live], asked, NT)
            share_grad = mm(values[:live], grad_only, NT)
            log_sum = log_rows[pl.ds(pair * 2 + head, 1), pl.ds(first, block)]
            shares = jnp.exp(scores - log_sum)
            key_at = lax.broadcasted_iota(jnp.int32, (block, block), 0)
            row_at = lax.broadcasted_iota(jnp.int32, (block, block), 1)
            last = jnp.where(key_at <= row_at, shares[first:], 0.0)
            shares = last if first == 0 else jnp.concatenate([shares[:first], last], axis=0)
            inner = jnp.sum(share_grad * shares, axis=0, keepdims=True)
            score_grad = (shares * (share_grad - inner)).astype(BF16)
            value_total[:live, :] += mm(shares.astype(BF16), grad_only)
            key_total[:live, :] += mm(score_grad, asked_only)
            part = mm(score_grad, biased[head][1][:live], TN)
            query_grad = part if query_grad is None else query_grad + part
        joined_grad[0, pl.ds(first, block), columns] = (query_grad * HEAD_DIM**-0.5).astype(BF16)
    joined_grad[1, :, columns] = key_total[...].astype(BF16)
    joined_grad[2, :, columns] = value_total[...].astype(BF16)


def back_comm_kernel(
    block, tile, group,
    length_ref, pass_ref, rows_in, log_rows, mlp_gain_grad, up_done, down_done, up_half, down_half,
    hidden_grad_in, out_in, attended_in, normed_in, joined_in, qkv_in, inputs_in,
    grad_input_out, small_sum, up_total, down_total, attn_total,
    hidden_grad, out_w, attended, inputs, grad_input,
    qkv_w, joined, branch_grad, attended_grad, normed, joined_grad, key_bias, key_total, value_total,
    grads, first, in_x, in_y, last, block_sum,
    up_x, up_y, up_last, up_block, down_x, down_y, down_last, down_block,
    up_in, up_mid, up_out, down_in, down_mid, down_out, attn_in, attn_mid, attn_out,
    small_own, small_slots, small_plane, small_reps,
    sends, recvs, up_sends, up_recvs, down_sends, down_recvs, z_sends, z_recvs,
    plane_sends, plane_recvs, rep_sends, rep_recvs, loads, saves,
):
    place = Place()
    rows, width = inputs.shape
    shards = small_slots.shape[0]
    reps = small_reps.shape[0]
    chunks = up_total.shape[0]
    groups = width // group
    pairs = width // PAIR
    per_group = group // PAIR
    others = [lax.rem(place.me + shift, shards) for shift in range(1, shards)]
    others_z = [lax.rem(place.z + shift, reps) for shift in range(1, reps)]
    take = [
        pltpu.make_async_copy(source, target, loads.at[index])
        for index, (source, target) in enumerate((
            (hidden_grad_in, hidden_grad), (out_in, out_w), (attended_in, attended), (joined_in, joined),
            (normed_in, normed), (qkv_in, qkv_w), (inputs_in, inputs),
        ))
    ]
    for copy in take:
        copy.start()
    enter(place, others, others_z)

    up_late = Scatter(place, None, up_half, up_x, up_y, up_last, up_sends, up_recvs, 0)
    down_late = Scatter(place, None, down_half, down_x, down_y, down_last, down_sends, down_recvs, 0)

    def message(index):
        return Scatter(
            place, grads.at[index], first.at[index], in_x.at[index], in_y.at[index], last.at[index],
            sends, recvs, index,
        )

    out_msg = message(0)
    qkv_msg = [message(1 + index) for index in range(groups)]

    lines = {}

    def line(key, source, inward, middle, outward, total):
        lines[key] = Column(place, source, inward, middle, outward, total, z_sends, z_recvs, len(lines))

    for index in range(chunks):
        final = index == chunks - 1
        line(("d", index), down_block if final else down_done.at[index],
             down_in.at[index], down_mid.at[index], down_out.at[index], down_total.at[index])
        line(("u", index), up_block if final else up_done.at[index],
             up_in.at[index], up_mid.at[index], up_out.at[index], up_total.at[index])
    for index in range(1 + groups):
        line(("a", index), block_sum.at[index], attn_in.at[index], attn_mid.at[index], attn_out.at[index],
             attn_total.at[index])

    down_late.spread()
    up_late.spread()
    for index in range(chunks - 1):
        lines["d", index].begin()
        lines["u", index].begin()

    fill_bias(length_ref[0], key_bias)
    take[0].wait()
    take[1].wait()

    @pl.loop(0, rows // tile)
    def _(step):
        at = pl.ds(step * tile, tile)
        shown = hidden_grad[at, :].astype(BF16)
        branch_grad[at, :] = shown
        attended_grad[at, :] = mm(shown, out_w[...], NT).astype(BF16)

    lines["d", 0].cross()
    take[2].wait()
    grads[0] = mm(attended[...], branch_grad[...], TN).astype(BF16).reshape(grads.shape[1:])
    out_msg.swap()
    down_late.fold()
    for copy in take[3:]:
        copy.wait()

    def late_close(message, target, key):
        message.close(target)
        lines[key].begin()

    def close(index):
        message(index).close(block_sum.at[index])
        lines["a", index].begin()

    def send(index):
        message(index).merge()
        message(index).spread()

    after_pair = [
        lambda: (lines["u", 0].cross(), up_late.fold(), send(0), lines["d", 0].settle()),
        lambda: (lines["d", 1].cross(), lines["u", 1].cross(), late_close(down_late, down_block, ("d", 2)),
                 late_close(up_late, up_block, ("u", 2)), lines["u", 0].settle(), out_msg.fold()),
        lambda: (send(1),),
        lambda: (lines["d", 1].settle(), lines["u", 1].settle(), lines["d", 2].cross(), lines["u", 2].cross(),
                 close(0), qkv_msg[0].fold()),
        lambda: (send(2), close(1)),
        lambda: (lines["a", 0].cross(), lines["d", 2].settle(), lines["u", 2].settle(), lines["a", 1].cross(),
                 qkv_msg[1].fold()),
    ]

    @pl.loop(0, pairs)
    def _(pair):
        attention_columns(
            joined, log_rows, attended_grad, joined_grad, key_bias, key_total, value_total, pair, block
        )

        @pl.when(lax.rem(pair, per_group) == per_group - 1)
        def _():
            index = pair // per_group
            columns = pl.ds(pl.multiple_of(index * group, group), group)
            for plane in range(3):
                part = mm(normed[...], joined_grad[plane, :, columns], TN).astype(BF16)
                grads[1 + index, :, :, :, :, pl.ds(plane * group, group)] = part.reshape(
                    grads.shape[1:5] + (group,)
                )
            message(1 + index).swap()

        for index in range(pairs):
            @pl.when(pair == index)
            def _(index=index):
                after_pair[index]()

    small_own[...] = jnp.zeros_like(small_own)

    def after_rows(step):
        @pl.when(step == 0)
        def _():
            send(3)
            close(2)

        @pl.when(step == 1)
        def _():
            lines["a", 0].settle()

        @pl.when(step == 3)
        def _():
            qkv_msg[2].fold()
            lines["a", 1].settle()
            lines["a", 2].cross()

    @pl.loop(0, rows // 256)
    def _(step):
        at = pl.ds(step * 256, 256)
        grad = mm(joined_grad[0, at, :], qkv_w[0], NT)
        grad = grad + mm(joined_grad[1, at, :], qkv_w[1], NT)
        grad = grad + mm(joined_grad[2, at, :], qkv_w[2], NT)
        unit, scale = norm_parts(inputs[at, :].astype(F32) + rows_in[0:1, :])
        total = hidden_grad[at, :] + norm_back(unit, scale, grad, rows_in[1:2, :])
        grad_input[at, :] = total
        small_own[5:6, :] += jnp.sum(grad * unit, axis=0, keepdims=True)
        small_own[0:1, :] += jnp.sum(total, axis=0, keepdims=True)
        pltpu.make_async_copy(grad_input.at[at, :], grad_input_out.at[at, :], saves.at[step]).start()
        after_rows(step)

    places = lax.broadcasted_iota(jnp.int32, small_own.shape, 0)
    own = small_own[...]
    table = jnp.where((places == pass_ref[0]) & (places < 5), own[0:1], 0.0)
    own = jnp.where(places == 5, own, table)
    small_own[...] = jnp.where(places == 6, mlp_gain_grad[0:1], own)
    small_slots[place.me] = small_own[...]
    plane_copies = [
        remote(small_own, small_slots.at[place.me], plane_sends, plane_recvs, shift, place.at(other))
        for shift, other in enumerate(others)
    ]
    for copy in plane_copies:
        copy.start()
    close(3)
    lines["a", 2].settle()
    for copy in plane_copies:
        copy.wait_recv()
    total = small_slots[0]
    for shard in range(1, shards):
        total = total + small_slots[shard]
    small_plane[...] = total
    small_reps[place.z] = total
    rep_copies = [
        remote(small_plane, small_reps.at[place.z], rep_sends, rep_recvs, shift, (place.me, other))
        for shift, other in enumerate(others_z)
    ]
    for copy in rep_copies:
        copy.start()
    lines["a", 3].cross()
    for copy in rep_copies:
        copy.wait_recv()
    total = small_reps[0]
    for rep in range(1, reps):
        total = total + small_reps[rep]
    small_sum[...] = total
    lines["a", 3].settle()
    for key in lines:
        lines[key].finish()
    for index in range(1 + groups):
        message(index).drain()
    up_late.drain(swapped=False)
    down_late.drain(swapped=False)
    for copy in plane_copies + rep_copies:
        copy.wait_send()
    for step in range(rows // 256):
        at = pl.ds(step * 256, 256)
        pltpu.make_async_copy(grad_input.at[at, :], grad_input_out.at[at, :], saves.at[step]).wait()


def back_comm(reps, seq_lens, pass_idx, rows_in, log_rows, mlp_gain_grad, up_done, down_done, up_half, down_half,
              hidden_grad, out_w, attended, normed, joined, qkv_w, inputs):
    rows, width = inputs.shape
    _, _, up_part, chunk = up_half.shape
    down_part = down_half.shape[2]
    chunks = up_done.shape[0] + 1
    shards = width // up_part
    group = 4 * HEAD_DIM
    count = 1 + width // group
    wide = 3 * group
    vm = lambda *shape: pltpu.VMEM(shape, BF16)
    vf = lambda *shape: pltpu.VMEM(shape, F32)
    return pl.pallas_call(
        functools.partial(back_comm_kernel, 256, 512, group),
        out_shape=[
            shaped((rows, width), F32), shaped((8, width), F32), shaped((chunks, up_part, chunk), BF16),
            shaped((chunks, down_part, width), BF16), shaped((count, up_part, wide), BF16),
        ],
        in_specs=smem_spec(2) + vmem_spec(7) + any_spec(7),
        out_specs=any_spec(1) + vmem_spec(4),
        scratch_shapes=[
            vf(rows, width), vm(width, width), vm(rows, width), vm(rows, width), vf(rows, width),
            vm(3, width, width), vm(3, rows, width), vm(rows, width), vm(rows, width), vm(rows, width),
            vm(3, rows, width), vm(rows, PAIR), vf(rows, PAIR), vf(rows, PAIR),
        ]
        + scatter_scratch(count, up_part, wide)
        + [
            vm(count, up_part, wide),
            vm(2, up_part, chunk // 2), vm(2, up_part, chunk // 2), vm(up_part, chunk), vm(up_part, chunk),
            vm(2, down_part, width // 2), vm(2, down_part, width // 2), vm(down_part, width), vm(down_part, width),
        ]
        + [vm(chunks, up_part, chunk)] * 3
        + [vm(chunks, down_part, width)] * 3
        + [vm(count, up_part, wide)] * 3
        + [vf(8, width), vf(shards, 8, width), vf(8, width), vf(reps, 8, width)]
        + dma((count, 5), (count, 5), (1, 5), (1, 5), (1, 5), (1, 5), (2 * chunks + count, 3), (2 * chunks + count, 3),
              (shards - 1,), (shards - 1,), (reps - 1,), (reps - 1,), (7,), (rows // 256,)),
        compiler_params=pltpu.CompilerParams(
            vmem_limit_bytes=VMEM_LIMIT, collective_id=3, has_side_effects=True
        ),
    )(seq_lens, pass_idx, rows_in, log_rows, mlp_gain_grad, up_done, down_done, up_half, down_half,
      hidden_grad, out_w, attended, normed, joined, qkv_w, inputs)


def place_kernel(
    small_sum, outputs_in, grad_input_in, up_in, down_in, attn_in,
    table_out, attn_gain_out, mlp_gain_out, outputs_out, grad_input_out, qkv_out, out_out, up_out, down_out,
    outputs, grad_input, up_total, down_total, attn_total, qkv, out, up, down, loads, saves,
):
    slices, part, chunk = up_in.shape
    width = small_sum.shape[1]
    shards = width // part
    lanes = chunk // shards
    groups = attn_in.shape[0] - 1
    group = attn_in.shape[2] // 3
    take = [
        pltpu.make_async_copy(source, target, loads.at[index])
        for index, (source, target) in enumerate((
            (grad_input_in, grad_input), (up_in, up_total), (attn_in, attn_total), (down_in, down_total),
            (outputs_in, outputs),
        ))
    ]
    give = [
        pltpu.make_async_copy(source, target, saves.at[index])
        for index, (source, target) in enumerate((
            (grad_input, grad_input_out), (up, up_out), (qkv, qkv_out), (out, out_out), (down, down_out),
            (outputs, outputs_out),
        ))
    ]
    for copy in take:
        copy.start()
    first = lax.axis_index("shard") * part
    rows_at = lax.broadcasted_iota(jnp.int32, (width, part), 0)
    lanes_at = lax.broadcasted_iota(jnp.int32, (width, part), 1)
    chosen = (rows_at == lanes_at + first).astype(F32)
    own = lax.dot_general(small_sum[...], chosen, NN, precision=lax.Precision.HIGHEST, preferred_element_type=F32)
    table_out[...] = own[0 : table_out.shape[0]]
    attn_gain_out[...] = own[5:6]
    mlp_gain_out[...] = own[6:7]
    take[0].wait()
    give[0].start()
    take[1].wait()
    for index in range(slices):
        for shard in range(shards):
            up[:, (slices * shard + index) * lanes : (slices * shard + index + 1) * lanes] = up_total[
                index, :, shard * lanes : (shard + 1) * lanes
            ].astype(F32)
    give[1].start()
    take[2].wait()
    for index in range(groups):
        for plane in range(3):
            start = plane * width + index * group
            qkv[:, start : start + group] = attn_total[1 + index, :, plane * group : (plane + 1) * group].astype(F32)
    out[...] = attn_total[0].astype(F32)
    give[2].start()
    give[3].start()
    take[3].wait()
    count = down_total.shape[1]
    for index in range(slices):
        down[index * count : (index + 1) * count, :] = down_total[index].astype(F32)
    give[4].start()
    take[4].wait()
    give[5].start()
    for copy in give:
        copy.wait()


def finish_places(passes, small_sum, outputs, grad_input, up_total, down_total, attn_total):
    rows, width = outputs.shape
    slices, part, chunk = up_total.shape
    down_rows = slices * down_total.shape[1]
    vf = lambda *shape: pltpu.VMEM(shape, F32)
    like = lambda ref: pltpu.VMEM(ref.shape, ref.dtype)
    return pl.pallas_call(
        place_kernel,
        out_shape=[
            shaped((passes, part), F32), shaped((1, part), F32), shaped((1, part), F32), shaped((rows, width), BF16),
            shaped((rows, width), F32), shaped((part, 3 * width), F32), shaped((part, width), F32),
            shaped((part, slices * chunk), F32), shaped((down_rows, width), F32),
        ],
        in_specs=vmem_spec(1) + any_spec(5),
        out_specs=vmem_spec(3) + any_spec(6),
        scratch_shapes=[
            like(outputs), like(grad_input), like(up_total), like(down_total), like(attn_total),
            vf(part, 3 * width), vf(part, width), vf(part, slices * chunk), vf(down_rows, width),
        ]
        + dma((5,), (6,)),
        compiler_params=pltpu.CompilerParams(vmem_limit_bytes=VMEM_LIMIT),
    )(small_sum, outputs, grad_input, up_total, down_total, attn_total)


def direct(reps, inputs, seq_lens, pass_idx, pass_table, gain_attn, w_qkv, w_out, gain_mlp, w_up, w_down, cotangent):
    slices = 3
    ahead = 2
    rows_in, log_rows, normed, joined, attended, hidden, qkv_w, out_w, up_have, down_have = front_comm(
        ahead, slices, seq_lens, pass_idx, inputs[0], pass_table, gain_attn[None], gain_mlp[None], w_qkv, w_out,
        w_up, w_down,
    )
    outputs, hidden_grad, mlp_gain_grad, up_done, down_done, up_half, down_half = mlp_comm(
        ahead, slices, hidden, cotangent[0], rows_in, up_have, down_have, w_up, w_down
    )
    grad_input, small_sum, up_total, down_total, attn_total = back_comm(
        reps, seq_lens, pass_idx, rows_in, log_rows, mlp_gain_grad, up_done, down_done, up_half, down_half,
        hidden_grad, out_w, attended, normed, joined, qkv_w, inputs[0],
    )
    table, attn_gain, mlp_gain, outputs, grad_input, qkv, out, up, down = finish_places(
        pass_table.shape[0], small_sum, outputs, grad_input, up_total, down_total, attn_total
    )
    return (outputs[None], grad_input[None], table, attn_gain[0], qkv, out, mlp_gain[0], up, down)


def solution(mesh):
    shards, reps = mesh.shape["shard"], mesh.shape["rep"]
    run = functools.partial(direct, reps) if (shards, reps) == (8, 4) else body
    part = P(("shard", "rep"), None, None)
    return jax.shard_map(
        run,
        mesh=mesh,
        in_specs=(
            part, P(("shard", "rep")), P(("shard", "rep")), P(None, "shard"), P("shard"), P("shard", None),
            P("shard", None), P("shard"), P("shard", None), P("shard", None), part,
        ),
        out_specs=(
            part, part, P(None, "shard"), P("shard"), P("shard", None), P("shard", None), P("shard"),
            P("shard", None), P("shard", None),
        ),
        check_vma=False,
    )
```

```python
import functools
import math

import jax
import jax.numpy as jnp
from jax import lax
from jax.experimental import pallas as pl
from jax.experimental.pallas import tpu as pltpu
from jax.sharding import PartitionSpec as P

HEADS = 12
HEAD_DIM = 64
PAIR = 2 * HEAD_DIM
EPSILON = 1e-05
MASKED = -1e30
BF16 = jnp.bfloat16
F32 = jnp.float32
VMEM_LIMIT = 64 * 1024 * 1024 - 65536

NN = (((1,), (0,)), ((), ()))
NT = (((1,), (1,)), ((), ()))
TN = (((0,), (0,)), ((), ()))


def mm(a, b, dims=NN):
    return lax.dot_general(a, b, dims, preferred_element_type=F32)


def norm_parts(values):
    average = jnp.mean(values, axis=-1, keepdims=True)
    centred = values - average
    variance = jnp.mean(centred * centred, axis=-1, keepdims=True)
    scale = lax.rsqrt(variance + EPSILON)
    return centred * scale, scale


def norm_back(unit, scale, grad, gain):
    scaled = grad * gain
    part = scaled - jnp.mean(scaled, axis=-1, keepdims=True)
    return scale * (part - unit * jnp.mean(scaled * unit, axis=-1, keepdims=True))


def lanes_of(shape):
    return lax.broadcasted_iota(jnp.int32, shape, len(shape) - 1)


def head_only(values, head, zero_at=None):
    lanes = lanes_of(values.shape)
    own = (lanes < HEAD_DIM) if head == 0 else (lanes >= HEAD_DIM)
    return jnp.where(own, values, jnp.zeros_like(values)), own, lanes


def query_with_bias(query, head):
    kept, own, lanes = head_only(query * BF16(HEAD_DIM**-0.5), head)
    spot = HEAD_DIM if head == 0 else 0
    return jnp.where(lanes == spot, jnp.ones_like(kept), kept), kept


def key_with_bias(keys, bias, head):
    kept, own, lanes = head_only(keys, head)
    spot = HEAD_DIM if head == 0 else 0
    return jnp.where(lanes == spot, bias, kept), kept


def attention_front(length, joined, attended, log_sums, key_bias, pair, block):
    rows = attended.shape[0]
    width = attended.shape[1]
    at = pl.multiple_of(pair * PAIR, PAIR)
    keys = joined[:, pl.ds(width + at, PAIR)]
    values = joined[:, pl.ds(2 * width + at, PAIR)]
    bias = key_bias[...]
    biased = [key_with_bias(keys, bias, head)[0] for head in range(2)]
    for first in range(0, rows, block):
        live = first + block
        query = joined[pl.ds(first, block), pl.ds(at, PAIR)]
        mixed = []
        sums = []
        for head in range(2):
            asked, _ = query_with_bias(query, head)
            scores = mm(asked, biased[head][:live], NT)
            row_at = lax.broadcasted_iota(jnp.int32, (block, block), 0)
            key_at = lax.broadcasted_iota(jnp.int32, (block, block), 1)
            last = jnp.where(key_at <= row_at, scores[:, first:], MASKED)
            scores = last if first == 0 else jnp.concatenate([scores[:, :first], last], axis=1)
            top = jnp.max(scores, axis=-1, keepdims=True)
            weights = jnp.exp(scores - top)
            total = jnp.sum(weights, axis=-1, keepdims=True)
            mixed.append(mm(weights.astype(BF16), values[:live]) / total)
            sums.append(top + jnp.log(total))
        lanes = lanes_of(mixed[0].shape)
        attended[pl.ds(first, block), pl.ds(at, PAIR)] = jnp.where(
            lanes < HEAD_DIM, mixed[0], mixed[1]
        ).astype(BF16)
        log_sums[pair, pl.ds(first, block), :] = jnp.where(lanes < HEAD_DIM, sums[0], sums[1])


def fill_bias(length, key_bias):
    rows = key_bias.shape[0]
    places = lax.broadcasted_iota(jnp.int32, key_bias.shape, 0)
    key_bias[...] = jnp.where(places < length, 0.0, MASKED).astype(BF16)


def front_kernel(
    block, tile, length_ref, inputs, pass_row, gain, w_qkv, w_out,
    joined_out, attended_out, sums_out, hidden_out, normed, key_bias,
):
    rows, width = inputs.shape
    length = length_ref[0]
    fill_bias(length, key_bias)

    @pl.loop(0, rows // 256)
    def _(step):
        at = pl.ds(step * 256, 256)
        entered = inputs[at, :].astype(F32) + pass_row[0:1, :]
        normed[at, :] = (norm_parts(entered)[0] * gain[0:1, :]).astype(BF16)

    @pl.loop(0, 3)
    def _(part):
        columns = pl.ds(pl.multiple_of(part * width, width), width)

        @pl.loop(0, rows // tile)
        def _(step):
            at = pl.ds(step * tile, tile)
            joined_out[at, columns] = mm(normed[at, :], w_qkv[:, columns]).astype(BF16)

    @pl.loop(0, HEADS // 2)
    def _(pair):
        attention_front(length, joined_out, attended_out, sums_out, key_bias, pair, block)

    @pl.loop(0, rows // tile)
    def _(step):
        at = pl.ds(step * tile, tile)
        entered = inputs[at, :].astype(F32) + pass_row[0:1, :]
        hidden_out[at, :] = entered + mm(attended_out[at, :], w_out[...])


def gelu_both(values):
    outer = math.sqrt(2.0 / math.pi)
    square = values * values
    bent = jnp.tanh(outer * values * (1.0 + 0.044715 * square))
    half = 0.5 * (1.0 + bent)
    slope = half + 0.5 * values * (1.0 - bent * bent) * (outer * (1.0 + 3 * 0.044715 * square))
    return values * half, slope


def mlp_kernel(
    tile, chunk, hidden, cotangent, gain, w_up, w_down,
    outputs, hidden_grad, gain_grad, up_grad, down_grad,
    second, mixed, second_grad, active, rising_grad,
):
    rows, width = hidden.shape
    chunks = w_down.shape[0] // chunk

    @pl.loop(0, rows // 256)
    def _(step):
        at = pl.ds(step * 256, 256)
        second[at, :] = (norm_parts(hidden[at, :])[0] * gain[0:1, :]).astype(BF16)
        mixed[at, :] = hidden[at, :]
        second_grad[at, :] = jnp.zeros((256, width), F32)

    @pl.loop(0, chunks)
    def _(part):
        units = pl.ds(pl.multiple_of(part * chunk, chunk), chunk)

        @pl.loop(0, rows // tile)
        def _(step):
            at = pl.ds(step * tile, tile)
            rising = mm(second[at, :], w_up[:, units])
            active_grad = mm(cotangent[at, :], w_down[units, :], NT)
            bent, slope = gelu_both(rising)
            shown = bent.astype(BF16)
            moved = (slope * active_grad).astype(BF16)
            active[at, :] = shown
            rising_grad[at, :] = moved
            mixed[at, :] += mm(shown, w_down[units, :])
            second_grad[at, :] += mm(moved, w_up[:, units], NT)

        down_grad[units, :] = mm(active[...], cotangent[...], TN).astype(BF16)
        up_grad[:, units] = mm(second[...], rising_grad[...], TN).astype(BF16)

    gain_grad[...] = jnp.zeros_like(gain_grad)

    @pl.loop(0, rows // 256)
    def _(step):
        at = pl.ds(step * 256, 256)
        outputs[at, :] = mixed[at, :].astype(BF16)
        unit, scale = norm_parts(hidden[at, :])
        grad = second_grad[at, :]
        hidden_grad[at, :] = cotangent[at, :].astype(F32) + norm_back(unit, scale, grad, gain[0:1, :])
        gain_grad[0:1, :] += jnp.sum(grad * unit, axis=0, keepdims=True)


def attention_back(joined, log_rows, grads, joined_grad, key_bias, key_total, value_total, pair, block):
    rows = grads.shape[0]
    width = grads.shape[1]
    at = pl.multiple_of(pair * PAIR, PAIR)
    keys = joined[:, pl.ds(width + at, PAIR)]
    values = joined[:, pl.ds(2 * width + at, PAIR)]
    bias = key_bias[...]
    biased = [key_with_bias(keys, bias, head) for head in range(2)]
    key_total[...] = jnp.zeros_like(key_total)
    value_total[...] = jnp.zeros_like(value_total)
    for first in range(0, rows, block):
        live = first + block
        query = joined[pl.ds(first, block), pl.ds(at, PAIR)]
        grad = grads[pl.ds(first, block), pl.ds(at, PAIR)]
        query_grad = None
        for head in range(2):
            asked, asked_only = query_with_bias(query, head)
            grad_only = head_only(grad, head)[0]
            scores = mm(biased[head][0][:live], asked, NT)
            share_grad = mm(values[:live], grad_only, NT)
            log_sum = log_rows[pl.ds(pair * 2 + head, 1), pl.ds(first, block)]
            shares = jnp.exp(scores - log_sum)
            key_at = lax.broadcasted_iota(jnp.int32, (block, block), 0)
            row_at = lax.broadcasted_iota(jnp.int32, (block, block), 1)
            last = jnp.where(key_at <= row_at, shares[first:], 0.0)
            shares = last if first == 0 else jnp.concatenate([shares[:first], last], axis=0)
            inner = jnp.sum(share_grad * shares, axis=0, keepdims=True)
            score_grad = (shares * (share_grad - inner)).astype(BF16)
            value_total[:live, :] += mm(shares.astype(BF16), grad_only)
            key_total[:live, :] += mm(score_grad, asked_only)
            part = mm(score_grad, biased[head][1][:live], TN)
            query_grad = part if query_grad is None else query_grad + part
        joined_grad[pl.ds(first, block), pl.ds(at, PAIR)] = (
            query_grad * HEAD_DIM**-0.5
        ).astype(BF16)
    joined_grad[:, pl.ds(width + at, PAIR)] = key_total[...].astype(BF16)
    joined_grad[:, pl.ds(2 * width + at, PAIR)] = value_total[...].astype(BF16)


def back_kernel(
    block, tile, length_ref, inputs, pass_row, gain, w_qkv, w_out, joined, log_rows, attended, hidden_grad,
    grad_input, gain_grad, table_grad, qkv_grad, out_grad,
    branch_grad, attended_grad, normed, joined_grad, key_bias, key_total, value_total,
):
    rows, width = inputs.shape
    length = length_ref[0]
    fill_bias(length, key_bias)

    @pl.loop(0, rows // 256)
    def _(step):
        at = pl.ds(step * 256, 256)
        branch_grad[at, :] = hidden_grad[at, :].astype(BF16)
        entered = inputs[at, :].astype(F32) + pass_row[0:1, :]
        normed[at, :] = (norm_parts(entered)[0] * gain[0:1, :]).astype(BF16)

    @pl.loop(0, rows // tile)
    def _(step):
        at = pl.ds(step * tile, tile)
        attended_grad[at, :] = mm(branch_grad[at, :], w_out[...], NT).astype(BF16)

    out_grad[...] = mm(attended[...], branch_grad[...], TN).astype(BF16)

    @pl.loop(0, HEADS // 2)
    def _(pair):
        attention_back(
            joined, log_rows, attended_grad, joined_grad, key_bias, key_total, value_total, pair, block
        )

    @pl.loop(0, 3)
    def _(part):
        columns = pl.ds(pl.multiple_of(part * width, width), width)
        qkv_grad[:, columns] = mm(normed[...], joined_grad[:, columns], TN).astype(BF16)

    gain_grad[...] = jnp.zeros_like(gain_grad)
    table_grad[...] = jnp.zeros_like(table_grad)

    @pl.loop(0, rows // 256)
    def _(step):
        at = pl.ds(step * 256, 256)
        grad = mm(joined_grad[at, :], w_qkv[...], NT)
        unit, scale = norm_parts(inputs[at, :].astype(F32) + pass_row[0:1, :])
        total = hidden_grad[at, :] + norm_back(unit, scale, grad, gain[0:1, :])
        grad_input[at, :] = total
        gain_grad[0:1, :] += jnp.sum(grad * unit, axis=0, keepdims=True)
        table_grad[0:1, :] += jnp.sum(total, axis=0, keepdims=True)


def whole(count):
    return [pl.BlockSpec(memory_space=pltpu.VMEM)] * count


def call(kernel, outs, scratch, *args, scalars=0):
    specs = [pl.BlockSpec(memory_space=pltpu.SMEM)] * scalars + whole(len(args) - scalars)
    return pl.pallas_call(
        kernel,
        out_shape=[jax.ShapeDtypeStruct(shape, kind) for shape, kind in outs],
        in_specs=specs,
        out_specs=whole(len(outs)),
        scratch_shapes=[pltpu.VMEM(shape, kind) for shape, kind in scratch],
        compiler_params=pltpu.CompilerParams(vmem_limit_bytes=VMEM_LIMIT),
    )(*args)


def body(
    inputs, seq_lens, pass_idx, pass_table, gain_attn, w_qkv, w_out, gain_mlp, w_up, w_down, cotangent,
):
    _, rows, width = inputs.shape
    inputs2 = inputs[0]
    out_cot = cotangent[0]
    gather = functools.partial(lax.all_gather, axis_name="shard", tiled=True)
    table = gather(pass_table, axis=1)
    attn_gain = jnp.broadcast_to(gather(gain_attn, axis=0).astype(F32)[None, :], (8, width))
    mlp_gain = jnp.broadcast_to(gather(gain_mlp, axis=0).astype(F32)[None, :], (8, width))
    qkv_w = gather(w_qkv, axis=0)
    out_w = gather(w_out, axis=0)
    up_w = gather(w_up, axis=0)
    down_w = gather(w_down, axis=0)
    chosen = (pass_idx[:, None] == jnp.arange(table.shape[0], dtype=jnp.int32)[None, :]).astype(F32)
    pass_row = jnp.broadcast_to(
        jnp.sum(chosen[0][:, None] * table.astype(F32), axis=0, keepdims=True), (8, width)
    )
    block = 256
    tile = 512
    joined, attended, sums, hidden = call(
        functools.partial(front_kernel, block, tile),
        [((rows, 3 * width), BF16), ((rows, width), BF16), ((HEADS // 2, rows, PAIR), F32), ((rows, width), F32)],
        [((rows, width), BF16), ((rows, PAIR), BF16)],
        seq_lens, inputs2, pass_row, attn_gain, qkv_w, out_w, scalars=1,
    )
    chunk = 1024
    outputs, hidden_grad, mlp_gain_grad, up_grad, down_grad = call(
        functools.partial(mlp_kernel, tile, chunk),
        [((rows, width), BF16), ((rows, width), F32), ((8, width), F32), (up_w.shape, BF16), (down_w.shape, BF16)],
        [((rows, width), BF16), ((rows, width), F32), ((rows, width), F32), ((rows, chunk), BF16), ((rows, chunk), BF16)],
        hidden, out_cot, mlp_gain, up_w, down_w,
    )
    log_rows = jnp.stack([sums[:, :, 0], sums[:, :, HEAD_DIM]], axis=1).reshape(HEADS, rows)
    grad_input, attn_gain_grad, table_row, qkv_grad, out_grad = call(
        functools.partial(back_kernel, block, tile),
        [((rows, width), F32), ((8, width), F32), ((8, width), F32), (qkv_w.shape, BF16), (out_w.shape, BF16)],
        [((rows, width), BF16), ((rows, width), BF16), ((rows, width), BF16), ((rows, 3 * width), BF16),
         ((rows, PAIR), BF16), ((rows, PAIR), F32), ((rows, PAIR), F32)],
        seq_lens, inputs2, pass_row, attn_gain, qkv_w, out_w, joined, log_rows, attended, hidden_grad, scalars=1,
    )
    scatter = lambda grad, dim=0: lax.psum_scatter(grad, "shard", scatter_dimension=dim, tiled=True)
    up_part, down_part = scatter(up_grad), scatter(down_grad)
    out_part, qkv_part = scatter(out_grad), scatter(qkv_grad)
    small = jnp.concatenate(
        [chosen[0][:, None] * table_row[0:1], attn_gain_grad[0:1], mlp_gain_grad[0:1]], axis=0
    )
    small = lax.psum(scatter(small, 1), "rep")
    up_sum, down_sum, out_sum, qkv_sum = lax.psum((up_part, down_part, out_part, qkv_part), "rep")
    count = table.shape[0]
    return (
        outputs[None], grad_input[None], small[:count], small[count], qkv_sum.astype(F32), out_sum.astype(F32),
        small[count + 1], up_sum.astype(F32), down_sum.astype(F32),
    )


MESH = pl.DeviceIdType.MESH


class Place:
    def __init__(self):
        self.me = lax.axis_index("shard")
        self.z = lax.axis_index("rep")
        self.core = lax.rem(self.me, 2)
        self.x = lax.rem(self.me // 2, 2)
        self.y = self.me // 4
        self.by_x = self.me + 2 - 4 * self.x
        self.by_y = self.me + 4 - 8 * self.y
        self.by_core = self.me + 1 - 2 * self.core
        self.by_both = self.by_x + 4 - 8 * self.y
        self.side = lax.rem(self.z, 2)
        self.by_z = self.z + 1 - 2 * self.side

    def at(self, shard):
        return (shard, self.z)


def remote(src, dst, sends, recvs, index, device):
    return pltpu.make_async_remote_copy(
        src_ref=src, dst_ref=dst, send_sem=sends.at[index], recv_sem=recvs.at[index],
        device_id=device, device_id_type=MESH,
    )


class Gather:
    def __init__(self, place, part, fills, sends, recvs, local, row, shared):
        self.place, self.part, self.fills, self.shared = place, part, fills, shared
        self.sends, self.recvs, self.local, self.row = sends, recvs, local, row
        self.slots = 17 if shared else 9

    def piece(self, shard, columns=None, other=False):
        if not self.shared:
            return self.part(shard, None, columns)
        side = 1 - self.place.side if other else self.place.side
        return self.part(shard, side, columns)

    def make(self, slot):
        p = self.place
        rep = p.z
        if slot < 2:
            ref, shard = self.piece(p.me), (p.by_x, p.by_y)[slot]
        elif slot == 2:
            ref, shard = self.part(p.me, None, None), p.by_core
        elif slot == 3:
            ref, shard = self.piece(p.by_x, 0), p.by_y
        elif slot == 4:
            ref, shard = self.piece(p.by_y, 1), p.by_x
        else:
            kind = (slot - 5) % 4
            source = (p.by_x, p.by_y, p.by_both, p.by_both)[kind]
            ref = self.piece(source, None if kind < 2 else kind - 2, slot >= 13)
            shard = p.by_core
            if 9 <= slot < 13:
                shard, rep = p.me, p.by_z
        return remote(ref, ref, self.sends, self.recvs, (self.row, slot), (shard, rep))

    def fill(self):
        for source, target in self.fills:
            pltpu.make_async_copy(source, target, self.local.at[self.row]).start()

    def start(self):
        own = self.part(self.place.me, None, None)
        pltpu.make_async_copy(own, own, self.local.at[self.row]).wait()
        for slot in range(3):
            self.make(slot).start()

    def pass_on(self, slot, *targets):
        self.make(slot).wait_recv()
        for target in targets:
            if target < self.slots:
                self.make(target).start()

    def relay(self):
        self.pass_on(0, 3, 5, 9)
        self.pass_on(1, 4, 6, 10)

    def finish(self):
        self.pass_on(3, 7, 11)
        self.pass_on(4, 8, 12)

    def across(self):
        if self.shared:
            for slot in range(9, 13):
                self.pass_on(slot, slot + 4)

    def ready(self):
        for slot in (2, 5, 6, 7, 8) + ((13, 14, 15, 16) if self.shared else ()):
            self.make(slot).wait_recv()

    def drain(self):
        for slot in range(self.slots):
            self.make(slot).wait_send()


def enter(place, shards, reps=()):
    barrier = pltpu.get_barrier_semaphore()
    for shard in shards:
        pl.semaphore_signal(barrier, inc=1, device_id=(shard, place.z), device_id_type=MESH)
    for rep in reps:
        pl.semaphore_signal(barrier, inc=1, device_id=(place.me, rep), device_id_type=MESH)
    pl.semaphore_wait(barrier, len(shards) + len(reps))


def part_of(ref, rows, lead, start, width):
    def part(shard, side, half):
        count = rows if side is None else rows // 2
        first = shard * rows if side is None else shard * rows + side * count
        left, wide = (start, width) if half is None else (start + half * (width // 2), width // 2)
        return ref.at[lead + (pl.ds(pl.multiple_of(first, count), count), pl.ds(left, wide))]

    return part


def up_fills(own, ref, index, place, shards):
    part, chunk = own.shape[0], ref.shape[2]
    lanes = chunk // shards
    slices = own.shape[1] // chunk
    rows = pl.ds(pl.multiple_of(place.me * part, part), part)
    return [
        (own.at[:, pl.ds((slices * shard + index) * lanes, lanes)], ref.at[index, rows, pl.ds(shard * lanes, lanes)])
        for shard in range(shards)
    ]


def down_fills(own, ref, index, place, shards):
    count = ref.shape[1] // shards
    rows = pl.ds(pl.multiple_of(place.me * count, count), count)
    return [(own.at[pl.ds(index * count, count), :], ref.at[index, rows, :])]


def pair_columns(pair, width):
    return [pl.ds(pl.multiple_of(plane * width + pair * PAIR, PAIR), PAIR) for plane in range(3)]


def attention_rows(joined, attended, log_rows, key_bias, pair, block, between):
    rows, width = attended.shape
    columns, key_columns, value_columns = pair_columns(pair, width)
    keys = joined[:, key_columns]
    values = joined[:, value_columns]
    bias = key_bias[...]
    biased = [key_with_bias(keys, bias, head)[0] for head in range(2)]
    for first in range(0, rows, block):
        live = first + block
        query = joined[pl.ds(first, block), columns]
        mixed = []
        sums = []
        for head in range(2):
            asked, _ = query_with_bias(query, head)
            scores = mm(asked, biased[head][:live], NT)
            row_at = lax.broadcasted_iota(jnp.int32, (block, block), 0)
            key_at = lax.broadcasted_iota(jnp.int32, (block, block), 1)
            last = jnp.where(key_at <= row_at, scores[:, first:], MASKED)
            scores = last if first == 0 else jnp.concatenate([scores[:, :first], last], axis=1)
            top = jnp.max(scores, axis=-1, keepdims=True)
            weights = jnp.exp(scores - top)
            total = jnp.sum(weights, axis=-1, keepdims=True)
            mixed.append(mm(weights.astype(BF16), values[:live]) / total)
            sums.append(top + jnp.log(total))
        lanes = lanes_of(mixed[0].shape)
        attended[pl.ds(first, block), columns] = jnp.where(lanes < HEAD_DIM, mixed[0], mixed[1]).astype(BF16)
        turned = jnp.transpose(jnp.where(lanes < HEAD_DIM, sums[0], sums[1]))
        log_rows[pl.ds(pair * 2, 1), pl.ds(first, block)] = turned[0:1]
        log_rows[pl.ds(pair * 2 + 1, 1), pl.ds(first, block)] = turned[HEAD_DIM : HEAD_DIM + 1]
        between(first // block)


def norm_rows(inputs, pass_row, gain, normed):
    @pl.loop(0, inputs.shape[0] // 256)
    def _(step):
        at = pl.ds(step * 256, 256)
        entered = inputs[at, :].astype(F32) + pass_row
        normed[at, :] = (norm_parts(entered)[0] * gain).astype(BF16)


def select_lanes(place, part, width):
    rows = lax.broadcasted_iota(jnp.int32, (part, width), 0)
    lanes = lax.broadcasted_iota(jnp.int32, (part, width), 1)
    return lanes == rows + place.me * part


SHARED = (False, True, True, False, True, True, False, True, True, False)

PLAN = {
    "begin": "r0 s2",
    "normed": "f0 r1",
    (0, 0): "s3",
    (0, 1): "f1",
    (0, 2): "r2",
    (0, 3): "s4",
    (1, 2): "a1",
    (1, 3): "r3 f2",
    (2, 0): "s5",
    (2, 1): "r4",
    (2, 3): "a2 f3",
    (3, 0): "s6",
    (3, 3): "f4 r5",
    (4, 0): "s7",
    (4, 3): "a4 f5 r6",
    (5, 0): "s8",
    (5, 3): "r7",
    "row 1": "a5 f6 s9",
    "mlp 0 0": "f7 r8",
    "mlp 0 1": "r9",
    "mlp 0 down": "a7 f8",
    "mlp 0 up": "f9",
    "mlp 1 0": "a8",
}


def fore_comm_kernel(
    block, tile, group, slices,
    length_ref, pass_ref, table_own, attn_gain_own, mlp_gain_own,
    inputs_in, cotangent_in, qkv_own, out_own, up_own, down_own,
    rows_out, log_out, gain_grad,
    up_half, down_half, normed_out, joined_out, attended_out, qkv_out, out_out, outputs_out, hidden_grad_out,
    up_done_out, down_done_out,
    inputs, cotangent, slots, small_wide, small_own, normed, joined, attended, hidden, qkv_w, out_w, up_w, down_w,
    key_bias, mixed, hidden_grad, up_done, down_done,
    up_grads, up_first, up_x, up_y, up_last, down_grads, down_first, down_x, down_y, down_last,
    sends, recvs, local, small_sends, small_recvs, up_sends, up_recvs, down_sends, down_recvs, loads, saves,
):
    place = Place()
    rows, width = inputs.shape
    shards = slots.shape[0]
    part = qkv_own.shape[0]
    groups = width // group
    pairs = width // PAIR
    per_group = group // PAIR

    pieces = []

    def add(part_at, fills):
        row = len(pieces)
        pieces.append(Gather(place, part_at, fills, sends, recvs, local, row, SHARED[row]))

    own_rows = pl.ds(pl.multiple_of(place.me * part, part), part)
    for index in range(groups):
        columns = pl.ds(index * group, group)
        fills = [
            (qkv_own.at[:, pl.ds(plane * width + index * group, group)], qkv_w.at[plane, own_rows, columns])
            for plane in range(3)
        ]
        add(part_of(qkv_w, part, (slice(None),), index * group, group), fills)
    add(part_of(out_w, part, (), 0, width), [(out_own, out_w.at[own_rows, :])])
    for index in range(slices):
        add(part_of(up_w, part, (index,), 0, up_w.shape[2]), up_fills(up_own, up_w, index, place, shards))
        add(part_of(down_w, down_w.shape[1] // shards, (index,), 0, width),
            down_fills(down_own, down_w, index, place, shards))
    count = len(pieces)
    take = [
        pltpu.make_async_copy(inputs_in, inputs, loads.at[0]), pltpu.make_async_copy(cotangent_in, cotangent, loads.at[1]),
    ]
    pieces[0].fill()
    take[0].start()
    for piece in pieces[1:]:
        piece.fill()
    take[1].start()

    chosen = select_lanes(place, part, width).astype(BF16)
    small_wide[...] = jnp.zeros_like(small_wide)
    small_wide[0 : table_own.shape[0], :] = mm(table_own[...], chosen)
    small_wide[8:9, :] = mm(attn_gain_own[...], chosen)
    small_wide[9:10, :] = mm(mlp_gain_own[...], chosen)
    small_own[...] = small_wide[...].astype(BF16)
    slots[place.me] = small_own[...]

    others = [lax.rem(place.me + shift, shards) for shift in range(1, shards)]
    enter(place, others, [place.by_z])
    smalls = [
        remote(small_own, slots.at[place.me], small_sends, small_recvs, shift, place.at(other))
        for shift, other in enumerate(others)
    ]
    pieces[0].start()
    for copy in smalls:
        copy.start()
    pieces[1].start()

    def step_on(point):
        for what in PLAN.get(point, "").split():
            piece = pieces[int(what[1:])]
            {"s": piece.start, "r": piece.relay, "f": piece.finish, "a": piece.across}[what[0]]()

    def up_message(index):
        return Scatter(
            place, up_grads.at[lax.rem(index, 2)], up_first.at[index], up_x.at[index], up_y.at[index], up_last.at[index],
            up_sends, up_recvs, index,
        )

    def down_message(index):
        return Scatter(
            place, down_grads.at[lax.rem(index, 2)], down_first.at[index], down_x.at[index], down_y.at[index], down_last.at[index],
            down_sends, down_recvs, index,
        )

    fill_bias(length_ref[0], key_bias)
    for copy in smalls:
        copy.wait_recv()
    total = slots[0].astype(F32)
    for shard in range(1, shards):
        total = total + slots[shard].astype(F32)
    places = lax.broadcasted_iota(jnp.int32, total.shape, 0)
    rows_out[0:1, :] = jnp.sum(jnp.where(places == pass_ref[0], total, 0.0), axis=0, keepdims=True)
    rows_out[1:3, :] = total[8:10]
    rows_out[3:8, :] = jnp.zeros((5, width), F32)

    take[0].wait()
    step_on("begin")
    norm_rows(inputs, rows_out[0:1, :], rows_out[1:2, :], normed)
    step_on("normed")

    keep = {}

    def save(source, target, name=None):
        keep[name or len(keep)] = copy = pltpu.make_async_copy(source, target, saves.at[len(keep)])
        return copy

    save(normed, normed_out, "normed").start()
    qkv_save = save(qkv_w, qkv_out)

    @pl.loop(0, pairs)
    def _(pair):
        for index in range(groups):
            @pl.when(pair == index * per_group)
            def _(index=index):
                pieces[index].ready()
                if index == groups - 1:
                    qkv_save.start()

        @pl.when(lax.rem(pair, per_group) == 0)
        def _():
            columns = pl.ds(pl.multiple_of(pair * PAIR, group), group)

            @pl.loop(0, 3)
            def _(plane):
                target = pl.ds(pl.multiple_of(plane * width + pair * PAIR, group), group)
                joined[:, target] = mm(normed[...], qkv_w[plane, :, columns]).astype(BF16)

        def between(place_at):
            for index in range(pairs):
                if (index, place_at) in PLAN:
                    @pl.when(pair == index)
                    def _(index=index):
                        step_on((index, place_at))

        attention_rows(joined, attended, log_out, key_bias, pair, block, between)

    chunk = up_w.shape[2]
    second = attended
    active, rising_grad = joined.at[:, pl.ds(0, chunk)], joined.at[:, pl.ds(chunk, chunk)]
    save(attended, attended_out, "attended").start()
    save(joined, joined_out, "joined").start()
    pieces[groups].ready()
    save(out_w, out_out).start()
    gain = rows_out[2:3, :]
    for step in range(rows // tile):
        at = pl.ds(step * tile, tile)
        entered = inputs[at, :].astype(F32) + rows_out[0:1, :]
        hidden[at, :] = entered + mm(attended[at, :], out_w[...])
        step_on("row %d" % step)
        if step == 0:
            keep["attended"].wait()

        @pl.loop(0, tile // 256)
        def _(step_in):
            at = pl.ds(step * tile + step_in * 256, 256)
            values = hidden[at, :]
            second[at, :] = (norm_parts(values)[0] * gain).astype(BF16)
            mixed[at, :] = values
            hidden_grad[at, :] = jnp.zeros((256, width), F32)

    take[1].wait()
    keep["joined"].wait()

    @pl.loop(0, slices)
    def _(index_at):
        for index in range(slices):
            @pl.when(index_at == index)
            def _(index=index):
                pieces[groups + 1 + 2 * index].ready()
                pieces[groups + 2 + 2 * index].ready()

        @pl.loop(0, rows // tile)
        def _(step):
            at = pl.ds(step * tile, tile)
            rising = mm(second[at, :], up_w[index_at])
            active_grad = mm(cotangent[at, :], down_w[index_at], NT)
            bent, slope = gelu_both(rising)
            shown = bent.astype(BF16)
            moved = (slope * active_grad).astype(BF16)
            active[at, :] = shown
            rising_grad[at, :] = moved
            mixed[at, :] += mm(shown, down_w[index_at])
            hidden_grad[at, :] += mm(moved, up_w[index_at], NT)

            for index in range(slices):
                for inner in range(rows // tile):
                    if "mlp %d %d" % (index, inner) in PLAN:
                        @pl.when((index_at == index) & (step == inner))
                        def _(index=index, inner=inner):
                            step_on("mlp %d %d" % (index, inner))

            @pl.when((index_at > 0) & (step == 0))
            def _():
                message = up_message(index_at - 1)
                message.merge()
                message.spread()

            @pl.when((index_at > 0) & (step == 1))
            def _():
                down_message(index_at - 1).fold()

        @pl.when(index_at > 1)
        def _():
            down_message(index_at - 2).swap_copy().wait_send()
            up_message(index_at - 2).swap_copy().wait_send()

        slot = lax.rem(index_at, 2)
        down_grads[slot] = mm(active[...], cotangent[...], TN).astype(BF16).reshape(down_grads.shape[1:])
        down_message(index_at).swap()

        @pl.when(index_at == 0)
        def _():
            step_on("mlp 0 down")

        @pl.when(index_at > 0)
        def _():
            up_message(index_at - 1).fold()

        up_grads[slot] = mm(second[...], rising_grad[...], TN).astype(BF16).reshape(up_grads.shape[1:])
        up_message(index_at).swap()

        @pl.when(index_at == 0)
        def _():
            step_on("mlp 0 up")

        @pl.when(index_at < slices - 1)
        def _():
            message = down_message(index_at)
            message.merge()
            message.spread()

        @pl.when(index_at > 0)
        def _():
            down_message(index_at - 1).close(down_done.at[index_at - 1])
            up_message(index_at - 1).close(up_done.at[index_at - 1])

    down_message(slices - 1).merge()
    save(down_first.at[slices - 1], down_half).start()
    save(up_done, up_done_out).start()
    save(down_done, down_done_out).start()
    gain_grad[...] = jnp.zeros_like(gain_grad)
    keep["normed"].wait()
    first_row = len(keep) + 2

    @pl.loop(0, rows // 256)
    def _(step):
        at = pl.ds(step * 256, 256)
        normed[at, :] = mixed[at, :].astype(BF16)
        unit, scale = norm_parts(hidden[at, :])
        grad = hidden_grad[at, :]
        hidden_grad[at, :] = cotangent[at, :].astype(F32) + norm_back(unit, scale, grad, gain)
        gain_grad[0:1, :] += jnp.sum(grad * unit, axis=0, keepdims=True)
        pltpu.make_async_copy(hidden_grad.at[at, :], hidden_grad_out.at[at, :], saves.at[first_row + step]).start()

    save(normed, outputs_out).start()
    up_message(slices - 1).merge()
    save(up_first.at[slices - 1], up_half).start()
    for step in range(rows // 256):
        at = pl.ds(step * 256, 256)
        pltpu.make_async_copy(hidden_grad.at[at, :], hidden_grad_out.at[at, :], saves.at[first_row + step]).wait()
    for piece in pieces:
        piece.drain()
    for copy in smalls:
        copy.wait_send()
    for index in range(slices):
        up_message(index).drain(index >= slices - 2, index < slices - 1)
        down_message(index).drain(index >= slices - 2, index < slices - 1)
    for name, copy in keep.items():
        if name not in ("normed", "attended", "joined"):
            copy.wait()


def any_spec(count):
    return [pl.BlockSpec(memory_space=pl.ANY)] * count


def smem_spec(count):
    return [pl.BlockSpec(memory_space=pltpu.SMEM)] * count


def vmem_spec(count):
    return [pl.BlockSpec(memory_space=pltpu.VMEM)] * count


def shaped(shape, kind):
    return jax.ShapeDtypeStruct(shape, kind)


class Scatter:
    def __init__(self, place, grads, first, by_x, by_y, last, sends, recvs, row):
        self.place, self.grads, self.first = place, grads, first
        self.in_x, self.in_y, self.last = by_x, by_y, last
        self.sends, self.recvs, self.row = sends, recvs, row
        half = first.shape[-1] // 2
        self.left, self.right = pl.ds(0, half), pl.ds(half, half)

    def copy(self, slot, src, dst, shard):
        return remote(src, dst, self.sends, self.recvs, (self.row, slot), self.place.at(shard))

    def swap_copy(self):
        p = self.place
        return self.copy(0, self.grads.at[:, :, 1 - p.core], self.first, p.by_core)

    def spread_copies(self):
        p = self.place
        return [
            self.copy(1, self.first.at[:, 1 - p.x, :, self.left], self.in_x, p.by_x),
            self.copy(2, self.first.at[1 - p.y, :, :, self.right], self.in_y, p.by_y),
        ]

    def fold_copies(self):
        p = self.place
        return [
            self.copy(3, self.in_x.at[1 - p.y], self.last.at[:, self.left], p.by_y),
            self.copy(4, self.in_y.at[1 - p.x], self.last.at[:, self.right], p.by_x),
        ]

    def swap(self):
        self.swap_copy().start()

    def merge(self, target=None):
        p = self.place
        target = self.first if target is None else target
        self.swap_copy().wait_recv()
        for y in range(2):
            for x in range(2):
                total = self.grads[y, x, p.core].astype(F32) + self.first[y, x].astype(F32)
                target[y, x] = total.astype(BF16)

    def spread(self):
        for copy in self.spread_copies():
            copy.start()

    def fold(self):
        p = self.place
        for copy in self.spread_copies():
            copy.wait_recv()
        for other in range(2):
            total = self.first[other, p.x, :, self.left].astype(F32) + self.in_x[other].astype(F32)
            self.in_x[other] = total.astype(BF16)
            total = self.first[p.y, other, :, self.right].astype(F32) + self.in_y[other].astype(F32)
            self.in_y[other] = total.astype(BF16)
        for copy in self.fold_copies():
            copy.start()

    def close(self, target):
        p = self.place
        for copy in self.fold_copies():
            copy.wait_recv()
        target[:, self.left] = (self.last[:, self.left].astype(F32) + self.in_x[p.y].astype(F32)).astype(BF16)
        target[:, self.right] = (self.last[:, self.right].astype(F32) + self.in_y[p.x].astype(F32)).astype(BF16)

    def drain(self, swapped=True, spread=True):
        if swapped:
            self.swap_copy().wait_send()
        if spread:
            for copy in self.spread_copies() + self.fold_copies():
                copy.wait_send()


def scatter_scratch(count, part, columns, slots=None):
    return [
        pltpu.VMEM((slots or count, 2, 2, 2, part, columns), BF16), pltpu.VMEM((count, 2, 2, part, columns), BF16),
        pltpu.VMEM((count, 2, part, columns // 2), BF16), pltpu.VMEM((count, 2, part, columns // 2), BF16),
        pltpu.VMEM((count, part, columns), BF16),
    ]


def dma(*shapes):
    return [pltpu.SemaphoreType.DMA(shape) for shape in shapes]


def fore_comm(slices, seq_lens, pass_idx, table, attn_gain, mlp_gain, inputs, cotangent, qkv, out, up, down):
    rows, width = inputs.shape
    up_part, chunk = up.shape[0], up.shape[1] // slices
    down_part = down.shape[0] // slices
    shards = width // up_part
    group = 4 * HEAD_DIM
    groups = width // group
    count = groups + 1 + 2 * slices
    vm = lambda *shape: pltpu.VMEM(shape, BF16)
    vf = lambda *shape: pltpu.VMEM(shape, F32)
    return pl.pallas_call(
        functools.partial(fore_comm_kernel, 256, 512, group, slices),
        out_shape=[
            shaped((8, width), F32), shaped((16, rows), F32), shaped((8, width), F32),
            shaped((2, 2, up_part, chunk), BF16), shaped((2, 2, down_part, width), BF16),
            shaped((rows, width), BF16), shaped((rows, 3 * width), BF16), shaped((rows, width), BF16),
            shaped((3, width, width), BF16), shaped((width, width), BF16), shaped((rows, width), BF16),
            shaped((rows, width), F32), shaped((slices - 1, up_part, chunk), BF16),
            shaped((slices - 1, down_part, width), BF16),
        ],
        in_specs=smem_spec(2) + vmem_spec(3) + any_spec(6),
        out_specs=vmem_spec(3) + any_spec(11),
        scratch_shapes=[
            vm(rows, width), vm(rows, width), vm(shards, 16, width), vf(16, width), vm(16, width), vm(rows, width),
            vm(rows, 3 * width), vm(rows, width), vf(rows, width), vm(3, width, width), vm(width, width),
            vm(slices, width, chunk), vm(slices, chunk, width), vm(rows, PAIR), vf(rows, width), vf(rows, width),
            vm(slices - 1, up_part, chunk), vm(slices - 1, down_part, width),
        ]
        + scatter_scratch(slices, up_part, chunk, 2)
        + scatter_scratch(slices, down_part, width, 2)
        + dma((count, 17), (count, 17), (count,), (shards,), (shards,), (slices, 5), (slices, 5), (slices, 5),
              (slices, 5), (2,), (10 + rows // 256,)),
        compiler_params=pltpu.CompilerParams(
            vmem_limit_bytes=VMEM_LIMIT, collective_id=1, has_side_effects=True
        ),
    )(seq_lens, pass_idx, table, attn_gain, mlp_gain, inputs, cotangent, qkv, out, up, down)


class Column:
    def __init__(self, place, block, inward, middle, outward, total, sends, recvs, row):
        self.place, self.block, self.inward, self.middle = place, block, inward, middle
        self.outward, self.total = outward, total
        self.sends, self.recvs, self.row = sends, recvs, row
        self.end = (place.z == 0) | (place.z == 3)

    def copy(self, slot, src, dst, rep):
        return remote(src, dst, self.sends, self.recvs, (self.row, slot), (self.place.me, rep))

    def in_copy(self):
        return self.copy(0, self.block, self.inward, 1 + self.place.z // 3)

    def across_copy(self):
        return self.copy(1, self.middle, self.outward, 3 - self.place.z)

    def out_copy(self):
        return self.copy(2, self.total, self.outward, 3 * (self.place.z - 1))

    def begin(self):
        @pl.when(self.end)
        def _():
            self.in_copy().start()

    def cross(self):
        @pl.when(jnp.logical_not(self.end))
        def _():
            self.in_copy().wait_recv()
            self.middle[...] = (self.block[...].astype(F32) + self.inward[...].astype(F32)).astype(BF16)
            self.across_copy().start()

    def settle(self):
        @pl.when(jnp.logical_not(self.end))
        def _():
            self.across_copy().wait_recv()
            self.total[...] = (self.middle[...].astype(F32) + self.outward[...].astype(F32)).astype(BF16)
            self.out_copy().start()

    def finish(self):
        @pl.when(self.end)
        def _():
            self.out_copy().wait_recv()
            self.total[...] = self.outward[...]
            self.in_copy().wait_send()

        @pl.when(jnp.logical_not(self.end))
        def _():
            self.across_copy().wait_send()
            self.out_copy().wait_send()


def attention_columns(joined, log_rows, grads, joined_grad, key_bias, key_total, value_total, pair, block):
    rows, width = grads.shape
    columns, key_columns, value_columns = pair_columns(pair, width)
    keys = joined[:, key_columns]
    values = joined[:, value_columns]
    bias = key_bias[...]
    biased = [key_with_bias(keys, bias, head) for head in range(2)]
    key_total[...] = jnp.zeros_like(key_total)
    value_total[...] = jnp.zeros_like(value_total)
    for first in range(0, rows, block):
        live = first + block
        query = joined[pl.ds(first, block), columns]
        grad = grads[pl.ds(first, block), columns]
        query_grad = None
        for head in range(2):
            asked, asked_only = query_with_bias(query, head)
            grad_only = head_only(grad, head)[0]
            scores = mm(biased[head][0][:live], asked, NT)
            share_grad = mm(values[:live], grad_only, NT)
            log_sum = log_rows[pl.ds(pair * 2 + head, 1), pl.ds(first, block)]
            shares = jnp.exp(scores - log_sum)
            key_at = lax.broadcasted_iota(jnp.int32, (block, block), 0)
            row_at = lax.broadcasted_iota(jnp.int32, (block, block), 1)
            last = jnp.where(key_at <= row_at, shares[first:], 0.0)
            shares = last if first == 0 else jnp.concatenate([shares[:first], last], axis=0)
            inner = jnp.sum(share_grad * shares, axis=0, keepdims=True)
            score_grad = (shares * (share_grad - inner)).astype(BF16)
            value_total[:live, :] += mm(shares.astype(BF16), grad_only)
            key_total[:live, :] += mm(score_grad, asked_only)
            part = mm(score_grad, biased[head][1][:live], TN)
            query_grad = part if query_grad is None else query_grad + part
        joined_grad[0, pl.ds(first, block), columns] = (query_grad * HEAD_DIM**-0.5).astype(BF16)
    joined_grad[1, :, columns] = key_total[...].astype(BF16)
    joined_grad[2, :, columns] = value_total[...].astype(BF16)


def back_comm_kernel(
    block, tile, group,
    length_ref, pass_ref, rows_in, log_rows, mlp_gain_grad, up_done, down_done, up_half, down_half,
    hidden_grad_in, out_in, attended_in, normed_in, joined_in, qkv_in, inputs_in,
    grad_input_out, small_sum, up_total, down_total, attn_total,
    hidden_grad, out_w, attended, inputs, grad_input,
    qkv_w, joined, branch_grad, attended_grad, normed, joined_grad, key_bias, key_total, value_total,
    grads, first, in_x, in_y, last, block_sum,
    up_x, up_y, up_last, up_block, down_x, down_y, down_last, down_block,
    up_in, up_mid, up_out, down_in, down_mid, down_out, attn_in, attn_mid, attn_out,
    small_own, small_slots, small_plane, small_reps,
    sends, recvs, up_sends, up_recvs, down_sends, down_recvs, z_sends, z_recvs,
    plane_sends, plane_recvs, rep_sends, rep_recvs, loads, saves,
):
    place = Place()
    rows, width = inputs.shape
    shards = small_slots.shape[0]
    reps = small_reps.shape[0]
    chunks = up_total.shape[0]
    groups = width // group
    pairs = width // PAIR
    per_group = group // PAIR
    others = [lax.rem(place.me + shift, shards) for shift in range(1, shards)]
    others_z = [lax.rem(place.z + shift, reps) for shift in range(1, reps)]
    take = [
        pltpu.make_async_copy(source, target, loads.at[index])
        for index, (source, target) in enumerate((
            (hidden_grad_in, hidden_grad), (out_in, out_w), (attended_in, attended), (joined_in, joined),
            (normed_in, normed), (qkv_in, qkv_w), (inputs_in, inputs),
        ))
    ]
    for copy in take:
        copy.start()
    enter(place, others, others_z)

    up_late = Scatter(place, None, up_half, up_x, up_y, up_last, up_sends, up_recvs, 0)
    down_late = Scatter(place, None, down_half, down_x, down_y, down_last, down_sends, down_recvs, 0)

    def message(index):
        return Scatter(
            place, grads.at[index], first.at[index], in_x.at[index], in_y.at[index], last.at[index],
            sends, recvs, index,
        )

    out_msg = message(0)
    qkv_msg = [message(1 + index) for index in range(groups)]

    lines = {}

    def line(key, source, inward, middle, outward, total):
        lines[key] = Column(place, source, inward, middle, outward, total, z_sends, z_recvs, len(lines))

    for index in range(chunks):
        final = index == chunks - 1
        line(("d", index), down_block if final else down_done.at[index],
             down_in.at[index], down_mid.at[index], down_out.at[index], down_total.at[index])
        line(("u", index), up_block if final else up_done.at[index],
             up_in.at[index], up_mid.at[index], up_out.at[index], up_total.at[index])
    for index in range(1 + groups):
        line(("a", index), block_sum.at[index], attn_in.at[index], attn_mid.at[index], attn_out.at[index],
             attn_total.at[index])

    down_late.spread()
    up_late.spread()
    for index in range(chunks - 1):
        lines["d", index].begin()
        lines["u", index].begin()

    fill_bias(length_ref[0], key_bias)
    take[0].wait()
    take[1].wait()

    @pl.loop(0, rows // tile)
    def _(step):
        at = pl.ds(step * tile, tile)
        shown = hidden_grad[at, :].astype(BF16)
        branch_grad[at, :] = shown
        attended_grad[at, :] = mm(shown, out_w[...], NT).astype(BF16)

    lines["d", 0].cross()
    take[2].wait()
    grads[0] = mm(attended[...], branch_grad[...], TN).astype(BF16).reshape(grads.shape[1:])
    out_msg.swap()
    down_late.fold()
    for copy in take[3:]:
        copy.wait()

    def late_close(message, target, key):
        message.close(target)
        lines[key].begin()

    def close(index):
        message(index).close(block_sum.at[index])
        lines["a", index].begin()

    def send(index):
        message(index).merge()
        message(index).spread()

    after_pair = [
        lambda: (lines["u", 0].cross(), up_late.fold(), send(0), lines["d", 0].settle()),
        lambda: (lines["d", 1].cross(), lines["u", 1].cross(), late_close(down_late, down_block, ("d", 2)),
                 late_close(up_late, up_block, ("u", 2)), lines["u", 0].settle(), out_msg.fold()),
        lambda: (send(1),),
        lambda: (lines["d", 1].settle(), lines["u", 1].settle(), lines["d", 2].cross(), lines["u", 2].cross(),
                 close(0), qkv_msg[0].fold()),
        lambda: (send(2), close(1)),
        lambda: (lines["a", 0].cross(), lines["d", 2].settle(), lines["u", 2].settle(), lines["a", 1].cross(),
                 qkv_msg[1].fold()),
    ]

    @pl.loop(0, pairs)
    def _(pair):
        attention_columns(
            joined, log_rows, attended_grad, joined_grad, key_bias, key_total, value_total, pair, block
        )

        @pl.when(lax.rem(pair, per_group) == per_group - 1)
        def _():
            index = pair // per_group
            columns = pl.ds(pl.multiple_of(index * group, group), group)
            for plane in range(3):
                part = mm(normed[...], joined_grad[plane, :, columns], TN).astype(BF16)
                grads[1 + index, :, :, :, :, pl.ds(plane * group, group)] = part.reshape(
                    grads.shape[1:5] + (group,)
                )
            message(1 + index).swap()

        for index in range(pairs):
            @pl.when(pair == index)
            def _(index=index):
                after_pair[index]()

    small_own[...] = jnp.zeros_like(small_own)

    def after_rows(step):
        @pl.when(step == 0)
        def _():
            send(3)
            close(2)

        @pl.when(step == 1)
        def _():
            lines["a", 0].settle()

        @pl.when(step == 3)
        def _():
            qkv_msg[2].fold()
            lines["a", 1].settle()
            lines["a", 2].cross()

    @pl.loop(0, rows // 256)
    def _(step):
        at = pl.ds(step * 256, 256)
        grad = mm(joined_grad[0, at, :], qkv_w[0], NT)
        grad = grad + mm(joined_grad[1, at, :], qkv_w[1], NT)
        grad = grad + mm(joined_grad[2, at, :], qkv_w[2], NT)
        unit, scale = norm_parts(inputs[at, :].astype(F32) + rows_in[0:1, :])
        total = hidden_grad[at, :] + norm_back(unit, scale, grad, rows_in[1:2, :])
        grad_input[at, :] = total
        small_own[5:6, :] += jnp.sum(grad * unit, axis=0, keepdims=True)
        small_own[0:1, :] += jnp.sum(total, axis=0, keepdims=True)
        pltpu.make_async_copy(grad_input.at[at, :], grad_input_out.at[at, :], saves.at[step]).start()
        after_rows(step)

    places = lax.broadcasted_iota(jnp.int32, small_own.shape, 0)
    own = small_own[...]
    table = jnp.where((places == pass_ref[0]) & (places < 5), own[0:1], 0.0)
    own = jnp.where(places == 5, own, table)
    small_own[...] = jnp.where(places == 6, mlp_gain_grad[0:1], own)
    small_slots[place.me] = small_own[...]
    plane_copies = [
        remote(small_own, small_slots.at[place.me], plane_sends, plane_recvs, shift, place.at(other))
        for shift, other in enumerate(others)
    ]
    for copy in plane_copies:
        copy.start()
    close(3)
    lines["a", 2].settle()
    for copy in plane_copies:
        copy.wait_recv()
    total = small_slots[0]
    for shard in range(1, shards):
        total = total + small_slots[shard]
    small_plane[...] = total
    small_reps[place.z] = total
    rep_copies = [
        remote(small_plane, small_reps.at[place.z], rep_sends, rep_recvs, shift, (place.me, other))
        for shift, other in enumerate(others_z)
    ]
    for copy in rep_copies:
        copy.start()
    lines["a", 3].cross()
    for copy in rep_copies:
        copy.wait_recv()
    total = small_reps[0]
    for rep in range(1, reps):
        total = total + small_reps[rep]
    small_sum[...] = total
    lines["a", 3].settle()
    for key in lines:
        lines[key].finish()
    for index in range(1 + groups):
        message(index).drain()
    up_late.drain(swapped=False)
    down_late.drain(swapped=False)
    for copy in plane_copies + rep_copies:
        copy.wait_send()
    for step in range(rows // 256):
        at = pl.ds(step * 256, 256)
        pltpu.make_async_copy(grad_input.at[at, :], grad_input_out.at[at, :], saves.at[step]).wait()


def back_comm(reps, seq_lens, pass_idx, rows_in, log_rows, mlp_gain_grad, up_done, down_done, up_half, down_half,
              hidden_grad, out_w, attended, normed, joined, qkv_w, inputs):
    rows, width = inputs.shape
    _, _, up_part, chunk = up_half.shape
    down_part = down_half.shape[2]
    chunks = up_done.shape[0] + 1
    shards = width // up_part
    group = 4 * HEAD_DIM
    count = 1 + width // group
    wide = 3 * group
    vm = lambda *shape: pltpu.VMEM(shape, BF16)
    vf = lambda *shape: pltpu.VMEM(shape, F32)
    return pl.pallas_call(
        functools.partial(back_comm_kernel, 256, 512, group),
        out_shape=[
            shaped((rows, width), F32), shaped((8, width), F32), shaped((chunks, up_part, chunk), BF16),
            shaped((chunks, down_part, width), BF16), shaped((count, up_part, wide), BF16),
        ],
        in_specs=smem_spec(2) + vmem_spec(7) + any_spec(7),
        out_specs=any_spec(1) + vmem_spec(4),
        scratch_shapes=[
            vf(rows, width), vm(width, width), vm(rows, width), vm(rows, width), vf(rows, width),
            vm(3, width, width), vm(rows, 3 * width), vm(rows, width), vm(rows, width), vm(rows, width),
            vm(3, rows, width), vm(rows, PAIR), vf(rows, PAIR), vf(rows, PAIR),
        ]
        + scatter_scratch(count, up_part, wide)
        + [
            vm(count, up_part, wide),
            vm(2, up_part, chunk // 2), vm(2, up_part, chunk // 2), vm(up_part, chunk), vm(up_part, chunk),
            vm(2, down_part, width // 2), vm(2, down_part, width // 2), vm(down_part, width), vm(down_part, width),
        ]
        + [vm(chunks, up_part, chunk)] * 3
        + [vm(chunks, down_part, width)] * 3
        + [vm(count, up_part, wide)] * 3
        + [vf(8, width), vf(shards, 8, width), vf(8, width), vf(reps, 8, width)]
        + dma((count, 5), (count, 5), (1, 5), (1, 5), (1, 5), (1, 5), (2 * chunks + count, 3), (2 * chunks + count, 3),
              (shards - 1,), (shards - 1,), (reps - 1,), (reps - 1,), (7,), (rows // 256,)),
        compiler_params=pltpu.CompilerParams(
            vmem_limit_bytes=VMEM_LIMIT, collective_id=3, has_side_effects=True
        ),
    )(seq_lens, pass_idx, rows_in, log_rows, mlp_gain_grad, up_done, down_done, up_half, down_half,
      hidden_grad, out_w, attended, normed, joined, qkv_w, inputs)


def place_kernel(
    small_sum, outputs_in, grad_input_in, up_in, down_in, attn_in,
    table_out, attn_gain_out, mlp_gain_out, outputs_out, grad_input_out, qkv_out, out_out, up_out, down_out,
    outputs, grad_input, up_total, down_total, attn_total, qkv, out, up, down, loads, saves,
):
    slices, part, chunk = up_in.shape
    width = small_sum.shape[1]
    shards = width // part
    lanes = chunk // shards
    groups = attn_in.shape[0] - 1
    group = attn_in.shape[2] // 3
    take = [
        pltpu.make_async_copy(source, target, loads.at[index])
        for index, (source, target) in enumerate((
            (grad_input_in, grad_input), (up_in, up_total), (attn_in, attn_total), (down_in, down_total),
            (outputs_in, outputs),
        ))
    ]
    give = [
        pltpu.make_async_copy(source, target, saves.at[index])
        for index, (source, target) in enumerate((
            (grad_input, grad_input_out), (up, up_out), (qkv, qkv_out), (out, out_out), (down, down_out),
            (outputs, outputs_out),
        ))
    ]
    for copy in take:
        copy.start()
    first = lax.axis_index("shard") * part
    rows_at = lax.broadcasted_iota(jnp.int32, (width, part), 0)
    lanes_at = lax.broadcasted_iota(jnp.int32, (width, part), 1)
    chosen = (rows_at == lanes_at + first).astype(F32)
    own = lax.dot_general(small_sum[...], chosen, NN, precision=lax.Precision.HIGHEST, preferred_element_type=F32)
    table_out[...] = own[0 : table_out.shape[0]]
    attn_gain_out[...] = own[5:6]
    mlp_gain_out[...] = own[6:7]
    take[0].wait()
    give[0].start()
    take[1].wait()
    for index in range(slices):
        for shard in range(shards):
            up[:, (slices * shard + index) * lanes : (slices * shard + index + 1) * lanes] = up_total[
                index, :, shard * lanes : (shard + 1) * lanes
            ].astype(F32)
    give[1].start()
    take[2].wait()
    for index in range(groups):
        for plane in range(3):
            start = plane * width + index * group
            qkv[:, start : start + group] = attn_total[1 + index, :, plane * group : (plane + 1) * group].astype(F32)
    out[...] = attn_total[0].astype(F32)
    give[2].start()
    give[3].start()
    take[3].wait()
    count = down_total.shape[1]
    for index in range(slices):
        down[index * count : (index + 1) * count, :] = down_total[index].astype(F32)
    give[4].start()
    take[4].wait()
    give[5].start()
    for copy in give:
        copy.wait()


def finish_places(passes, small_sum, outputs, grad_input, up_total, down_total, attn_total):
    rows, width = outputs.shape
    slices, part, chunk = up_total.shape
    down_rows = slices * down_total.shape[1]
    vf = lambda *shape: pltpu.VMEM(shape, F32)
    like = lambda ref: pltpu.VMEM(ref.shape, ref.dtype)
    return pl.pallas_call(
        place_kernel,
        out_shape=[
            shaped((passes, part), F32), shaped((1, part), F32), shaped((1, part), F32), shaped((rows, width), BF16),
            shaped((rows, width), F32), shaped((part, 3 * width), F32), shaped((part, width), F32),
            shaped((part, slices * chunk), F32), shaped((down_rows, width), F32),
        ],
        in_specs=vmem_spec(1) + any_spec(5),
        out_specs=vmem_spec(3) + any_spec(6),
        scratch_shapes=[
            like(outputs), like(grad_input), like(up_total), like(down_total), like(attn_total),
            vf(part, 3 * width), vf(part, width), vf(part, slices * chunk), vf(down_rows, width),
        ]
        + dma((5,), (6,)),
        compiler_params=pltpu.CompilerParams(vmem_limit_bytes=VMEM_LIMIT),
    )(small_sum, outputs, grad_input, up_total, down_total, attn_total)


def direct(reps, inputs, seq_lens, pass_idx, pass_table, gain_attn, w_qkv, w_out, gain_mlp, w_up, w_down, cotangent):
    slices = 3
    (
        rows_in, log_rows, mlp_gain_grad, up_half, down_half,
        normed, joined, attended, qkv_w, out_w, outputs, hidden_grad, up_done, down_done,
    ) = fore_comm(
        slices, seq_lens, pass_idx, pass_table, gain_attn[None], gain_mlp[None], inputs[0], cotangent[0], w_qkv, w_out,
        w_up, w_down,
    )
    grad_input, small_sum, up_total, down_total, attn_total = back_comm(
        reps, seq_lens, pass_idx, rows_in, log_rows, mlp_gain_grad, up_done, down_done, up_half, down_half,
        hidden_grad, out_w, attended, normed, joined, qkv_w, inputs[0],
    )
    table, attn_gain, mlp_gain, outputs, grad_input, qkv, out, up, down = finish_places(
        pass_table.shape[0], small_sum, outputs, grad_input, up_total, down_total, attn_total
    )
    return (outputs[None], grad_input[None], table, attn_gain[0], qkv, out, mlp_gain[0], up, down)


def solution(mesh):
    shards, reps = mesh.shape["shard"], mesh.shape["rep"]
    run = functools.partial(direct, reps) if (shards, reps) == (8, 4) else body
    part = P(("shard", "rep"), None, None)
    return jax.shard_map(
        run,
        mesh=mesh,
        in_specs=(
            part, P(("shard", "rep")), P(("shard", "rep")), P(None, "shard"), P("shard"), P("shard", None),
            P("shard", None), P("shard"), P("shard", None), P("shard", None), part,
        ),
        out_specs=(
            part, part, P(None, "shard"), P("shard"), P("shard", None), P("shard", None), P("shard"),
            P("shard", None), P("shard", None),
        ),
        check_vma=False,
    )
```

```python
import functools
import math

import jax
import jax.numpy as jnp
from jax import lax
from jax.experimental import pallas as pl
from jax.experimental.pallas import tpu as pltpu
from jax.sharding import PartitionSpec as P

HEADS = 12
HEAD_DIM = 64
PAIR = 2 * HEAD_DIM
EPSILON = 1e-05
MASKED = -1e30
BF16 = jnp.bfloat16
F32 = jnp.float32
VMEM_LIMIT = 64 * 1024 * 1024 - 65536

NN = (((1,), (0,)), ((), ()))
NT = (((1,), (1,)), ((), ()))
TN = (((0,), (0,)), ((), ()))


def mm(a, b, dims=NN):
    return lax.dot_general(a, b, dims, preferred_element_type=F32)


def norm_parts(values):
    average = jnp.mean(values, axis=-1, keepdims=True)
    centred = values - average
    variance = jnp.mean(centred * centred, axis=-1, keepdims=True)
    scale = lax.rsqrt(variance + EPSILON)
    return centred * scale, scale


def norm_back(unit, scale, grad, gain):
    scaled = grad * gain
    part = scaled - jnp.mean(scaled, axis=-1, keepdims=True)
    return scale * (part - unit * jnp.mean(scaled * unit, axis=-1, keepdims=True))


def lanes_of(shape):
    return lax.broadcasted_iota(jnp.int32, shape, len(shape) - 1)


def head_only(values, head, zero_at=None):
    lanes = lanes_of(values.shape)
    own = (lanes < HEAD_DIM) if head == 0 else (lanes >= HEAD_DIM)
    return jnp.where(own, values, jnp.zeros_like(values)), own, lanes


def query_with_bias(query, head):
    kept, own, lanes = head_only(query * BF16(HEAD_DIM**-0.5), head)
    spot = HEAD_DIM if head == 0 else 0
    return jnp.where(lanes == spot, jnp.ones_like(kept), kept), kept


def key_with_bias(keys, bias, head):
    kept, own, lanes = head_only(keys, head)
    spot = HEAD_DIM if head == 0 else 0
    return jnp.where(lanes == spot, bias, kept), kept


def attention_front(length, joined, attended, log_sums, key_bias, pair, block):
    rows = attended.shape[0]
    width = attended.shape[1]
    at = pl.multiple_of(pair * PAIR, PAIR)
    keys = joined[:, pl.ds(width + at, PAIR)]
    values = joined[:, pl.ds(2 * width + at, PAIR)]
    bias = key_bias[...]
    biased = [key_with_bias(keys, bias, head)[0] for head in range(2)]
    for first in range(0, rows, block):
        live = first + block
        query = joined[pl.ds(first, block), pl.ds(at, PAIR)]
        mixed = []
        sums = []
        for head in range(2):
            asked, _ = query_with_bias(query, head)
            scores = mm(asked, biased[head][:live], NT)
            row_at = lax.broadcasted_iota(jnp.int32, (block, block), 0)
            key_at = lax.broadcasted_iota(jnp.int32, (block, block), 1)
            last = jnp.where(key_at <= row_at, scores[:, first:], MASKED)
            scores = last if first == 0 else jnp.concatenate([scores[:, :first], last], axis=1)
            top = jnp.max(scores, axis=-1, keepdims=True)
            weights = jnp.exp(scores - top)
            total = jnp.sum(weights, axis=-1, keepdims=True)
            mixed.append(mm(weights.astype(BF16), values[:live]) / total)
            sums.append(top + jnp.log(total))
        lanes = lanes_of(mixed[0].shape)
        attended[pl.ds(first, block), pl.ds(at, PAIR)] = jnp.where(
            lanes < HEAD_DIM, mixed[0], mixed[1]
        ).astype(BF16)
        log_sums[pair, pl.ds(first, block), :] = jnp.where(lanes < HEAD_DIM, sums[0], sums[1])


def fill_bias(length, key_bias):
    rows = key_bias.shape[0]
    places = lax.broadcasted_iota(jnp.int32, key_bias.shape, 0)
    key_bias[...] = jnp.where(places < length, 0.0, MASKED).astype(BF16)


def front_kernel(
    block, tile, length_ref, inputs, pass_row, gain, w_qkv, w_out,
    joined_out, attended_out, sums_out, hidden_out, normed, key_bias,
):
    rows, width = inputs.shape
    length = length_ref[0]
    fill_bias(length, key_bias)

    @pl.loop(0, rows // 256)
    def _(step):
        at = pl.ds(step * 256, 256)
        entered = inputs[at, :].astype(F32) + pass_row[0:1, :]
        normed[at, :] = (norm_parts(entered)[0] * gain[0:1, :]).astype(BF16)

    @pl.loop(0, 3)
    def _(part):
        columns = pl.ds(pl.multiple_of(part * width, width), width)

        @pl.loop(0, rows // tile)
        def _(step):
            at = pl.ds(step * tile, tile)
            joined_out[at, columns] = mm(normed[at, :], w_qkv[:, columns]).astype(BF16)

    @pl.loop(0, HEADS // 2)
    def _(pair):
        attention_front(length, joined_out, attended_out, sums_out, key_bias, pair, block)

    @pl.loop(0, rows // tile)
    def _(step):
        at = pl.ds(step * tile, tile)
        entered = inputs[at, :].astype(F32) + pass_row[0:1, :]
        hidden_out[at, :] = entered + mm(attended_out[at, :], w_out[...])


def gelu_both(values):
    outer = math.sqrt(2.0 / math.pi)
    square = values * values
    bent = jnp.tanh(outer * values * (1.0 + 0.044715 * square))
    half = 0.5 * (1.0 + bent)
    slope = half + 0.5 * values * (1.0 - bent * bent) * (outer * (1.0 + 3 * 0.044715 * square))
    return values * half, slope


def mlp_kernel(
    tile, chunk, hidden, cotangent, gain, w_up, w_down,
    outputs, hidden_grad, gain_grad, up_grad, down_grad,
    second, mixed, second_grad, active, rising_grad,
):
    rows, width = hidden.shape
    chunks = w_down.shape[0] // chunk

    @pl.loop(0, rows // 256)
    def _(step):
        at = pl.ds(step * 256, 256)
        second[at, :] = (norm_parts(hidden[at, :])[0] * gain[0:1, :]).astype(BF16)
        mixed[at, :] = hidden[at, :]
        second_grad[at, :] = jnp.zeros((256, width), F32)

    @pl.loop(0, chunks)
    def _(part):
        units = pl.ds(pl.multiple_of(part * chunk, chunk), chunk)

        @pl.loop(0, rows // tile)
        def _(step):
            at = pl.ds(step * tile, tile)
            rising = mm(second[at, :], w_up[:, units])
            active_grad = mm(cotangent[at, :], w_down[units, :], NT)
            bent, slope = gelu_both(rising)
            shown = bent.astype(BF16)
            moved = (slope * active_grad).astype(BF16)
            active[at, :] = shown
            rising_grad[at, :] = moved
            mixed[at, :] += mm(shown, w_down[units, :])
            second_grad[at, :] += mm(moved, w_up[:, units], NT)

        down_grad[units, :] = mm(active[...], cotangent[...], TN).astype(BF16)
        up_grad[:, units] = mm(second[...], rising_grad[...], TN).astype(BF16)

    gain_grad[...] = jnp.zeros_like(gain_grad)

    @pl.loop(0, rows // 256)
    def _(step):
        at = pl.ds(step * 256, 256)
        outputs[at, :] = mixed[at, :].astype(BF16)
        unit, scale = norm_parts(hidden[at, :])
        grad = second_grad[at, :]
        hidden_grad[at, :] = cotangent[at, :].astype(F32) + norm_back(unit, scale, grad, gain[0:1, :])
        gain_grad[0:1, :] += jnp.sum(grad * unit, axis=0, keepdims=True)


def attention_back(joined, log_rows, grads, joined_grad, key_bias, key_total, value_total, pair, block):
    rows = grads.shape[0]
    width = grads.shape[1]
    at = pl.multiple_of(pair * PAIR, PAIR)
    keys = joined[:, pl.ds(width + at, PAIR)]
    values = joined[:, pl.ds(2 * width + at, PAIR)]
    bias = key_bias[...]
    biased = [key_with_bias(keys, bias, head) for head in range(2)]
    key_total[...] = jnp.zeros_like(key_total)
    value_total[...] = jnp.zeros_like(value_total)
    for first in range(0, rows, block):
        live = first + block
        query = joined[pl.ds(first, block), pl.ds(at, PAIR)]
        grad = grads[pl.ds(first, block), pl.ds(at, PAIR)]
        query_grad = None
        for head in range(2):
            asked, asked_only = query_with_bias(query, head)
            grad_only = head_only(grad, head)[0]
            scores = mm(biased[head][0][:live], asked, NT)
            share_grad = mm(values[:live], grad_only, NT)
            log_sum = log_rows[pl.ds(pair * 2 + head, 1), pl.ds(first, block)]
            shares = jnp.exp(scores - log_sum)
            key_at = lax.broadcasted_iota(jnp.int32, (block, block), 0)
            row_at = lax.broadcasted_iota(jnp.int32, (block, block), 1)
            last = jnp.where(key_at <= row_at, shares[first:], 0.0)
            shares = last if first == 0 else jnp.concatenate([shares[:first], last], axis=0)
            inner = jnp.sum(share_grad * shares, axis=0, keepdims=True)
            score_grad = (shares * (share_grad - inner)).astype(BF16)
            value_total[:live, :] += mm(shares.astype(BF16), grad_only)
            key_total[:live, :] += mm(score_grad, asked_only)
            part = mm(score_grad, biased[head][1][:live], TN)
            query_grad = part if query_grad is None else query_grad + part
        joined_grad[pl.ds(first, block), pl.ds(at, PAIR)] = (
            query_grad * HEAD_DIM**-0.5
        ).astype(BF16)
    joined_grad[:, pl.ds(width + at, PAIR)] = key_total[...].astype(BF16)
    joined_grad[:, pl.ds(2 * width + at, PAIR)] = value_total[...].astype(BF16)


def back_kernel(
    block, tile, length_ref, inputs, pass_row, gain, w_qkv, w_out, joined, log_rows, attended, hidden_grad,
    grad_input, gain_grad, table_grad, qkv_grad, out_grad,
    branch_grad, attended_grad, normed, joined_grad, key_bias, key_total, value_total,
):
    rows, width = inputs.shape
    length = length_ref[0]
    fill_bias(length, key_bias)

    @pl.loop(0, rows // 256)
    def _(step):
        at = pl.ds(step * 256, 256)
        branch_grad[at, :] = hidden_grad[at, :].astype(BF16)
        entered = inputs[at, :].astype(F32) + pass_row[0:1, :]
        normed[at, :] = (norm_parts(entered)[0] * gain[0:1, :]).astype(BF16)

    @pl.loop(0, rows // tile)
    def _(step):
        at = pl.ds(step * tile, tile)
        attended_grad[at, :] = mm(branch_grad[at, :], w_out[...], NT).astype(BF16)

    out_grad[...] = mm(attended[...], branch_grad[...], TN).astype(BF16)

    @pl.loop(0, HEADS // 2)
    def _(pair):
        attention_back(
            joined, log_rows, attended_grad, joined_grad, key_bias, key_total, value_total, pair, block
        )

    @pl.loop(0, 3)
    def _(part):
        columns = pl.ds(pl.multiple_of(part * width, width), width)
        qkv_grad[:, columns] = mm(normed[...], joined_grad[:, columns], TN).astype(BF16)

    gain_grad[...] = jnp.zeros_like(gain_grad)
    table_grad[...] = jnp.zeros_like(table_grad)

    @pl.loop(0, rows // 256)
    def _(step):
        at = pl.ds(step * 256, 256)
        grad = mm(joined_grad[at, :], w_qkv[...], NT)
        unit, scale = norm_parts(inputs[at, :].astype(F32) + pass_row[0:1, :])
        total = hidden_grad[at, :] + norm_back(unit, scale, grad, gain[0:1, :])
        grad_input[at, :] = total
        gain_grad[0:1, :] += jnp.sum(grad * unit, axis=0, keepdims=True)
        table_grad[0:1, :] += jnp.sum(total, axis=0, keepdims=True)


def whole(count):
    return [pl.BlockSpec(memory_space=pltpu.VMEM)] * count


def call(kernel, outs, scratch, *args, scalars=0):
    specs = [pl.BlockSpec(memory_space=pltpu.SMEM)] * scalars + whole(len(args) - scalars)
    return pl.pallas_call(
        kernel,
        out_shape=[jax.ShapeDtypeStruct(shape, kind) for shape, kind in outs],
        in_specs=specs,
        out_specs=whole(len(outs)),
        scratch_shapes=[pltpu.VMEM(shape, kind) for shape, kind in scratch],
        compiler_params=pltpu.CompilerParams(vmem_limit_bytes=VMEM_LIMIT),
    )(*args)


def body(
    inputs, seq_lens, pass_idx, pass_table, gain_attn, w_qkv, w_out, gain_mlp, w_up, w_down, cotangent,
):
    _, rows, width = inputs.shape
    inputs2 = inputs[0]
    out_cot = cotangent[0]
    gather = functools.partial(lax.all_gather, axis_name="shard", tiled=True)
    table = gather(pass_table, axis=1)
    attn_gain = jnp.broadcast_to(gather(gain_attn, axis=0).astype(F32)[None, :], (8, width))
    mlp_gain = jnp.broadcast_to(gather(gain_mlp, axis=0).astype(F32)[None, :], (8, width))
    qkv_w = gather(w_qkv, axis=0)
    out_w = gather(w_out, axis=0)
    up_w = gather(w_up, axis=0)
    down_w = gather(w_down, axis=0)
    chosen = (pass_idx[:, None] == jnp.arange(table.shape[0], dtype=jnp.int32)[None, :]).astype(F32)
    pass_row = jnp.broadcast_to(
        jnp.sum(chosen[0][:, None] * table.astype(F32), axis=0, keepdims=True), (8, width)
    )
    block = 256
    tile = 512
    joined, attended, sums, hidden = call(
        functools.partial(front_kernel, block, tile),
        [((rows, 3 * width), BF16), ((rows, width), BF16), ((HEADS // 2, rows, PAIR), F32), ((rows, width), F32)],
        [((rows, width), BF16), ((rows, PAIR), BF16)],
        seq_lens, inputs2, pass_row, attn_gain, qkv_w, out_w, scalars=1,
    )
    chunk = 1024
    outputs, hidden_grad, mlp_gain_grad, up_grad, down_grad = call(
        functools.partial(mlp_kernel, tile, chunk),
        [((rows, width), BF16), ((rows, width), F32), ((8, width), F32), (up_w.shape, BF16), (down_w.shape, BF16)],
        [((rows, width), BF16), ((rows, width), F32), ((rows, width), F32), ((rows, chunk), BF16), ((rows, chunk), BF16)],
        hidden, out_cot, mlp_gain, up_w, down_w,
    )
    log_rows = jnp.stack([sums[:, :, 0], sums[:, :, HEAD_DIM]], axis=1).reshape(HEADS, rows)
    grad_input, attn_gain_grad, table_row, qkv_grad, out_grad = call(
        functools.partial(back_kernel, block, tile),
        [((rows, width), F32), ((8, width), F32), ((8, width), F32), (qkv_w.shape, BF16), (out_w.shape, BF16)],
        [((rows, width), BF16), ((rows, width), BF16), ((rows, width), BF16), ((rows, 3 * width), BF16),
         ((rows, PAIR), BF16), ((rows, PAIR), F32), ((rows, PAIR), F32)],
        seq_lens, inputs2, pass_row, attn_gain, qkv_w, out_w, joined, log_rows, attended, hidden_grad, scalars=1,
    )
    scatter = lambda grad, dim=0: lax.psum_scatter(grad, "shard", scatter_dimension=dim, tiled=True)
    up_part, down_part = scatter(up_grad), scatter(down_grad)
    out_part, qkv_part = scatter(out_grad), scatter(qkv_grad)
    small = jnp.concatenate(
        [chosen[0][:, None] * table_row[0:1], attn_gain_grad[0:1], mlp_gain_grad[0:1]], axis=0
    )
    small = lax.psum(scatter(small, 1), "rep")
    up_sum, down_sum, out_sum, qkv_sum = lax.psum((up_part, down_part, out_part, qkv_part), "rep")
    count = table.shape[0]
    return (
        outputs[None], grad_input[None], small[:count], small[count], qkv_sum.astype(F32), out_sum.astype(F32),
        small[count + 1], up_sum.astype(F32), down_sum.astype(F32),
    )


MESH = pl.DeviceIdType.MESH


class Place:
    def __init__(self):
        self.me = lax.axis_index("shard")
        self.z = lax.axis_index("rep")
        self.core = lax.rem(self.me, 2)
        self.x = lax.rem(self.me // 2, 2)
        self.y = self.me // 4
        self.by_x = self.me + 2 - 4 * self.x
        self.by_y = self.me + 4 - 8 * self.y
        self.by_core = self.me + 1 - 2 * self.core
        self.by_both = self.by_x + 4 - 8 * self.y
        self.side = lax.rem(self.z, 2)
        self.by_z = self.z + 1 - 2 * self.side

    def at(self, shard):
        return (shard, self.z)


def remote(src, dst, sends, recvs, index, device):
    return pltpu.make_async_remote_copy(
        src_ref=src, dst_ref=dst, send_sem=sends.at[index], recv_sem=recvs.at[index],
        device_id=device, device_id_type=MESH,
    )


class Gather:
    def __init__(self, place, part, fills, sends, recvs, local, row, shared):
        self.place, self.part, self.fills, self.shared = place, part, fills, shared
        self.sends, self.recvs, self.local, self.row = sends, recvs, local, row
        self.slots = 17 if shared else 9

    def piece(self, shard, columns=None, other=False):
        if not self.shared:
            return self.part(shard, None, columns)
        side = 1 - self.place.side if other else self.place.side
        return self.part(shard, side, columns)

    def make(self, slot):
        p = self.place
        rep = p.z
        if slot < 2:
            ref, shard = self.piece(p.me), (p.by_x, p.by_y)[slot]
        elif slot == 2:
            ref, shard = self.part(p.me, None, None), p.by_core
        elif slot == 3:
            ref, shard = self.piece(p.by_x, 0), p.by_y
        elif slot == 4:
            ref, shard = self.piece(p.by_y, 1), p.by_x
        else:
            kind = (slot - 5) % 4
            source = (p.by_x, p.by_y, p.by_both, p.by_both)[kind]
            ref = self.piece(source, None if kind < 2 else kind - 2, slot >= 13)
            shard = p.by_core
            if 9 <= slot < 13:
                shard, rep = p.me, p.by_z
        return remote(ref, ref, self.sends, self.recvs, (self.row, slot), (shard, rep))

    def fill(self):
        for source, target in self.fills:
            pltpu.make_async_copy(source, target, self.local.at[self.row]).start()

    def start(self):
        own = self.part(self.place.me, None, None)
        pltpu.make_async_copy(own, own, self.local.at[self.row]).wait()
        for slot in range(3):
            self.make(slot).start()

    def pass_on(self, slot, *targets):
        self.make(slot).wait_recv()
        for target in targets:
            if target < self.slots:
                self.make(target).start()

    def relay(self):
        self.pass_on(0, 3, 5, 9)
        self.pass_on(1, 4, 6, 10)

    def finish(self):
        self.pass_on(3, 7, 11)
        self.pass_on(4, 8, 12)

    def across(self):
        if self.shared:
            for slot in range(9, 13):
                self.pass_on(slot, slot + 4)

    def ready(self):
        for slot in (2, 5, 6, 7, 8) + ((13, 14, 15, 16) if self.shared else ()):
            self.make(slot).wait_recv()

    def drain(self):
        for slot in range(self.slots):
            self.make(slot).wait_send()


def enter(place, shards, reps=()):
    barrier = pltpu.get_barrier_semaphore()
    for shard in shards:
        pl.semaphore_signal(barrier, inc=1, device_id=(shard, place.z), device_id_type=MESH)
    for rep in reps:
        pl.semaphore_signal(barrier, inc=1, device_id=(place.me, rep), device_id_type=MESH)
    pl.semaphore_wait(barrier, len(shards) + len(reps))


def part_of(ref, rows, lead, start, width):
    def part(shard, side, half):
        count, first, left, wide = rows, shard * rows, start, width
        if side is None and half is not None:
            side, half = half, None
        if side is not None:
            count = rows // 2
            first = first + side * count
        if half is not None:
            wide = width // 2
            left = start + half * wide
        return ref.at[lead + (pl.ds(pl.multiple_of(first, count), count), pl.ds(left, wide))]

    return part


def up_fills(own, ref, index, place, shards):
    part, chunk = own.shape[0], ref.shape[2]
    lanes = chunk // shards
    slices = own.shape[1] // chunk
    rows = pl.ds(pl.multiple_of(place.me * part, part), part)
    return [
        (own.at[:, pl.ds((slices * shard + index) * lanes, lanes)], ref.at[index, rows, pl.ds(shard * lanes, lanes)])
        for shard in range(shards)
    ]


def down_fills(own, ref, index, place, shards):
    count = ref.shape[1] // shards
    rows = pl.ds(pl.multiple_of(place.me * count, count), count)
    return [(own.at[pl.ds(index * count, count), :], ref.at[index, rows, :])]


def pair_columns(pair):
    return [pl.ds(pl.multiple_of((3 * pair + plane) * PAIR, PAIR), PAIR) for plane in range(3)]


def attention_rows(joined, attended, log_rows, key_bias, pair, block, between):
    rows = attended.shape[0]
    columns = pl.ds(pl.multiple_of(pair * PAIR, PAIR), PAIR)
    query_columns, key_columns, value_columns = pair_columns(pair)
    keys = joined[:, key_columns]
    values = joined[:, value_columns]
    bias = key_bias[...]
    biased = [key_with_bias(keys, bias, head)[0] for head in range(2)]
    for first in range(0, rows, block):
        live = first + block
        query = joined[pl.ds(first, block), query_columns]
        mixed = []
        sums = []
        for head in range(2):
            asked, _ = query_with_bias(query, head)
            scores = mm(asked, biased[head][:live], NT)
            row_at = lax.broadcasted_iota(jnp.int32, (block, block), 0)
            key_at = lax.broadcasted_iota(jnp.int32, (block, block), 1)
            last = jnp.where(key_at <= row_at, scores[:, first:], MASKED)
            scores = last if first == 0 else jnp.concatenate([scores[:, :first], last], axis=1)
            top = jnp.max(scores, axis=-1, keepdims=True)
            weights = jnp.exp(scores - top)
            total = jnp.sum(weights, axis=-1, keepdims=True)
            mixed.append(mm(weights.astype(BF16), values[:live]) / total)
            sums.append(top + jnp.log(total))
        lanes = lanes_of(mixed[0].shape)
        attended[pl.ds(first, block), columns] = jnp.where(lanes < HEAD_DIM, mixed[0], mixed[1]).astype(BF16)
        turned = jnp.transpose(jnp.where(lanes < HEAD_DIM, sums[0], sums[1]))
        log_rows[pl.ds(pair * 2, 1), pl.ds(first, block)] = turned[0:1]
        log_rows[pl.ds(pair * 2 + 1, 1), pl.ds(first, block)] = turned[HEAD_DIM : HEAD_DIM + 1]
        between(first // block)


def norm_rows(inputs, pass_row, gain, normed):
    @pl.loop(0, inputs.shape[0] // 256)
    def _(step):
        at = pl.ds(step * 256, 256)
        entered = inputs[at, :].astype(F32) + pass_row
        normed[at, :] = (norm_parts(entered)[0] * gain).astype(BF16)


SHARED = (False, False, True, True, False, True, True, False, True, True, False)
SPANS = ((0, 1), (1, 1), (2, 2), (4, 2))

PLAN = {
    "begin": "r0 s2",
    "normed": "f0 r1",
    (0, 0): "r2 s3",
    (0, 1): "f1",
    (0, 3): "f2 s4",
    (1, 1): "r3",
    (1, 2): "a2",
    (1, 3): "s5",
    (2, 0): "f3 r4",
    (2, 2): "s6",
    (2, 3): "r5",
    (3, 1): "a3 f4",
    (3, 2): "s7",
    (4, 0): "f5 r6",
    (4, 3): "s8",
    (5, 1): "a5 r7 f6",
    (5, 3): "s9",
    "row 0": "r8",
    "row 1": "a6 f7 s10",
    "mlp 0 0": "f8 r9",
    "mlp 0 1": "r10",
    "mlp 0 down": "a8 f9",
    "mlp 1 0": "a9 f10",
}


def fore_comm_kernel(
    block, tile, slices,
    length_ref, pass_ref, table_own, attn_gain_own, mlp_gain_own,
    inputs_in, cotangent_in, qkv_own, out_own, up_own, down_own,
    rows_out, log_out, gain_grad,
    up_half, down_half, normed_out, joined_out, attended_out, qkv_out, out_out, outputs_out, hidden_grad_out,
    up_done_out, down_done_out,
    inputs, cotangent, slots, small_wide, small_own, normed, joined, attended, hidden, qkv_w, out_w, up_w, down_w,
    key_bias, mixed, hidden_grad, up_done, down_done,
    up_grads, up_first, up_x, up_y, up_last, down_grads, down_first, down_x, down_y, down_last,
    sends, recvs, local, small_sends, small_recvs, up_sends, up_recvs, down_sends, down_recvs, loads, saves,
):
    place = Place()
    rows, width = inputs.shape
    shards = slots.shape[0]
    part = qkv_own.shape[0]
    groups = len(SPANS)
    pairs = width // PAIR

    pieces = []

    def add(part_at, fills):
        row = len(pieces)
        pieces.append(Gather(place, part_at, fills, sends, recvs, local, row, SHARED[row]))

    own_rows = pl.ds(pl.multiple_of(place.me * part, part), part)
    for start, number in SPANS:
        fills = [
            (qkv_own.at[:, pl.ds(plane * width + pair * PAIR, PAIR)], qkv_w.at[own_rows, columns])
            for pair in range(start, start + number)
            for plane, columns in enumerate(pair_columns(pair))
        ]
        add(part_of(qkv_w, part, (), start * 3 * PAIR, number * 3 * PAIR), fills)
    add(part_of(out_w, part, (), 0, width), [(out_own, out_w.at[own_rows, :])])
    for index in range(slices):
        add(part_of(up_w, part, (index,), 0, up_w.shape[2]), up_fills(up_own, up_w, index, place, shards))
        add(part_of(down_w, down_w.shape[1] // shards, (index,), 0, width),
            down_fills(down_own, down_w, index, place, shards))
    count = len(pieces)
    take = [
        pltpu.make_async_copy(inputs_in, inputs, loads.at[0]), pltpu.make_async_copy(cotangent_in, cotangent, loads.at[1]),
    ]
    pieces[0].fill()
    take[0].start()
    for piece in pieces[1:]:
        piece.fill()
    take[1].start()

    small_wide[...] = jnp.zeros_like(small_wide)
    small_wide[0 : table_own.shape[0], 0:part] = table_own[...].astype(F32)
    small_wide[8:9, 0:part] = attn_gain_own[...].astype(F32)
    small_wide[9:10, 0:part] = mlp_gain_own[...].astype(F32)
    small_own[...] = small_wide[...].astype(BF16)
    slots[place.me] = small_own[...]

    others = [lax.rem(place.me + shift, shards) for shift in range(1, shards)]
    enter(place, others, [place.by_z])
    smalls = [
        remote(small_own, slots.at[place.me], small_sends, small_recvs, shift, place.at(other))
        for shift, other in enumerate(others)
    ]
    for copy in smalls:
        copy.start()
    pieces[0].start()
    pieces[1].start()

    def step_on(point):
        for what in PLAN.get(point, "").split():
            piece = pieces[int(what[1:])]
            {"s": piece.start, "r": piece.relay, "f": piece.finish, "a": piece.across}[what[0]]()

    def up_message(index):
        return Scatter(
            place, up_grads.at[lax.rem(index, 2)], up_first.at[index], up_x.at[index], up_y.at[index], up_last.at[index],
            up_sends, up_recvs, index,
        )

    def down_message(index):
        return Scatter(
            place, down_grads.at[lax.rem(index, 2)], down_first.at[index], down_x.at[index], down_y.at[index], down_last.at[index],
            down_sends, down_recvs, index,
        )

    fill_bias(length_ref[0], key_bias)
    for copy in smalls:
        copy.wait_recv()
    total = jnp.concatenate([slots[shard].astype(F32)[:, 0:part] for shard in range(shards)], axis=1)
    places = lax.broadcasted_iota(jnp.int32, total.shape, 0)
    rows_out[0:1, :] = jnp.sum(jnp.where(places == pass_ref[0], total, 0.0), axis=0, keepdims=True)
    rows_out[1:3, :] = total[8:10]
    rows_out[3:8, :] = jnp.zeros((5, width), F32)

    take[0].wait()
    step_on("begin")
    norm_rows(inputs, rows_out[0:1, :], rows_out[1:2, :], normed)
    step_on("normed")

    keep = {}

    def save(source, target, name=None):
        keep[name or len(keep)] = copy = pltpu.make_async_copy(source, target, saves.at[len(keep)])
        return copy

    save(normed, normed_out, "normed").start()
    qkv_save = save(qkv_w, qkv_out)

    @pl.loop(0, pairs)
    def _(pair):
        for index, (start, number) in enumerate(SPANS):
            @pl.when(pair == start)
            def _(index=index, start=start, number=number):
                pieces[index].ready()
                if index == groups - 1:
                    qkv_save.start()
                columns = pl.ds(start * 3 * PAIR, number * 3 * PAIR)

                @pl.loop(0, rows // tile)
                def _(step):
                    at = pl.ds(step * tile, tile)
                    joined[at, columns] = mm(normed[at, :], qkv_w[:, columns]).astype(BF16)

        def between(place_at):
            for index in range(pairs):
                if (index, place_at) in PLAN:
                    @pl.when(pair == index)
                    def _(index=index):
                        step_on((index, place_at))

        attention_rows(joined, attended, log_out, key_bias, pair, block, between)

    chunk = up_w.shape[2]
    second = attended
    active, rising_grad = joined.at[:, pl.ds(0, chunk)], joined.at[:, pl.ds(chunk, chunk)]
    save(attended, attended_out, "attended").start()
    save(joined, joined_out, "joined").start()
    pieces[groups].ready()
    save(out_w, out_out).start()
    gain = rows_out[2:3, :]
    for step in range(rows // tile):
        at = pl.ds(step * tile, tile)
        entered = inputs[at, :].astype(F32) + rows_out[0:1, :]
        hidden[at, :] = entered + mm(attended[at, :], out_w[...])
        step_on("row %d" % step)
        if step == 0:
            keep["attended"].wait()

        @pl.loop(0, tile // 256)
        def _(step_in):
            at = pl.ds(step * tile + step_in * 256, 256)
            values = hidden[at, :]
            second[at, :] = (norm_parts(values)[0] * gain).astype(BF16)
            mixed[at, :] = values
            hidden_grad[at, :] = jnp.zeros((256, width), F32)

    take[1].wait()
    keep["joined"].wait()

    @pl.loop(0, slices)
    def _(index_at):
        for index in range(slices):
            @pl.when(index_at == index)
            def _(index=index):
                pieces[groups + 1 + 2 * index].ready()
                pieces[groups + 2 + 2 * index].ready()

        @pl.loop(0, rows // tile)
        def _(step):
            at = pl.ds(step * tile, tile)
            rising = mm(second[at, :], up_w[index_at])
            active_grad = mm(cotangent[at, :], down_w[index_at], NT)
            bent, slope = gelu_both(rising)
            shown = bent.astype(BF16)
            moved = (slope * active_grad).astype(BF16)
            active[at, :] = shown
            rising_grad[at, :] = moved
            mixed[at, :] += mm(shown, down_w[index_at])
            hidden_grad[at, :] += mm(moved, up_w[index_at], NT)

            for index in range(slices):
                for inner in range(rows // tile):
                    if "mlp %d %d" % (index, inner) in PLAN:
                        @pl.when((index_at == index) & (step == inner))
                        def _(index=index, inner=inner):
                            step_on("mlp %d %d" % (index, inner))

            @pl.when((index_at > 0) & (step == 0))
            def _():
                message = up_message(index_at - 1)
                message.merge()
                message.spread()

            @pl.when((index_at > 0) & (step == 1))
            def _():
                down_message(index_at - 1).fold()

        @pl.when(index_at > 1)
        def _():
            down_message(index_at - 2).swap_copy().wait_send()
            up_message(index_at - 2).swap_copy().wait_send()

        slot = lax.rem(index_at, 2)
        down_grads[slot] = mm(active[...], cotangent[...], TN).astype(BF16).reshape(down_grads.shape[1:])
        down_message(index_at).swap()

        @pl.when(index_at == 0)
        def _():
            step_on("mlp 0 down")

        @pl.when(index_at > 0)
        def _():
            up_message(index_at - 1).fold()

        up_grads[slot] = mm(second[...], rising_grad[...], TN).astype(BF16).reshape(up_grads.shape[1:])
        up_message(index_at).swap()

        @pl.when(index_at == 0)
        def _():
            step_on("mlp 0 up")

        @pl.when(index_at < slices - 1)
        def _():
            message = down_message(index_at)
            message.merge()
            message.spread()

        @pl.when(index_at > 0)
        def _():
            down_message(index_at - 1).close(down_done.at[index_at - 1])
            up_message(index_at - 1).close(up_done.at[index_at - 1])

    down_message(slices - 1).merge()
    save(down_first.at[slices - 1], down_half).start()
    save(up_done, up_done_out).start()
    save(down_done, down_done_out).start()
    gain_grad[...] = jnp.zeros_like(gain_grad)
    keep["normed"].wait()
    first_row = len(keep) + 2

    @pl.loop(0, rows // 256)
    def _(step):
        at = pl.ds(step * 256, 256)
        normed[at, :] = mixed[at, :].astype(BF16)
        unit, scale = norm_parts(hidden[at, :])
        grad = hidden_grad[at, :]
        hidden_grad[at, :] = cotangent[at, :].astype(F32) + norm_back(unit, scale, grad, gain)
        gain_grad[0:1, :] += jnp.sum(grad * unit, axis=0, keepdims=True)
        pltpu.make_async_copy(hidden_grad.at[at, :], hidden_grad_out.at[at, :], saves.at[first_row + step]).start()

    save(normed, outputs_out).start()
    up_message(slices - 1).merge()
    save(up_first.at[slices - 1], up_half).start()
    for step in range(rows // 256):
        at = pl.ds(step * 256, 256)
        pltpu.make_async_copy(hidden_grad.at[at, :], hidden_grad_out.at[at, :], saves.at[first_row + step]).wait()
    for piece in pieces:
        piece.drain()
    for copy in smalls:
        copy.wait_send()
    for index in range(slices):
        up_message(index).drain(index >= slices - 2, index < slices - 1)
        down_message(index).drain(index >= slices - 2, index < slices - 1)
    for name, copy in keep.items():
        if name not in ("normed", "attended", "joined"):
            copy.wait()


def any_spec(count):
    return [pl.BlockSpec(memory_space=pl.ANY)] * count


def smem_spec(count):
    return [pl.BlockSpec(memory_space=pltpu.SMEM)] * count


def vmem_spec(count):
    return [pl.BlockSpec(memory_space=pltpu.VMEM)] * count


def shaped(shape, kind):
    return jax.ShapeDtypeStruct(shape, kind)


class Scatter:
    def __init__(self, place, grads, first, by_x, by_y, last, sends, recvs, row):
        self.place, self.grads, self.first = place, grads, first
        self.in_x, self.in_y, self.last = by_x, by_y, last
        self.sends, self.recvs, self.row = sends, recvs, row
        half = first.shape[-2] // 2
        self.upper, self.lower = pl.ds(0, half), pl.ds(half, half)

    def copy(self, slot, src, dst, shard):
        return remote(src, dst, self.sends, self.recvs, (self.row, slot), self.place.at(shard))

    def swap_copy(self):
        p = self.place
        return self.copy(0, self.grads.at[:, :, 1 - p.core], self.first, p.by_core)

    def spread_copies(self):
        p = self.place
        return [
            self.copy(1, self.first.at[:, 1 - p.x, self.upper], self.in_x, p.by_x),
            self.copy(2, self.first.at[1 - p.y, :, self.lower], self.in_y, p.by_y),
        ]

    def fold_copies(self):
        p = self.place
        return [
            self.copy(3, self.in_x.at[1 - p.y], self.last.at[self.upper], p.by_y),
            self.copy(4, self.in_y.at[1 - p.x], self.last.at[self.lower], p.by_x),
        ]

    def swap(self):
        self.swap_copy().start()

    def merge(self, target=None):
        p = self.place
        target = self.first if target is None else target
        self.swap_copy().wait_recv()
        for y in range(2):
            for x in range(2):
                total = self.grads[y, x, p.core].astype(F32) + self.first[y, x].astype(F32)
                target[y, x] = total.astype(BF16)

    def spread(self):
        for copy in self.spread_copies():
            copy.start()

    def fold(self):
        p = self.place
        for copy in self.spread_copies():
            copy.wait_recv()
        for other in range(2):
            total = self.first[other, p.x, self.upper].astype(F32) + self.in_x[other].astype(F32)
            self.in_x[other] = total.astype(BF16)
            total = self.first[p.y, other, self.lower].astype(F32) + self.in_y[other].astype(F32)
            self.in_y[other] = total.astype(BF16)
        for copy in self.fold_copies():
            copy.start()

    def close(self, target):
        p = self.place
        for copy in self.fold_copies():
            copy.wait_recv()
        target[self.upper] = (self.last[self.upper].astype(F32) + self.in_x[p.y].astype(F32)).astype(BF16)
        target[self.lower] = (self.last[self.lower].astype(F32) + self.in_y[p.x].astype(F32)).astype(BF16)

    def drain(self, swapped=True, spread=True):
        if swapped:
            self.swap_copy().wait_send()
        if spread:
            for copy in self.spread_copies() + self.fold_copies():
                copy.wait_send()


def scatter_scratch(count, part, columns, slots=None):
    return [
        pltpu.VMEM((slots or count, 2, 2, 2, part, columns), BF16), pltpu.VMEM((count, 2, 2, part, columns), BF16),
        pltpu.VMEM((count, 2, part // 2, columns), BF16), pltpu.VMEM((count, 2, part // 2, columns), BF16),
        pltpu.VMEM((count, part, columns), BF16),
    ]


def dma(*shapes):
    return [pltpu.SemaphoreType.DMA(shape) for shape in shapes]


def fore_comm(slices, seq_lens, pass_idx, table, attn_gain, mlp_gain, inputs, cotangent, qkv, out, up, down):
    rows, width = inputs.shape
    up_part, chunk = up.shape[0], up.shape[1] // slices
    down_part = down.shape[0] // slices
    shards = width // up_part
    count = len(SPANS) + 1 + 2 * slices
    vm = lambda *shape: pltpu.VMEM(shape, BF16)
    vf = lambda *shape: pltpu.VMEM(shape, F32)
    return pl.pallas_call(
        functools.partial(fore_comm_kernel, 256, 512, slices),
        out_shape=[
            shaped((8, width), F32), shaped((16, rows), F32), shaped((8, width), F32),
            shaped((2, 2, up_part, chunk), BF16), shaped((2, 2, down_part, width), BF16),
            shaped((rows, width), BF16), shaped((rows, 3 * width), BF16), shaped((rows, width), BF16),
            shaped((width, 3 * width), BF16), shaped((width, width), BF16), shaped((rows, width), BF16),
            shaped((rows, width), F32), shaped((slices - 1, up_part, chunk), BF16),
            shaped((slices - 1, down_part, width), BF16),
        ],
        in_specs=smem_spec(2) + vmem_spec(3) + any_spec(6),
        out_specs=vmem_spec(3) + any_spec(11),
        scratch_shapes=[
            vm(rows, width), vm(rows, width), vm(shards, 16, PAIR), vf(16, PAIR), vm(16, PAIR), vm(rows, width),
            vm(rows, 3 * width), vm(rows, width), vf(rows, width), vm(width, 3 * width), vm(width, width),
            vm(slices, width, chunk), vm(slices, chunk, width), vm(rows, PAIR), vf(rows, width), vf(rows, width),
            vm(slices - 1, up_part, chunk), vm(slices - 1, down_part, width),
        ]
        + scatter_scratch(slices, up_part, chunk, 2)
        + scatter_scratch(slices, down_part, width, 2)
        + dma((count, 17), (count, 17), (count,), (shards,), (shards,), (slices, 5), (slices, 5), (slices, 5),
              (slices, 5), (2,), (10 + rows // 256,)),
        compiler_params=pltpu.CompilerParams(
            vmem_limit_bytes=VMEM_LIMIT, collective_id=1, has_side_effects=True
        ),
    )(seq_lens, pass_idx, table, attn_gain, mlp_gain, inputs, cotangent, qkv, out, up, down)


class Column:
    def __init__(self, place, block, inward, middle, outward, total, sends, recvs, row):
        self.place, self.block, self.inward, self.middle = place, block, inward, middle
        self.outward, self.total = outward, total
        self.sends, self.recvs, self.row = sends, recvs, row
        self.end = (place.z == 0) | (place.z == 3)

    def copy(self, slot, src, dst, rep):
        return remote(src, dst, self.sends, self.recvs, (self.row, slot), (self.place.me, rep))

    def in_copy(self):
        return self.copy(0, self.block, self.inward, 1 + self.place.z // 3)

    def across_copy(self):
        return self.copy(1, self.middle, self.outward, 3 - self.place.z)

    def out_copy(self):
        return self.copy(2, self.total, self.outward, 3 * (self.place.z - 1))

    def begin(self):
        @pl.when(self.end)
        def _():
            self.in_copy().start()

    def cross(self):
        @pl.when(jnp.logical_not(self.end))
        def _():
            self.in_copy().wait_recv()
            self.middle[...] = (self.block[...].astype(F32) + self.inward[...].astype(F32)).astype(BF16)
            self.across_copy().start()

    def settle(self):
        @pl.when(jnp.logical_not(self.end))
        def _():
            self.across_copy().wait_recv()
            self.total[...] = (self.middle[...].astype(F32) + self.outward[...].astype(F32)).astype(BF16)
            self.out_copy().start()

    def finish(self):
        @pl.when(self.end)
        def _():
            self.out_copy().wait_recv()
            self.total[...] = self.outward[...]
            self.in_copy().wait_send()

        @pl.when(jnp.logical_not(self.end))
        def _():
            self.across_copy().wait_send()
            self.out_copy().wait_send()


def attention_columns(
    joined, log_rows, grads, joined_grad, key_bias, key_total, value_total, pair, block, between,
):
    rows = grads.shape[0]
    columns = pl.ds(pl.multiple_of(pair * PAIR, PAIR), PAIR)
    query_columns, key_columns, value_columns = pair_columns(pair)
    keys = joined[:, key_columns]
    values = joined[:, value_columns]
    bias = key_bias[...]
    biased = [key_with_bias(keys, bias, head) for head in range(2)]
    key_total[...] = jnp.zeros_like(key_total)
    value_total[...] = jnp.zeros_like(value_total)
    for first in range(0, rows, block):
        live = first + block
        query = joined[pl.ds(first, block), query_columns]
        grad = grads[pl.ds(first, block), columns]
        query_grad = None
        for head in range(2):
            asked, asked_only = query_with_bias(query, head)
            grad_only = head_only(grad, head)[0]
            scores = mm(biased[head][0][:live], asked, NT)
            share_grad = mm(values[:live], grad_only, NT)
            log_sum = log_rows[pl.ds(pair * 2 + head, 1), pl.ds(first, block)]
            shares = jnp.exp(scores - log_sum)
            key_at = lax.broadcasted_iota(jnp.int32, (block, block), 0)
            row_at = lax.broadcasted_iota(jnp.int32, (block, block), 1)
            last = jnp.where(key_at <= row_at, shares[first:], 0.0)
            shares = last if first == 0 else jnp.concatenate([shares[:first], last], axis=0)
            inner = jnp.sum(share_grad * shares, axis=0, keepdims=True)
            score_grad = (shares * (share_grad - inner)).astype(BF16)
            value_total[:live, :] += mm(shares.astype(BF16), grad_only)
            key_total[:live, :] += mm(score_grad, asked_only)
            part = mm(score_grad, biased[head][1][:live], TN)
            query_grad = part if query_grad is None else query_grad + part
        joined_grad[pl.ds(first, block), query_columns] = (query_grad * HEAD_DIM**-0.5).astype(BF16)
        if live == rows:
            joined_grad[:, key_columns] = key_total[...].astype(BF16)
            joined_grad[:, value_columns] = value_total[...].astype(BF16)
        if first // block % 2 == 1:
            between(first // block - 1)
            between(first // block)


def back_comm_kernel(
    block, tile,
    length_ref, pass_ref, rows_in, log_rows, mlp_gain_grad, up_done, down_done, up_half, down_half,
    hidden_grad_in, out_in, attended_in, normed_in, joined_in, qkv_in, inputs_in,
    grad_input_out, small_sum, up_total, down_total, attn_total,
    hidden_grad, out_w, attended, inputs, grad_input,
    qkv_w, joined, branch_grad, attended_grad, normed, joined_grad, key_bias, key_total, value_total,
    grads, first, in_x, in_y, last, block_sum,
    up_x, up_y, up_last, up_block, down_x, down_y, down_last, down_block,
    up_in, up_mid, up_out, down_in, down_mid, down_out, attn_in, attn_mid, attn_out,
    small_own, small_parts, small_slots, small_plane, small_reps,
    sends, recvs, up_sends, up_recvs, down_sends, down_recvs, z_sends, z_recvs,
    plane_sends, plane_recvs, rep_sends, rep_recvs, loads, saves,
):
    place = Place()
    rows, width = inputs.shape
    shards = small_slots.shape[0]
    reps = small_reps.shape[0]
    chunks = up_total.shape[0]
    pairs = width // PAIR
    others = [lax.rem(place.me + shift, shards) for shift in range(1, shards)]
    others_z = [lax.rem(place.z + shift, reps) for shift in range(1, reps)]
    take = [
        pltpu.make_async_copy(source, target, loads.at[index])
        for index, (source, target) in enumerate((
            (hidden_grad_in, hidden_grad), (out_in, out_w), (attended_in, attended), (joined_in, joined),
            (normed_in, normed), (qkv_in, qkv_w), (inputs_in, inputs),
        ))
    ]
    for copy in take:
        copy.start()
    enter(place, others, others_z)

    up_late = Scatter(place, None, up_half, up_x, up_y, up_last, up_sends, up_recvs, 0)
    down_late = Scatter(place, None, down_half, down_x, down_y, down_last, down_sends, down_recvs, 0)

    half = 3 * PAIR
    sent = [(0, 0, 2 * half), (1, 0, 2 * half), (2, 0, 2 * half), (3, 0, half), (3, half, half)]

    def message(index):
        slot, start, wide = sent[index]
        view = lambda ref: ref.at[(slot,) + (slice(None),) * (len(ref.shape) - 2) + (pl.ds(start, wide),)]
        return Scatter(
            place, view(grads), view(first), view(in_x), view(in_y), view(last), sends, recvs, index,
        )

    lines = {}

    def line(key, source, inward, middle, outward, total):
        lines[key] = Column(place, source, inward, middle, outward, total, z_sends, z_recvs, len(lines))

    for index in range(chunks):
        final = index == chunks - 1
        line(("d", index), down_block if final else down_done.at[index],
             down_in.at[index], down_mid.at[index], down_out.at[index], down_total.at[index])
        line(("u", index), up_block if final else up_done.at[index],
             up_in.at[index], up_mid.at[index], up_out.at[index], up_total.at[index])
    for index, (slot, start, wide) in enumerate(sent):
        line(("a", index), *(
            ref.at[slot, :, pl.ds(start, wide)] for ref in (block_sum, attn_in, attn_mid, attn_out, attn_total)
        ))

    down_late.spread()
    up_late.spread()
    for index in range(chunks - 1):
        lines["d", index].begin()
        lines["u", index].begin()

    fill_bias(length_ref[0], key_bias)
    take[0].wait()
    take[1].wait()

    @pl.loop(0, rows // tile)
    def _(step):
        at = pl.ds(step * tile, tile)
        shown = hidden_grad[at, :].astype(BF16)
        branch_grad[at, :] = shown
        attended_grad[at, :] = mm(shown, out_w[...], NT).astype(BF16)

    take[2].wait()
    grads[0] = mm(attended[...], branch_grad[...], TN).astype(BF16).reshape(grads.shape[1:])
    message(0).swap()
    lines["d", 0].cross()
    down_late.fold()
    take[3].wait()

    def late_close(late, target, key):
        late.close(target)
        lines[key].begin()

    def close(index):
        slot, start, wide = sent[index]
        message(index).close(block_sum.at[slot, :, pl.ds(start, wide)])
        lines["a", index].begin()

    def send(index):
        message(index).merge()
        message(index).spread()

    def fold(index):
        message(index).fold()

    def cross(*keys):
        for key in keys:
            lines[key[0], int(key[1])].cross()

    def settle(*keys):
        for key in keys:
            lines[key[0], int(key[1])].settle()

    def gradient(index):
        slot, start, wide = sent[index]
        columns = pl.ds((slot - 1) * 2 * half + start, wide)
        part = mm(normed[...], joined_grad[:, columns], TN).astype(BF16)
        grads[slot, :, :, :, :, pl.ds(start, wide)] = part.reshape(grads.shape[1:5] + (wide,))
        message(index).swap()

    plan = {
        (0, 1): lambda: send(0),
        (0, 2): lambda: (cross("u0"), up_late.fold()),
        (0, 3): lambda: late_close(down_late, down_block, ("d", 2)),
        (1, 0): lambda: settle("d0"),
        (1, 2): lambda: (cross("d1"), fold(0)),
        (1, 3): lambda: (late_close(up_late, up_block, ("u", 2)), settle("u0"), take[4].wait(), gradient(1)),
        (2, 0): lambda: (cross("u1"), close(0)),
        (2, 2): lambda: (send(1), settle("d1")),
        (2, 3): lambda: cross("d2"),
        (3, 2): lambda: (settle("u1"), cross("u2")),
        (3, 3): lambda: (fold(1), gradient(2)),
        (4, 0): lambda: (cross("a0"), settle("d2")),
        (4, 1): lambda: send(2),
        (4, 2): lambda: close(1),
        (4, 3): lambda: (settle("u2"), gradient(3)),
        (5, 0): lambda: fold(2),
        (5, 1): lambda: (send(3), settle("a0")),
        (5, 2): lambda: cross("a1"),
        (5, 3): lambda: (close(2), gradient(4), fold(3)),
    }

    @pl.loop(0, pairs)
    def _(pair):
        def between(place_at):
            for index in range(pairs):
                if (index, place_at) in plan:
                    @pl.when(pair == index)
                    def _(index=index):
                        plan[index, place_at]()

        attention_columns(
            joined, log_rows, attended_grad, joined_grad, key_bias, key_total, value_total, pair, block, between
        )

    small_own[...] = jnp.zeros_like(small_own)
    take[5].wait()
    take[6].wait()
    after_rows = [
        lambda: (send(4), settle("a1")),
        lambda: (close(3), cross("a2")),
        lambda: fold(4),
        lambda: cross("a3"),
    ]

    @pl.loop(0, rows // 256)
    def _(step):
        at = pl.ds(step * 256, 256)
        grad = mm(joined_grad[at, :], qkv_w[...], NT)
        unit, scale = norm_parts(inputs[at, :].astype(F32) + rows_in[0:1, :])
        total = hidden_grad[at, :] + norm_back(unit, scale, grad, rows_in[1:2, :])
        grad_input[at, :] = total
        small_own[5:6, :] += jnp.sum(grad * unit, axis=0, keepdims=True)
        small_own[0:1, :] += jnp.sum(total, axis=0, keepdims=True)
        pltpu.make_async_copy(grad_input.at[at, :], grad_input_out.at[at, :], saves.at[step]).start()
        for index in range(rows // 256):
            @pl.when(step == index)
            def _(index=index):
                after_rows[index]()

    places = lax.broadcasted_iota(jnp.int32, small_own.shape, 0)
    own = small_own[...]
    table = jnp.where((places == pass_ref[0]) & (places < 5), own[0:1], 0.0)
    own = jnp.where(places == 5, own, table)
    own = jnp.where(places == 6, mlp_gain_grad[0:1], own)
    part = width // shards
    small_parts[...] = jnp.zeros_like(small_parts)
    for shard in range(shards):
        small_parts[shard, :, 0:part] = own[:, shard * part : (shard + 1) * part]
    small_slots[place.me] = small_parts[place.me]
    plane_copies = [
        remote(small_parts.at[other], small_slots.at[place.me], plane_sends, plane_recvs, shift, place.at(other))
        for shift, other in enumerate(others)
    ]
    for copy in plane_copies:
        copy.start()
    close(4)
    settle("a2")
    for copy in plane_copies:
        copy.wait_recv()
    total = small_slots[0]
    for shard in range(1, shards):
        total = total + small_slots[shard]
    small_plane[...] = total
    small_reps[place.z] = total
    rep_copies = [
        remote(small_plane, small_reps.at[place.z], rep_sends, rep_recvs, shift, (place.me, other))
        for shift, other in enumerate(others_z)
    ]
    for copy in rep_copies:
        copy.start()
    settle("a3")
    cross("a4")
    for copy in rep_copies:
        copy.wait_recv()
    total = small_reps[0]
    for rep in range(1, reps):
        total = total + small_reps[rep]
    small_sum[...] = total
    settle("a4")
    for key in lines:
        lines[key].finish()
    for index in range(len(sent)):
        message(index).drain()
    up_late.drain(swapped=False)
    down_late.drain(swapped=False)
    for copy in plane_copies + rep_copies:
        copy.wait_send()
    for step in range(rows // 256):
        at = pl.ds(step * 256, 256)
        pltpu.make_async_copy(grad_input.at[at, :], grad_input_out.at[at, :], saves.at[step]).wait()


def back_comm(reps, seq_lens, pass_idx, rows_in, log_rows, mlp_gain_grad, up_done, down_done, up_half, down_half,
              hidden_grad, out_w, attended, normed, joined, qkv_w, inputs):
    rows, width = inputs.shape
    _, _, up_part, chunk = up_half.shape
    down_part = down_half.shape[2]
    chunks = up_done.shape[0] + 1
    shards = width // up_part
    group = 4 * HEAD_DIM
    count = 1 + width // group
    wide = 3 * group
    vm = lambda *shape: pltpu.VMEM(shape, BF16)
    vf = lambda *shape: pltpu.VMEM(shape, F32)
    return pl.pallas_call(
        functools.partial(back_comm_kernel, 256, 512),
        out_shape=[
            shaped((rows, width), F32), shaped((8, PAIR), F32), shaped((chunks, up_part, chunk), BF16),
            shaped((chunks, down_part, width), BF16), shaped((count, up_part, wide), BF16),
        ],
        in_specs=smem_spec(2) + vmem_spec(7) + any_spec(7),
        out_specs=any_spec(1) + vmem_spec(4),
        scratch_shapes=[
            vf(rows, width), vm(width, width), vm(rows, width), vm(rows, width), vf(rows, width),
            vm(width, 3 * width), vm(rows, 3 * width), vm(rows, width), vm(rows, width), vm(rows, width),
            vm(rows, 3 * width), vm(rows, PAIR), vf(rows, PAIR), vf(rows, PAIR),
        ]
        + scatter_scratch(count, up_part, wide)
        + [
            vm(count, up_part, wide),
            vm(2, up_part // 2, chunk), vm(2, up_part // 2, chunk), vm(up_part, chunk), vm(up_part, chunk),
            vm(2, down_part // 2, width), vm(2, down_part // 2, width), vm(down_part, width), vm(down_part, width),
        ]
        + [vm(chunks, up_part, chunk)] * 3
        + [vm(chunks, down_part, width)] * 3
        + [vm(count, up_part, wide)] * 3
        + [vf(8, width), vf(shards, 8, PAIR), vf(shards, 8, PAIR), vf(8, PAIR), vf(reps, 8, PAIR)]
        + dma((count + 1, 5), (count + 1, 5), (1, 5), (1, 5), (1, 5), (1, 5), (2 * chunks + count + 1, 3),
              (2 * chunks + count + 1, 3),
              (shards - 1,), (shards - 1,), (reps - 1,), (reps - 1,), (7,), (rows // 256,)),
        compiler_params=pltpu.CompilerParams(
            vmem_limit_bytes=VMEM_LIMIT, collective_id=3, has_side_effects=True
        ),
    )(seq_lens, pass_idx, rows_in, log_rows, mlp_gain_grad, up_done, down_done, up_half, down_half,
      hidden_grad, out_w, attended, normed, joined, qkv_w, inputs)


def place_kernel(
    small_sum, outputs_in, grad_input_in, up_in, down_in, attn_in,
    table_out, attn_gain_out, mlp_gain_out, outputs_out, grad_input_out, qkv_out, out_out, up_out, down_out,
    outputs, grad_input, up_total, down_total, attn_total, qkv, out, up, down, loads, saves,
):
    slices, part, chunk = up_in.shape
    width = outputs.shape[1]
    shards = width // part
    lanes = chunk // shards
    take = [
        pltpu.make_async_copy(source, target, loads.at[index])
        for index, (source, target) in enumerate((
            (grad_input_in, grad_input), (up_in, up_total), (attn_in, attn_total), (down_in, down_total),
            (outputs_in, outputs),
        ))
    ]
    give = [
        pltpu.make_async_copy(source, target, saves.at[index])
        for index, (source, target) in enumerate((
            (grad_input, grad_input_out), (up, up_out), (qkv, qkv_out), (out, out_out), (down, down_out),
            (outputs, outputs_out),
        ))
    ]
    for copy in take:
        copy.start()
    table_out[...] = small_sum[0 : table_out.shape[0], 0:part]
    attn_gain_out[...] = small_sum[5:6, 0:part]
    mlp_gain_out[...] = small_sum[6:7, 0:part]
    take[0].wait()
    give[0].start()
    take[1].wait()
    for index in range(slices):
        for shard in range(shards):
            up[:, (slices * shard + index) * lanes : (slices * shard + index + 1) * lanes] = up_total[
                index, :, shard * lanes : (shard + 1) * lanes
            ].astype(F32)
    give[1].start()
    take[2].wait()
    for pair in range(width // PAIR):
        for plane in range(3):
            start = plane * width + pair * PAIR
            source = (3 * (pair % 2) + plane) * PAIR
            qkv[:, start : start + PAIR] = attn_total[1 + pair // 2, :, source : source + PAIR].astype(F32)
    out[...] = attn_total[0].astype(F32)
    give[2].start()
    give[3].start()
    take[3].wait()
    count = down_total.shape[1]
    for index in range(slices):
        down[index * count : (index + 1) * count, :] = down_total[index].astype(F32)
    give[4].start()
    take[4].wait()
    give[5].start()
    for copy in give:
        copy.wait()


def finish_places(passes, small_sum, outputs, grad_input, up_total, down_total, attn_total):
    rows, width = outputs.shape
    slices, part, chunk = up_total.shape
    down_rows = slices * down_total.shape[1]
    vf = lambda *shape: pltpu.VMEM(shape, F32)
    like = lambda ref: pltpu.VMEM(ref.shape, ref.dtype)
    return pl.pallas_call(
        place_kernel,
        out_shape=[
            shaped((passes, part), F32), shaped((1, part), F32), shaped((1, part), F32), shaped((rows, width), BF16),
            shaped((rows, width), F32), shaped((part, 3 * width), F32), shaped((part, width), F32),
            shaped((part, slices * chunk), F32), shaped((down_rows, width), F32),
        ],
        in_specs=vmem_spec(1) + any_spec(5),
        out_specs=vmem_spec(3) + any_spec(6),
        scratch_shapes=[
            like(outputs), like(grad_input), like(up_total), like(down_total), like(attn_total),
            vf(part, 3 * width), vf(part, width), vf(part, slices * chunk), vf(down_rows, width),
        ]
        + dma((5,), (6,)),
        compiler_params=pltpu.CompilerParams(vmem_limit_bytes=VMEM_LIMIT),
    )(small_sum, outputs, grad_input, up_total, down_total, attn_total)


def direct(reps, inputs, seq_lens, pass_idx, pass_table, gain_attn, w_qkv, w_out, gain_mlp, w_up, w_down, cotangent):
    slices = 3
    (
        rows_in, log_rows, mlp_gain_grad, up_half, down_half,
        normed, joined, attended, qkv_w, out_w, outputs, hidden_grad, up_done, down_done,
    ) = fore_comm(
        slices, seq_lens, pass_idx, pass_table, gain_attn[None], gain_mlp[None], inputs[0], cotangent[0], w_qkv, w_out,
        w_up, w_down,
    )
    grad_input, small_sum, up_total, down_total, attn_total = back_comm(
        reps, seq_lens, pass_idx, rows_in, log_rows, mlp_gain_grad, up_done, down_done, up_half, down_half,
        hidden_grad, out_w, attended, normed, joined, qkv_w, inputs[0],
    )
    table, attn_gain, mlp_gain, outputs, grad_input, qkv, out, up, down = finish_places(
        pass_table.shape[0], small_sum, outputs, grad_input, up_total, down_total, attn_total
    )
    return (outputs[None], grad_input[None], table, attn_gain[0], qkv, out, mlp_gain[0], up, down)


def solution(mesh):
    shards, reps = mesh.shape["shard"], mesh.shape["rep"]
    run = functools.partial(direct, reps) if (shards, reps) == (8, 4) else body
    part = P(("shard", "rep"), None, None)
    return jax.shard_map(
        run,
        mesh=mesh,
        in_specs=(
            part, P(("shard", "rep")), P(("shard", "rep")), P(None, "shard"), P("shard"), P("shard", None),
            P("shard", None), P("shard"), P("shard", None), P("shard", None), part,
        ),
        out_specs=(
            part, part, P(None, "shard"), P("shard"), P("shard", None), P("shard", None), P("shard"),
            P("shard", None), P("shard", None),
        ),
        check_vma=False,
    )
```

```python
import functools
import math

import jax
import jax.numpy as jnp
from jax import lax
from jax.experimental import pallas as pl
from jax.experimental.pallas import tpu as pltpu
from jax.sharding import PartitionSpec as P

HEADS = 12
HEAD_DIM = 64
PAIR = 2 * HEAD_DIM
EPSILON = 1e-05
MASKED = -1e30
BF16 = jnp.bfloat16
F32 = jnp.float32
VMEM_LIMIT = 64 * 1024 * 1024 - 65536

NN = (((1,), (0,)), ((), ()))
NT = (((1,), (1,)), ((), ()))
TN = (((0,), (0,)), ((), ()))


def mm(a, b, dims=NN):
    return lax.dot_general(a, b, dims, preferred_element_type=F32)


def norm_parts(values):
    average = jnp.mean(values, axis=-1, keepdims=True)
    centred = values - average
    variance = jnp.mean(centred * centred, axis=-1, keepdims=True)
    scale = lax.rsqrt(variance + EPSILON)
    return centred * scale, scale


def norm_back(unit, scale, grad, gain):
    scaled = grad * gain
    part = scaled - jnp.mean(scaled, axis=-1, keepdims=True)
    return scale * (part - unit * jnp.mean(scaled * unit, axis=-1, keepdims=True))


def lanes_of(shape):
    return lax.broadcasted_iota(jnp.int32, shape, len(shape) - 1)


def head_only(values, head, zero_at=None):
    lanes = lanes_of(values.shape)
    own = (lanes < HEAD_DIM) if head == 0 else (lanes >= HEAD_DIM)
    return jnp.where(own, values, jnp.zeros_like(values)), own, lanes


def query_with_bias(query, head):
    kept, own, lanes = head_only(query * BF16(HEAD_DIM**-0.5), head)
    spot = HEAD_DIM if head == 0 else 0
    return jnp.where(lanes == spot, jnp.ones_like(kept), kept), kept


def key_with_bias(keys, bias, head):
    kept, own, lanes = head_only(keys, head)
    spot = HEAD_DIM if head == 0 else 0
    return jnp.where(lanes == spot, bias, kept), kept


def attention_front(length, joined, attended, log_sums, key_bias, pair, block):
    rows = attended.shape[0]
    width = attended.shape[1]
    at = pl.multiple_of(pair * PAIR, PAIR)
    keys = joined[:, pl.ds(width + at, PAIR)]
    values = joined[:, pl.ds(2 * width + at, PAIR)]
    bias = key_bias[...]
    biased = [key_with_bias(keys, bias, head)[0] for head in range(2)]
    for first in range(0, rows, block):
        live = first + block
        query = joined[pl.ds(first, block), pl.ds(at, PAIR)]
        mixed = []
        sums = []
        for head in range(2):
            asked, _ = query_with_bias(query, head)
            scores = mm(asked, biased[head][:live], NT)
            row_at = lax.broadcasted_iota(jnp.int32, (block, block), 0)
            key_at = lax.broadcasted_iota(jnp.int32, (block, block), 1)
            last = jnp.where(key_at <= row_at, scores[:, first:], MASKED)
            scores = last if first == 0 else jnp.concatenate([scores[:, :first], last], axis=1)
            top = jnp.max(scores, axis=-1, keepdims=True)
            weights = jnp.exp(scores - top)
            total = jnp.sum(weights, axis=-1, keepdims=True)
            mixed.append(mm(weights.astype(BF16), values[:live]) / total)
            sums.append(top + jnp.log(total))
        lanes = lanes_of(mixed[0].shape)
        attended[pl.ds(first, block), pl.ds(at, PAIR)] = jnp.where(
            lanes < HEAD_DIM, mixed[0], mixed[1]
        ).astype(BF16)
        log_sums[pair, pl.ds(first, block), :] = jnp.where(lanes < HEAD_DIM, sums[0], sums[1])


def fill_bias(length, key_bias):
    rows = key_bias.shape[0]
    places = lax.broadcasted_iota(jnp.int32, key_bias.shape, 0)
    key_bias[...] = jnp.where(places < length, 0.0, MASKED).astype(BF16)


def front_kernel(
    block, tile, length_ref, inputs, pass_row, gain, w_qkv, w_out,
    joined_out, attended_out, sums_out, hidden_out, normed, key_bias,
):
    rows, width = inputs.shape
    length = length_ref[0]
    fill_bias(length, key_bias)

    @pl.loop(0, rows // 256)
    def _(step):
        at = pl.ds(step * 256, 256)
        entered = inputs[at, :].astype(F32) + pass_row[0:1, :]
        normed[at, :] = (norm_parts(entered)[0] * gain[0:1, :]).astype(BF16)

    @pl.loop(0, 3)
    def _(part):
        columns = pl.ds(pl.multiple_of(part * width, width), width)

        @pl.loop(0, rows // tile)
        def _(step):
            at = pl.ds(step * tile, tile)
            joined_out[at, columns] = mm(normed[at, :], w_qkv[:, columns]).astype(BF16)

    @pl.loop(0, HEADS // 2)
    def _(pair):
        attention_front(length, joined_out, attended_out, sums_out, key_bias, pair, block)

    @pl.loop(0, rows // tile)
    def _(step):
        at = pl.ds(step * tile, tile)
        entered = inputs[at, :].astype(F32) + pass_row[0:1, :]
        hidden_out[at, :] = entered + mm(attended_out[at, :], w_out[...])


def gelu_both(values):
    outer = math.sqrt(2.0 / math.pi)
    square = values * values
    bent = jnp.tanh(outer * values * (1.0 + 0.044715 * square))
    half = 0.5 * (1.0 + bent)
    slope = half + 0.5 * values * (1.0 - bent * bent) * (outer * (1.0 + 3 * 0.044715 * square))
    return values * half, slope


def mlp_kernel(
    tile, chunk, hidden, cotangent, gain, w_up, w_down,
    outputs, hidden_grad, gain_grad, up_grad, down_grad,
    second, mixed, second_grad, active, rising_grad,
):
    rows, width = hidden.shape
    chunks = w_down.shape[0] // chunk

    @pl.loop(0, rows // 256)
    def _(step):
        at = pl.ds(step * 256, 256)
        second[at, :] = (norm_parts(hidden[at, :])[0] * gain[0:1, :]).astype(BF16)
        mixed[at, :] = hidden[at, :]
        second_grad[at, :] = jnp.zeros((256, width), F32)

    @pl.loop(0, chunks)
    def _(part):
        units = pl.ds(pl.multiple_of(part * chunk, chunk), chunk)

        @pl.loop(0, rows // tile)
        def _(step):
            at = pl.ds(step * tile, tile)
            rising = mm(second[at, :], w_up[:, units])
            active_grad = mm(cotangent[at, :], w_down[units, :], NT)
            bent, slope = gelu_both(rising)
            shown = bent.astype(BF16)
            moved = (slope * active_grad).astype(BF16)
            active[at, :] = shown
            rising_grad[at, :] = moved
            mixed[at, :] += mm(shown, w_down[units, :])
            second_grad[at, :] += mm(moved, w_up[:, units], NT)

        down_grad[units, :] = mm(active[...], cotangent[...], TN).astype(BF16)
        up_grad[:, units] = mm(second[...], rising_grad[...], TN).astype(BF16)

    gain_grad[...] = jnp.zeros_like(gain_grad)

    @pl.loop(0, rows // 256)
    def _(step):
        at = pl.ds(step * 256, 256)
        outputs[at, :] = mixed[at, :].astype(BF16)
        unit, scale = norm_parts(hidden[at, :])
        grad = second_grad[at, :]
        hidden_grad[at, :] = cotangent[at, :].astype(F32) + norm_back(unit, scale, grad, gain[0:1, :])
        gain_grad[0:1, :] += jnp.sum(grad * unit, axis=0, keepdims=True)


def attention_back(joined, log_rows, grads, joined_grad, key_bias, key_total, value_total, pair, block):
    rows = grads.shape[0]
    width = grads.shape[1]
    at = pl.multiple_of(pair * PAIR, PAIR)
    keys = joined[:, pl.ds(width + at, PAIR)]
    values = joined[:, pl.ds(2 * width + at, PAIR)]
    bias = key_bias[...]
    biased = [key_with_bias(keys, bias, head) for head in range(2)]
    key_total[...] = jnp.zeros_like(key_total)
    value_total[...] = jnp.zeros_like(value_total)
    for first in range(0, rows, block):
        live = first + block
        query = joined[pl.ds(first, block), pl.ds(at, PAIR)]
        grad = grads[pl.ds(first, block), pl.ds(at, PAIR)]
        query_grad = None
        for head in range(2):
            asked, asked_only = query_with_bias(query, head)
            grad_only = head_only(grad, head)[0]
            scores = mm(biased[head][0][:live], asked, NT)
            share_grad = mm(values[:live], grad_only, NT)
            log_sum = log_rows[pl.ds(pair * 2 + head, 1), pl.ds(first, block)]
            shares = jnp.exp(scores - log_sum)
            key_at = lax.broadcasted_iota(jnp.int32, (block, block), 0)
            row_at = lax.broadcasted_iota(jnp.int32, (block, block), 1)
            last = jnp.where(key_at <= row_at, shares[first:], 0.0)
            shares = last if first == 0 else jnp.concatenate([shares[:first], last], axis=0)
            inner = jnp.sum(share_grad * shares, axis=0, keepdims=True)
            score_grad = (shares * (share_grad - inner)).astype(BF16)
            value_total[:live, :] += mm(shares.astype(BF16), grad_only)
            key_total[:live, :] += mm(score_grad, asked_only)
            part = mm(score_grad, biased[head][1][:live], TN)
            query_grad = part if query_grad is None else query_grad + part
        joined_grad[pl.ds(first, block), pl.ds(at, PAIR)] = (
            query_grad * HEAD_DIM**-0.5
        ).astype(BF16)
    joined_grad[:, pl.ds(width + at, PAIR)] = key_total[...].astype(BF16)
    joined_grad[:, pl.ds(2 * width + at, PAIR)] = value_total[...].astype(BF16)


def back_kernel(
    block, tile, length_ref, inputs, pass_row, gain, w_qkv, w_out, joined, log_rows, attended, hidden_grad,
    grad_input, gain_grad, table_grad, qkv_grad, out_grad,
    branch_grad, attended_grad, normed, joined_grad, key_bias, key_total, value_total,
):
    rows, width = inputs.shape
    length = length_ref[0]
    fill_bias(length, key_bias)

    @pl.loop(0, rows // 256)
    def _(step):
        at = pl.ds(step * 256, 256)
        branch_grad[at, :] = hidden_grad[at, :].astype(BF16)
        entered = inputs[at, :].astype(F32) + pass_row[0:1, :]
        normed[at, :] = (norm_parts(entered)[0] * gain[0:1, :]).astype(BF16)

    @pl.loop(0, rows // tile)
    def _(step):
        at = pl.ds(step * tile, tile)
        attended_grad[at, :] = mm(branch_grad[at, :], w_out[...], NT).astype(BF16)

    out_grad[...] = mm(attended[...], branch_grad[...], TN).astype(BF16)

    @pl.loop(0, HEADS // 2)
    def _(pair):
        attention_back(
            joined, log_rows, attended_grad, joined_grad, key_bias, key_total, value_total, pair, block
        )

    @pl.loop(0, 3)
    def _(part):
        columns = pl.ds(pl.multiple_of(part * width, width), width)
        qkv_grad[:, columns] = mm(normed[...], joined_grad[:, columns], TN).astype(BF16)

    gain_grad[...] = jnp.zeros_like(gain_grad)
    table_grad[...] = jnp.zeros_like(table_grad)

    @pl.loop(0, rows // 256)
    def _(step):
        at = pl.ds(step * 256, 256)
        grad = mm(joined_grad[at, :], w_qkv[...], NT)
        unit, scale = norm_parts(inputs[at, :].astype(F32) + pass_row[0:1, :])
        total = hidden_grad[at, :] + norm_back(unit, scale, grad, gain[0:1, :])
        grad_input[at, :] = total
        gain_grad[0:1, :] += jnp.sum(grad * unit, axis=0, keepdims=True)
        table_grad[0:1, :] += jnp.sum(total, axis=0, keepdims=True)


def whole(count):
    return [pl.BlockSpec(memory_space=pltpu.VMEM)] * count


def call(kernel, outs, scratch, *args, scalars=0):
    specs = [pl.BlockSpec(memory_space=pltpu.SMEM)] * scalars + whole(len(args) - scalars)
    return pl.pallas_call(
        kernel,
        out_shape=[jax.ShapeDtypeStruct(shape, kind) for shape, kind in outs],
        in_specs=specs,
        out_specs=whole(len(outs)),
        scratch_shapes=[pltpu.VMEM(shape, kind) for shape, kind in scratch],
        compiler_params=pltpu.CompilerParams(vmem_limit_bytes=VMEM_LIMIT),
    )(*args)


def body(
    inputs, seq_lens, pass_idx, pass_table, gain_attn, w_qkv, w_out, gain_mlp, w_up, w_down, cotangent,
):
    _, rows, width = inputs.shape
    inputs2 = inputs[0]
    out_cot = cotangent[0]
    gather = functools.partial(lax.all_gather, axis_name="shard", tiled=True)
    table = gather(pass_table, axis=1)
    attn_gain = jnp.broadcast_to(gather(gain_attn, axis=0).astype(F32)[None, :], (8, width))
    mlp_gain = jnp.broadcast_to(gather(gain_mlp, axis=0).astype(F32)[None, :], (8, width))
    qkv_w = gather(w_qkv, axis=0)
    out_w = gather(w_out, axis=0)
    up_w = gather(w_up, axis=0)
    down_w = gather(w_down, axis=0)
    chosen = (pass_idx[:, None] == jnp.arange(table.shape[0], dtype=jnp.int32)[None, :]).astype(F32)
    pass_row = jnp.broadcast_to(
        jnp.sum(chosen[0][:, None] * table.astype(F32), axis=0, keepdims=True), (8, width)
    )
    block = 256
    tile = 512
    joined, attended, sums, hidden = call(
        functools.partial(front_kernel, block, tile),
        [((rows, 3 * width), BF16), ((rows, width), BF16), ((HEADS // 2, rows, PAIR), F32), ((rows, width), F32)],
        [((rows, width), BF16), ((rows, PAIR), BF16)],
        seq_lens, inputs2, pass_row, attn_gain, qkv_w, out_w, scalars=1,
    )
    chunk = 1024
    outputs, hidden_grad, mlp_gain_grad, up_grad, down_grad = call(
        functools.partial(mlp_kernel, tile, chunk),
        [((rows, width), BF16), ((rows, width), F32), ((8, width), F32), (up_w.shape, BF16), (down_w.shape, BF16)],
        [((rows, width), BF16), ((rows, width), F32), ((rows, width), F32), ((rows, chunk), BF16), ((rows, chunk), BF16)],
        hidden, out_cot, mlp_gain, up_w, down_w,
    )
    log_rows = jnp.stack([sums[:, :, 0], sums[:, :, HEAD_DIM]], axis=1).reshape(HEADS, rows)
    grad_input, attn_gain_grad, table_row, qkv_grad, out_grad = call(
        functools.partial(back_kernel, block, tile),
        [((rows, width), F32), ((8, width), F32), ((8, width), F32), (qkv_w.shape, BF16), (out_w.shape, BF16)],
        [((rows, width), BF16), ((rows, width), BF16), ((rows, width), BF16), ((rows, 3 * width), BF16),
         ((rows, PAIR), BF16), ((rows, PAIR), F32), ((rows, PAIR), F32)],
        seq_lens, inputs2, pass_row, attn_gain, qkv_w, out_w, joined, log_rows, attended, hidden_grad, scalars=1,
    )
    scatter = lambda grad, dim=0: lax.psum_scatter(grad, "shard", scatter_dimension=dim, tiled=True)
    up_part, down_part = scatter(up_grad), scatter(down_grad)
    out_part, qkv_part = scatter(out_grad), scatter(qkv_grad)
    small = jnp.concatenate(
        [chosen[0][:, None] * table_row[0:1], attn_gain_grad[0:1], mlp_gain_grad[0:1]], axis=0
    )
    small = lax.psum(scatter(small, 1), "rep")
    up_sum, down_sum, out_sum, qkv_sum = lax.psum((up_part, down_part, out_part, qkv_part), "rep")
    count = table.shape[0]
    return (
        outputs[None], grad_input[None], small[:count], small[count], qkv_sum.astype(F32), out_sum.astype(F32),
        small[count + 1], up_sum.astype(F32), down_sum.astype(F32),
    )


MESH = pl.DeviceIdType.MESH


class Place:
    def __init__(self):
        self.me = lax.axis_index("shard")
        self.z = lax.axis_index("rep")
        self.core = lax.rem(self.me, 2)
        self.x = lax.rem(self.me // 2, 2)
        self.y = self.me // 4
        self.by_x = self.me + 2 - 4 * self.x
        self.by_y = self.me + 4 - 8 * self.y
        self.by_core = self.me + 1 - 2 * self.core
        self.by_both = self.by_x + 4 - 8 * self.y
        self.side = lax.rem(self.z, 2)
        self.by_z = self.z + 1 - 2 * self.side

    def at(self, shard):
        return (shard, self.z)


def remote(src, dst, sends, recvs, index, device):
    return pltpu.make_async_remote_copy(
        src_ref=src, dst_ref=dst, send_sem=sends.at[index], recv_sem=recvs.at[index],
        device_id=device, device_id_type=MESH,
    )


class Gather:
    def __init__(self, place, part, fills, sends, recvs, local, row, shared):
        self.place, self.part, self.fills, self.shared = place, part, fills, shared
        self.sends, self.recvs, self.local, self.row = sends, recvs, local, row
        self.slots = 17 if shared else 9

    def piece(self, shard, columns=None, other=False):
        if not self.shared:
            return self.part(shard, None, columns)
        side = 1 - self.place.side if other else self.place.side
        return self.part(shard, side, columns)

    def make(self, slot):
        p = self.place
        rep = p.z
        if slot < 2:
            ref, shard = self.piece(p.me), (p.by_x, p.by_y)[slot]
        elif slot == 2:
            ref, shard = self.part(p.me, None, None), p.by_core
        elif slot == 3:
            ref, shard = self.piece(p.by_x, 0), p.by_y
        elif slot == 4:
            ref, shard = self.piece(p.by_y, 1), p.by_x
        else:
            kind = (slot - 5) % 4
            source = (p.by_x, p.by_y, p.by_both, p.by_both)[kind]
            ref = self.piece(source, None if kind < 2 else kind - 2, slot >= 13)
            shard = p.by_core
            if 9 <= slot < 13:
                shard, rep = p.me, p.by_z
        return remote(ref, ref, self.sends, self.recvs, (self.row, slot), (shard, rep))

    def fill(self):
        for source, target in self.fills:
            pltpu.make_async_copy(source, target, self.local.at[self.row]).start()

    def start(self):
        own = self.part(self.place.me, None, None)
        pltpu.make_async_copy(own, own, self.local.at[self.row]).wait()
        for slot in range(3):
            self.make(slot).start()

    def pass_on(self, slot, *targets):
        self.make(slot).wait_recv()
        for target in targets:
            if target < self.slots:
                self.make(target).start()

    def relay(self):
        self.pass_on(0, 3, 5, 9)
        self.pass_on(1, 4, 6, 10)

    def finish(self):
        self.pass_on(3, 7, 11)
        self.pass_on(4, 8, 12)

    def across(self):
        if self.shared:
            for slot in range(9, 13):
                self.pass_on(slot, slot + 4)

    def ready(self):
        for slot in (2, 5, 6, 7, 8) + ((13, 14, 15, 16) if self.shared else ()):
            self.make(slot).wait_recv()

    def drain(self):
        for slot in range(self.slots):
            self.make(slot).wait_send()


def enter(place, shards, reps=()):
    barrier = pltpu.get_barrier_semaphore()
    for shard in shards:
        pl.semaphore_signal(barrier, inc=1, device_id=(shard, place.z), device_id_type=MESH)
    for rep in reps:
        pl.semaphore_signal(barrier, inc=1, device_id=(place.me, rep), device_id_type=MESH)
    pl.semaphore_wait(barrier, len(shards) + len(reps))


def part_of(ref, rows, lead, start, width):
    def part(shard, side, half):
        count, first, left, wide = rows, shard * rows, start, width
        if side is None and half is not None:
            side, half = half, None
        if side is not None:
            count = rows // 2
            first = first + side * count
        if half is not None:
            wide = width // 2
            left = start + half * wide
        return ref.at[lead + (pl.ds(pl.multiple_of(first, count), count), pl.ds(left, wide))]

    return part


def up_fills(own, ref, index, place, shards):
    part, chunk = own.shape[0], ref.shape[2]
    lanes = chunk // shards
    slices = own.shape[1] // chunk
    rows = pl.ds(pl.multiple_of(place.me * part, part), part)
    return [
        (own.at[:, pl.ds((slices * shard + index) * lanes, lanes)], ref.at[index, rows, pl.ds(shard * lanes, lanes)])
        for shard in range(shards)
    ]


def down_fills(own, ref, index, place, shards):
    count = ref.shape[1] // shards
    rows = pl.ds(pl.multiple_of(place.me * count, count), count)
    return [(own.at[pl.ds(index * count, count), :], ref.at[index, rows, :])]


def pair_columns(pair):
    return [pl.ds(pl.multiple_of((3 * pair + plane) * PAIR, PAIR), PAIR) for plane in range(3)]


def attention_rows(joined, attended, log_rows, key_bias, pair, block, between):
    rows = attended.shape[0]
    columns = pl.ds(pl.multiple_of(pair * PAIR, PAIR), PAIR)
    query_columns, key_columns, value_columns = pair_columns(pair)
    keys = joined[:, key_columns]
    values = joined[:, value_columns]
    bias = key_bias[...]
    biased = [key_with_bias(keys, bias, head)[0] for head in range(2)]
    for first in range(0, rows, block):
        live = first + block
        query = joined[pl.ds(first, block), query_columns]
        mixed = []
        sums = []
        for head in range(2):
            asked, _ = query_with_bias(query, head)
            scores = mm(asked, biased[head][:live], NT)
            row_at = lax.broadcasted_iota(jnp.int32, (block, block), 0)
            key_at = lax.broadcasted_iota(jnp.int32, (block, block), 1)
            last = jnp.where(key_at <= row_at, scores[:, first:], MASKED)
            scores = last if first == 0 else jnp.concatenate([scores[:, :first], last], axis=1)
            top = jnp.max(scores, axis=-1, keepdims=True)
            weights = jnp.exp(scores - top)
            total = jnp.sum(weights, axis=-1, keepdims=True)
            mixed.append(mm(weights.astype(BF16), values[:live]) / total)
            sums.append(top + jnp.log(total))
        lanes = lanes_of(mixed[0].shape)
        attended[pl.ds(first, block), columns] = jnp.where(lanes < HEAD_DIM, mixed[0], mixed[1]).astype(BF16)
        turned = jnp.transpose(jnp.where(lanes < HEAD_DIM, sums[0], sums[1]))
        log_rows[pl.ds(pair * 2, 1), pl.ds(first, block)] = turned[0:1]
        log_rows[pl.ds(pair * 2 + 1, 1), pl.ds(first, block)] = turned[HEAD_DIM : HEAD_DIM + 1]
        between(first // block)


def norm_rows(inputs, pass_row, gain, normed):
    @pl.loop(0, inputs.shape[0] // 256)
    def _(step):
        at = pl.ds(step * 256, 256)
        entered = inputs[at, :].astype(F32) + pass_row
        normed[at, :] = (norm_parts(entered)[0] * gain).astype(BF16)


SHARED = (False, False, True, True, False, True, True, False, True, True, False)
SPANS = ((0, 1), (1, 1), (2, 2), (4, 2))

PLAN = {
    "begin": "r0 s2",
    "normed": "f0 r1",
    (0, 0): "r2 s3",
    (0, 1): "f1",
    (0, 3): "f2 s4",
    (1, 1): "r3",
    (1, 2): "a2",
    (1, 3): "s5",
    (2, 0): "f3 r4",
    (2, 2): "s6",
    (2, 3): "r5",
    (3, 1): "a3 f4",
    (3, 2): "s7",
    (4, 0): "f5 r6",
    (4, 3): "s8",
    (5, 1): "a5 r7 f6",
    (5, 3): "s9",
    "row 0": "r8",
    "row 1": "a6 f7 s10",
    "mlp 0 0": "f8 r9",
    "mlp 0 1": "r10",
    "mlp 0 down": "a8 f9",
    "mlp 1 0": "a9 f10",
}


def fore_comm_kernel(
    block, tile, slices,
    length_ref, pass_ref, table_own, attn_gain_own, mlp_gain_own,
    inputs_in, cotangent_in, qkv_own, out_own, up_own, down_own,
    rows_out, log_out, gain_grad,
    up_half, down_half, normed_out, joined_out, attended_out, qkv_out, out_out, outputs_out, hidden_grad_out,
    up_done_out, down_done_out,
    inputs, cotangent, slots, small_wide, small_own, normed, joined, attended, hidden, qkv_w, out_w, up_w, down_w,
    key_bias, mixed, hidden_grad, up_done, down_done,
    up_grads, up_first, up_x, up_y, up_last, down_grads, down_first, down_x, down_y, down_last,
    sends, recvs, local, small_sends, small_recvs, up_sends, up_recvs, down_sends, down_recvs, loads, saves,
):
    place = Place()
    rows, width = inputs.shape
    shards = slots.shape[0]
    part = qkv_own.shape[0]
    groups = len(SPANS)
    pairs = width // PAIR

    pieces = []

    def add(part_at, fills):
        row = len(pieces)
        pieces.append(Gather(place, part_at, fills, sends, recvs, local, row, SHARED[row]))

    own_rows = pl.ds(pl.multiple_of(place.me * part, part), part)
    for start, number in SPANS:
        fills = [
            (qkv_own.at[:, pl.ds(plane * width + pair * PAIR, PAIR)], qkv_w.at[own_rows, columns])
            for pair in range(start, start + number)
            for plane, columns in enumerate(pair_columns(pair))
        ]
        add(part_of(qkv_w, part, (), start * 3 * PAIR, number * 3 * PAIR), fills)
    add(part_of(out_w, part, (), 0, width), [(out_own, out_w.at[own_rows, :])])
    for index in range(slices):
        add(part_of(up_w, part, (index,), 0, up_w.shape[2]), up_fills(up_own, up_w, index, place, shards))
        add(part_of(down_w, down_w.shape[1] // shards, (index,), 0, width),
            down_fills(down_own, down_w, index, place, shards))
    count = len(pieces)
    take = [
        pltpu.make_async_copy(inputs_in, inputs, loads.at[0]), pltpu.make_async_copy(cotangent_in, cotangent, loads.at[1]),
    ]
    pieces[0].fill()
    take[0].start()
    for piece in pieces[1:]:
        piece.fill()
    take[1].start()

    small_wide[...] = jnp.zeros_like(small_wide)
    small_wide[0 : table_own.shape[0], 0:part] = table_own[...].astype(F32)
    small_wide[8:9, 0:part] = attn_gain_own[...].astype(F32)
    small_wide[9:10, 0:part] = mlp_gain_own[...].astype(F32)
    small_own[...] = small_wide[...].astype(BF16)
    slots[place.me] = small_own[...]

    others = [lax.rem(place.me + shift, shards) for shift in range(1, shards)]
    enter(place, others, [place.by_z])
    smalls = [
        remote(small_own, slots.at[place.me], small_sends, small_recvs, shift, place.at(other))
        for shift, other in enumerate(others)
    ]
    for copy in smalls:
        copy.start()
    pieces[0].start()
    pieces[1].start()

    def step_on(point):
        for what in PLAN.get(point, "").split():
            piece = pieces[int(what[1:])]
            {"s": piece.start, "r": piece.relay, "f": piece.finish, "a": piece.across}[what[0]]()

    def up_message(index):
        return Scatter(
            place, up_grads.at[lax.rem(index, 2)], up_first.at[index], up_x.at[index], up_y.at[index], up_last.at[index],
            up_sends, up_recvs, index,
        )

    def down_message(index):
        return Scatter(
            place, down_grads.at[lax.rem(index, 2)], down_first.at[index], down_x.at[index], down_y.at[index], down_last.at[index],
            down_sends, down_recvs, index,
        )

    fill_bias(length_ref[0], key_bias)
    for copy in smalls:
        copy.wait_recv()
    total = jnp.concatenate([slots[shard].astype(F32)[:, 0:part] for shard in range(shards)], axis=1)
    places = lax.broadcasted_iota(jnp.int32, total.shape, 0)
    rows_out[0:1, :] = jnp.sum(jnp.where(places == pass_ref[0], total, 0.0), axis=0, keepdims=True)
    rows_out[1:3, :] = total[8:10]
    rows_out[3:8, :] = jnp.zeros((5, width), F32)

    take[0].wait()
    step_on("begin")
    norm_rows(inputs, rows_out[0:1, :], rows_out[1:2, :], normed)
    step_on("normed")

    keep = {}

    def save(source, target, name=None):
        keep[name or len(keep)] = copy = pltpu.make_async_copy(source, target, saves.at[len(keep)])
        return copy

    save(normed, normed_out, "normed").start()
    qkv_save = save(qkv_w, qkv_out)

    @pl.loop(0, pairs)
    def _(pair):
        for index, (start, number) in enumerate(SPANS):
            @pl.when(pair == start)
            def _(index=index, start=start, number=number):
                pieces[index].ready()
                if index == groups - 1:
                    qkv_save.start()
                columns = pl.ds(start * 3 * PAIR, number * 3 * PAIR)

                @pl.loop(0, rows // tile)
                def _(step):
                    at = pl.ds(step * tile, tile)
                    joined[at, columns] = mm(normed[at, :], qkv_w[:, columns]).astype(BF16)

        def between(place_at):
            for index in range(pairs):
                if (index, place_at) in PLAN:
                    @pl.when(pair == index)
                    def _(index=index):
                        step_on((index, place_at))

        attention_rows(joined, attended, log_out, key_bias, pair, block, between)

    chunk = up_w.shape[2]
    second = attended
    active, rising_grad = joined.at[:, pl.ds(0, chunk)], joined.at[:, pl.ds(chunk, chunk)]
    save(attended, attended_out, "attended").start()
    save(joined, joined_out, "joined").start()
    pieces[groups].ready()
    save(out_w, out_out).start()
    gain = rows_out[2:3, :]
    for step in range(rows // tile):
        at = pl.ds(step * tile, tile)
        entered = inputs[at, :].astype(F32) + rows_out[0:1, :]
        hidden[at, :] = entered + mm(attended[at, :], out_w[...])
        step_on("row %d" % step)
        if step == 0:
            keep["attended"].wait()

        @pl.loop(0, tile // 256)
        def _(step_in):
            at = pl.ds(step * tile + step_in * 256, 256)
            values = hidden[at, :]
            second[at, :] = (norm_parts(values)[0] * gain).astype(BF16)
            mixed[at, :] = values
            hidden_grad[at, :] = jnp.zeros((256, width), F32)

    take[1].wait()
    keep["joined"].wait()

    @pl.loop(0, slices)
    def _(index_at):
        for index in range(slices):
            @pl.when(index_at == index)
            def _(index=index):
                pieces[groups + 1 + 2 * index].ready()
                pieces[groups + 2 + 2 * index].ready()

        @pl.loop(0, rows // tile)
        def _(step):
            at = pl.ds(step * tile, tile)
            rising = mm(second[at, :], up_w[index_at])
            active_grad = mm(cotangent[at, :], down_w[index_at], NT)
            bent, slope = gelu_both(rising)
            shown = bent.astype(BF16)
            moved = (slope * active_grad).astype(BF16)
            active[at, :] = shown
            rising_grad[at, :] = moved
            mixed[at, :] += mm(shown, down_w[index_at])
            hidden_grad[at, :] += mm(moved, up_w[index_at], NT)

            for index in range(slices):
                for inner in range(rows // tile):
                    if "mlp %d %d" % (index, inner) in PLAN:
                        @pl.when((index_at == index) & (step == inner))
                        def _(index=index, inner=inner):
                            step_on("mlp %d %d" % (index, inner))

            @pl.when((index_at > 0) & (step == 0))
            def _():
                message = up_message(index_at - 1)
                message.merge()
                message.spread()

            @pl.when((index_at > 0) & (step == 1))
            def _():
                down_message(index_at - 1).fold()

        @pl.when(index_at > 1)
        def _():
            down_message(index_at - 2).swap_copy().wait_send()
            up_message(index_at - 2).swap_copy().wait_send()

        slot = lax.rem(index_at, 2)
        down_grads[slot] = mm(active[...], cotangent[...], TN).astype(BF16).reshape(down_grads.shape[1:])
        down_message(index_at).swap()

        @pl.when(index_at == 0)
        def _():
            step_on("mlp 0 down")

        @pl.when(index_at > 0)
        def _():
            up_message(index_at - 1).fold()

        up_grads[slot] = mm(second[...], rising_grad[...], TN).astype(BF16).reshape(up_grads.shape[1:])
        up_message(index_at).swap()

        @pl.when(index_at == 0)
        def _():
            step_on("mlp 0 up")

        @pl.when(index_at < slices - 1)
        def _():
            message = down_message(index_at)
            message.merge()
            message.spread()

        @pl.when(index_at > 0)
        def _():
            down_message(index_at - 1).close(down_done.at[index_at - 1])
            up_message(index_at - 1).close(up_done.at[index_at - 1])

    down_message(slices - 1).merge()
    save(down_first.at[slices - 1], down_half).start()
    save(up_done, up_done_out).start()
    save(down_done, down_done_out).start()
    gain_grad[...] = jnp.zeros_like(gain_grad)
    keep["normed"].wait()
    first_row = len(keep) + 2

    @pl.loop(0, rows // 256)
    def _(step):
        at = pl.ds(step * 256, 256)
        normed[at, :] = mixed[at, :].astype(BF16)
        unit, scale = norm_parts(hidden[at, :])
        grad = hidden_grad[at, :]
        hidden_grad[at, :] = cotangent[at, :].astype(F32) + norm_back(unit, scale, grad, gain)
        gain_grad[0:1, :] += jnp.sum(grad * unit, axis=0, keepdims=True)
        pltpu.make_async_copy(hidden_grad.at[at, :], hidden_grad_out.at[at, :], saves.at[first_row + step]).start()

    save(normed, outputs_out).start()
    up_message(slices - 1).merge()
    save(up_first.at[slices - 1], up_half).start()
    for step in range(rows // 256):
        at = pl.ds(step * 256, 256)
        pltpu.make_async_copy(hidden_grad.at[at, :], hidden_grad_out.at[at, :], saves.at[first_row + step]).wait()
    for piece in pieces:
        piece.drain()
    for copy in smalls:
        copy.wait_send()
    for index in range(slices):
        up_message(index).drain(index >= slices - 2, index < slices - 1)
        down_message(index).drain(index >= slices - 2, index < slices - 1)
    for name, copy in keep.items():
        if name not in ("normed", "attended", "joined"):
            copy.wait()


def any_spec(count):
    return [pl.BlockSpec(memory_space=pl.ANY)] * count


def smem_spec(count):
    return [pl.BlockSpec(memory_space=pltpu.SMEM)] * count


def vmem_spec(count):
    return [pl.BlockSpec(memory_space=pltpu.VMEM)] * count


def shaped(shape, kind):
    return jax.ShapeDtypeStruct(shape, kind)


class Scatter:
    def __init__(self, place, grads, first, by_x, by_y, last, sends, recvs, row):
        self.place, self.grads, self.first = place, grads, first
        self.in_x, self.in_y, self.last = by_x, by_y, last
        self.sends, self.recvs, self.row = sends, recvs, row
        half = first.shape[-2] // 2
        self.upper, self.lower = pl.ds(0, half), pl.ds(half, half)

    def copy(self, slot, src, dst, shard):
        return remote(src, dst, self.sends, self.recvs, (self.row, slot), self.place.at(shard))

    def swap_copy(self):
        p = self.place
        return self.copy(0, self.grads.at[:, :, 1 - p.core], self.first, p.by_core)

    def spread_copies(self):
        p = self.place
        return [
            self.copy(1, self.first.at[:, 1 - p.x, self.upper], self.in_x, p.by_x),
            self.copy(2, self.first.at[1 - p.y, :, self.lower], self.in_y, p.by_y),
        ]

    def fold_copies(self):
        p = self.place
        return [
            self.copy(3, self.in_x.at[1 - p.y], self.last.at[self.upper], p.by_y),
            self.copy(4, self.in_y.at[1 - p.x], self.last.at[self.lower], p.by_x),
        ]

    def swap(self):
        self.swap_copy().start()

    def merge(self, target=None):
        p = self.place
        target = self.first if target is None else target
        self.swap_copy().wait_recv()
        for y in range(2):
            for x in range(2):
                total = self.grads[y, x, p.core].astype(F32) + self.first[y, x].astype(F32)
                target[y, x] = total.astype(BF16)

    def spread(self):
        for copy in self.spread_copies():
            copy.start()

    def fold(self):
        p = self.place
        for copy in self.spread_copies():
            copy.wait_recv()
        for other in range(2):
            total = self.first[other, p.x, self.upper].astype(F32) + self.in_x[other].astype(F32)
            self.in_x[other] = total.astype(BF16)
            total = self.first[p.y, other, self.lower].astype(F32) + self.in_y[other].astype(F32)
            self.in_y[other] = total.astype(BF16)
        for copy in self.fold_copies():
            copy.start()

    def close(self, target):
        p = self.place
        for copy in self.fold_copies():
            copy.wait_recv()
        target[self.upper] = (self.last[self.upper].astype(F32) + self.in_x[p.y].astype(F32)).astype(BF16)
        target[self.lower] = (self.last[self.lower].astype(F32) + self.in_y[p.x].astype(F32)).astype(BF16)

    def drain(self, swapped=True, spread=True):
        if swapped:
            self.swap_copy().wait_send()
        if spread:
            for copy in self.spread_copies() + self.fold_copies():
                copy.wait_send()


def scatter_scratch(count, part, columns, slots=None):
    return [
        pltpu.VMEM((slots or count, 2, 2, 2, part, columns), BF16), pltpu.VMEM((count, 2, 2, part, columns), BF16),
        pltpu.VMEM((count, 2, part // 2, columns), BF16), pltpu.VMEM((count, 2, part // 2, columns), BF16),
        pltpu.VMEM((count, part, columns), BF16),
    ]


def dma(*shapes):
    return [pltpu.SemaphoreType.DMA(shape) for shape in shapes]


def fore_comm(slices, seq_lens, pass_idx, table, attn_gain, mlp_gain, inputs, cotangent, qkv, out, up, down):
    rows, width = inputs.shape
    up_part, chunk = up.shape[0], up.shape[1] // slices
    down_part = down.shape[0] // slices
    shards = width // up_part
    count = len(SPANS) + 1 + 2 * slices
    vm = lambda *shape: pltpu.VMEM(shape, BF16)
    vf = lambda *shape: pltpu.VMEM(shape, F32)
    return pl.pallas_call(
        functools.partial(fore_comm_kernel, 256, 512, slices),
        out_shape=[
            shaped((8, width), F32), shaped((16, rows), F32), shaped((8, width), F32),
            shaped((2, 2, up_part, chunk), BF16), shaped((2, 2, down_part, width), BF16),
            shaped((rows, width), BF16), shaped((rows, 3 * width), BF16), shaped((rows, width), BF16),
            shaped((width, 3 * width), BF16), shaped((width, width), BF16), shaped((rows, width), BF16),
            shaped((rows, width), F32), shaped((slices - 1, up_part, chunk), BF16),
            shaped((slices - 1, down_part, width), BF16),
        ],
        in_specs=smem_spec(2) + vmem_spec(3) + any_spec(6),
        out_specs=vmem_spec(3) + any_spec(11),
        scratch_shapes=[
            vm(rows, width), vm(rows, width), vm(shards, 16, PAIR), vf(16, PAIR), vm(16, PAIR), vm(rows, width),
            vm(rows, 3 * width), vm(rows, width), vf(rows, width), vm(width, 3 * width), vm(width, width),
            vm(slices, width, chunk), vm(slices, chunk, width), vm(rows, PAIR), vf(rows, width), vf(rows, width),
            vm(slices - 1, up_part, chunk), vm(slices - 1, down_part, width),
        ]
        + scatter_scratch(slices, up_part, chunk, 2)
        + scatter_scratch(slices, down_part, width, 2)
        + dma((count, 17), (count, 17), (count,), (shards,), (shards,), (slices, 5), (slices, 5), (slices, 5),
              (slices, 5), (2,), (10 + rows // 256,)),
        compiler_params=pltpu.CompilerParams(
            vmem_limit_bytes=VMEM_LIMIT, collective_id=1, has_side_effects=True
        ),
    )(seq_lens, pass_idx, table, attn_gain, mlp_gain, inputs, cotangent, qkv, out, up, down)


class Column:
    def __init__(self, place, block, inward, middle, outward, total, sends, recvs, row):
        self.place, self.block, self.inward, self.middle = place, block, inward, middle
        self.outward, self.total = outward, total
        self.sends, self.recvs, self.row = sends, recvs, row
        self.end = (place.z == 0) | (place.z == 3)

    def copy(self, slot, src, dst, rep):
        return remote(src, dst, self.sends, self.recvs, (self.row, slot), (self.place.me, rep))

    def in_copy(self):
        return self.copy(0, self.block, self.inward, 1 + self.place.z // 3)

    def across_copy(self):
        return self.copy(1, self.middle, self.outward, 3 - self.place.z)

    def out_copy(self):
        return self.copy(2, self.total, self.outward, 3 * (self.place.z - 1))

    def begin(self):
        @pl.when(self.end)
        def _():
            self.in_copy().start()

    def cross(self):
        @pl.when(jnp.logical_not(self.end))
        def _():
            self.in_copy().wait_recv()
            self.middle[...] = (self.block[...].astype(F32) + self.inward[...].astype(F32)).astype(BF16)
            self.across_copy().start()

    def settle(self):
        @pl.when(jnp.logical_not(self.end))
        def _():
            self.across_copy().wait_recv()
            self.total[...] = (self.middle[...].astype(F32) + self.outward[...].astype(F32)).astype(BF16)
            self.out_copy().start()

    def finish(self):
        @pl.when(self.end)
        def _():
            self.out_copy().wait_recv()
            self.total[...] = self.outward[...]
            self.in_copy().wait_send()

        @pl.when(jnp.logical_not(self.end))
        def _():
            self.across_copy().wait_send()
            self.out_copy().wait_send()


def attention_columns(
    joined, log_rows, grads, joined_grad, key_bias, key_total, value_total, pair, block, between,
):
    rows = grads.shape[0]
    columns = pl.ds(pl.multiple_of(pair * PAIR, PAIR), PAIR)
    query_columns, key_columns, value_columns = pair_columns(pair)
    keys = joined[:, key_columns]
    values = joined[:, value_columns]
    bias = key_bias[...]
    biased = [key_with_bias(keys, bias, head) for head in range(2)]
    key_total[...] = jnp.zeros_like(key_total)
    value_total[...] = jnp.zeros_like(value_total)
    for first in range(0, rows, block):
        live = first + block
        query = joined[pl.ds(first, block), query_columns]
        grad = grads[pl.ds(first, block), columns]
        query_grad = None
        for head in range(2):
            asked, asked_only = query_with_bias(query, head)
            grad_only = head_only(grad, head)[0]
            scores = mm(biased[head][0][:live], asked, NT)
            share_grad = mm(values[:live], grad_only, NT)
            log_sum = log_rows[pl.ds(pair * 2 + head, 1), pl.ds(first, block)]
            shares = jnp.exp(scores - log_sum)
            key_at = lax.broadcasted_iota(jnp.int32, (block, block), 0)
            row_at = lax.broadcasted_iota(jnp.int32, (block, block), 1)
            last = jnp.where(key_at <= row_at, shares[first:], 0.0)
            shares = last if first == 0 else jnp.concatenate([shares[:first], last], axis=0)
            inner = jnp.sum(share_grad * shares, axis=0, keepdims=True)
            score_grad = (shares * (share_grad - inner)).astype(BF16)
            value_total[:live, :] += mm(shares.astype(BF16), grad_only)
            key_total[:live, :] += mm(score_grad, asked_only)
            part = mm(score_grad, biased[head][1][:live], TN)
            query_grad = part if query_grad is None else query_grad + part
        joined_grad[pl.ds(first, block), query_columns] = (query_grad * HEAD_DIM**-0.5).astype(BF16)
        if live == rows:
            joined_grad[:, key_columns] = key_total[...].astype(BF16)
            joined_grad[:, value_columns] = value_total[...].astype(BF16)
        if first // block % 2 == 1:
            between(first // block - 1)
            between(first // block)


def back_comm_kernel(
    block, tile,
    length_ref, pass_ref, rows_in, log_rows, mlp_gain_grad, up_done, down_done, up_half, down_half,
    hidden_grad_in, out_in, attended_in, normed_in, joined_in, qkv_in, inputs_in,
    grad_input_out, small_sum, up_total_out, down_total_out, attn_total,
    hidden_grad, out_w, attended, inputs, grad_input, up_total, down_total,
    qkv_w, joined, branch_grad, attended_grad, normed, joined_grad, key_bias, key_total, value_total,
    grads, first, in_x, in_y, last, block_sum,
    up_x, up_y, up_last, up_block, down_x, down_y, down_last, down_block,
    up_in, up_mid, up_out, down_in, down_mid, down_out, attn_in, attn_mid, attn_out,
    small_own, small_parts, small_slots, small_plane, small_reps,
    sends, recvs, up_sends, up_recvs, down_sends, down_recvs, z_sends, z_recvs,
    plane_sends, plane_recvs, rep_sends, rep_recvs, loads, saves,
):
    place = Place()
    rows, width = inputs.shape
    shards = small_slots.shape[0]
    reps = small_reps.shape[0]
    chunks = up_total.shape[0]
    pairs = width // PAIR
    others = [lax.rem(place.me + shift, shards) for shift in range(1, shards)]
    others_z = [lax.rem(place.z + shift, reps) for shift in range(1, reps)]
    take = [
        pltpu.make_async_copy(source, target, loads.at[index])
        for index, (source, target) in enumerate((
            (hidden_grad_in, hidden_grad), (out_in, out_w), (attended_in, attended), (joined_in, joined),
            (normed_in, normed), (qkv_in, qkv_w), (inputs_in, inputs),
        ))
    ]
    for copy in take:
        copy.start()
    enter(place, others, others_z)

    up_late = Scatter(place, None, up_half, up_x, up_y, up_last, up_sends, up_recvs, 0)
    down_late = Scatter(place, None, down_half, down_x, down_y, down_last, down_sends, down_recvs, 0)

    half = 3 * PAIR
    sent = [(0, 0, 2 * half), (1, 0, 2 * half), (2, 0, 2 * half), (3, 0, half), (3, half, half)]

    def message(index):
        slot, start, wide = sent[index]
        view = lambda ref: ref.at[(slot,) + (slice(None),) * (len(ref.shape) - 2) + (pl.ds(start, wide),)]
        return Scatter(
            place, view(grads), view(first), view(in_x), view(in_y), view(last), sends, recvs, index,
        )

    lines = {}

    def line(key, source, inward, middle, outward, total):
        lines[key] = Column(place, source, inward, middle, outward, total, z_sends, z_recvs, len(lines))

    for index in range(chunks):
        final = index == chunks - 1
        line(("d", index), down_block if final else down_done.at[index],
             down_in.at[index], down_mid.at[index], down_out.at[index], down_total.at[index])
        line(("u", index), up_block if final else up_done.at[index],
             up_in.at[index], up_mid.at[index], up_out.at[index], up_total.at[index])
    for index, (slot, start, wide) in enumerate(sent):
        line(("a", index), *(
            ref.at[slot, :, pl.ds(start, wide)] for ref in (block_sum, attn_in, attn_mid, attn_out, attn_total)
        ))

    down_late.spread()
    up_late.spread()
    for index in range(chunks - 1):
        lines["d", index].begin()
        lines["u", index].begin()

    fill_bias(length_ref[0], key_bias)
    take[0].wait()
    take[1].wait()

    @pl.loop(0, rows // tile)
    def _(step):
        at = pl.ds(step * tile, tile)
        shown = hidden_grad[at, :].astype(BF16)
        branch_grad[at, :] = shown
        attended_grad[at, :] = mm(shown, out_w[...], NT).astype(BF16)

    take[2].wait()
    grads[0] = mm(attended[...], branch_grad[...], TN).astype(BF16).reshape(grads.shape[1:])
    message(0).swap()
    lines["d", 0].cross()
    down_late.fold()
    take[3].wait()

    def late_close(late, target, key):
        late.close(target)
        lines[key].begin()

    def close(index):
        slot, start, wide = sent[index]
        message(index).close(block_sum.at[slot, :, pl.ds(start, wide)])
        lines["a", index].begin()

    def send(index):
        message(index).merge()
        message(index).spread()

    def fold(index):
        message(index).fold()

    def cross(*keys):
        for key in keys:
            lines[key[0], int(key[1])].cross()

    def settle(*keys):
        for key in keys:
            lines[key[0], int(key[1])].settle()

    def gradient(index):
        slot, start, wide = sent[index]
        columns = pl.ds((slot - 1) * 2 * half + start, wide)
        part = mm(normed[...], joined_grad[:, columns], TN).astype(BF16)
        grads[slot, :, :, :, :, pl.ds(start, wide)] = part.reshape(grads.shape[1:5] + (wide,))
        message(index).swap()

    plan = {
        (0, 1): lambda: send(0),
        (0, 2): lambda: (cross("u0"), up_late.fold()),
        (0, 3): lambda: late_close(down_late, down_block, ("d", 2)),
        (1, 0): lambda: settle("d0"),
        (1, 2): lambda: (cross("d1"), fold(0)),
        (1, 3): lambda: (late_close(up_late, up_block, ("u", 2)), settle("u0"), take[4].wait(), gradient(1)),
        (2, 0): lambda: (cross("u1"), close(0)),
        (2, 2): lambda: (send(1), settle("d1")),
        (2, 3): lambda: cross("d2"),
        (3, 2): lambda: (settle("u1"), cross("u2")),
        (3, 3): lambda: (fold(1), gradient(2)),
        (4, 0): lambda: (cross("a0"), settle("d2")),
        (4, 1): lambda: send(2),
        (4, 2): lambda: close(1),
        (4, 3): lambda: (settle("u2"), gradient(3)),
        (5, 0): lambda: fold(2),
        (5, 1): lambda: (send(3), settle("a0")),
        (5, 2): lambda: cross("a1"),
        (5, 3): lambda: (close(2), gradient(4), fold(3)),
    }

    @pl.loop(0, pairs)
    def _(pair):
        def between(place_at):
            for index in range(pairs):
                if (index, place_at) in plan:
                    @pl.when(pair == index)
                    def _(index=index):
                        plan[index, place_at]()

        attention_columns(
            joined, log_rows, attended_grad, joined_grad, key_bias, key_total, value_total, pair, block, between
        )

    small_own[...] = jnp.zeros_like(small_own)
    take[5].wait()
    take[6].wait()
    after_rows = [
        lambda: (send(4), settle("a1")),
        lambda: (close(3), cross("a2")),
        lambda: fold(4),
        lambda: cross("a3"),
    ]

    @pl.loop(0, rows // 256)
    def _(step):
        at = pl.ds(step * 256, 256)
        grad = mm(joined_grad[at, :], qkv_w[...], NT)
        unit, scale = norm_parts(inputs[at, :].astype(F32) + rows_in[0:1, :])
        total = hidden_grad[at, :] + norm_back(unit, scale, grad, rows_in[1:2, :])
        grad_input[at, :] = total
        small_own[5:6, :] += jnp.sum(grad * unit, axis=0, keepdims=True)
        small_own[0:1, :] += jnp.sum(total, axis=0, keepdims=True)
        pltpu.make_async_copy(grad_input.at[at, :], grad_input_out.at[at, :], saves.at[step]).start()
        for index in range(rows // 256):
            @pl.when(step == index)
            def _(index=index):
                after_rows[index]()

    places = lax.broadcasted_iota(jnp.int32, small_own.shape, 0)
    own = small_own[...]
    table = jnp.where((places == pass_ref[0]) & (places < 5), own[0:1], 0.0)
    own = jnp.where(places == 5, own, table)
    own = jnp.where(places == 6, mlp_gain_grad[0:1], own)
    part = width // shards
    small_parts[...] = jnp.zeros_like(small_parts)
    for shard in range(shards):
        small_parts[shard, :, 0:part] = own[:, shard * part : (shard + 1) * part]
    small_slots[place.me] = small_parts[place.me]
    plane_copies = [
        remote(small_parts.at[other], small_slots.at[place.me], plane_sends, plane_recvs, shift, place.at(other))
        for shift, other in enumerate(others)
    ]
    for copy in plane_copies:
        copy.start()
    close(4)
    settle("a2")
    early = [key for key in lines if key[0] != "a" or key[1] < 2]
    for key in early:
        lines[key].finish()
    give = [
        pltpu.make_async_copy(source, target, saves.at[rows // 256 + index])
        for index, (source, target) in enumerate(((up_total, up_total_out), (down_total, down_total_out)))
    ]
    for copy in give:
        copy.start()
    for copy in plane_copies:
        copy.wait_recv()
    total = small_slots[0]
    for shard in range(1, shards):
        total = total + small_slots[shard]
    small_plane[...] = total
    small_reps[place.z] = total
    rep_copies = [
        remote(small_plane, small_reps.at[place.z], rep_sends, rep_recvs, shift, (place.me, other))
        for shift, other in enumerate(others_z)
    ]
    for copy in rep_copies:
        copy.start()
    settle("a3")
    cross("a4")
    for copy in rep_copies:
        copy.wait_recv()
    total = small_reps[0]
    for rep in range(1, reps):
        total = total + small_reps[rep]
    small_sum[...] = total
    settle("a4")
    for key in lines:
        if key not in early:
            lines[key].finish()
    for copy in give:
        copy.wait()
    for index in range(len(sent)):
        message(index).drain()
    up_late.drain(swapped=False)
    down_late.drain(swapped=False)
    for copy in plane_copies + rep_copies:
        copy.wait_send()
    for step in range(rows // 256):
        at = pl.ds(step * 256, 256)
        pltpu.make_async_copy(grad_input.at[at, :], grad_input_out.at[at, :], saves.at[step]).wait()


def back_comm(reps, seq_lens, pass_idx, rows_in, log_rows, mlp_gain_grad, up_done, down_done, up_half, down_half,
              hidden_grad, out_w, attended, normed, joined, qkv_w, inputs):
    rows, width = inputs.shape
    _, _, up_part, chunk = up_half.shape
    down_part = down_half.shape[2]
    chunks = up_done.shape[0] + 1
    shards = width // up_part
    group = 4 * HEAD_DIM
    count = 1 + width // group
    wide = 3 * group
    vm = lambda *shape: pltpu.VMEM(shape, BF16)
    vf = lambda *shape: pltpu.VMEM(shape, F32)
    return pl.pallas_call(
        functools.partial(back_comm_kernel, 256, 512),
        out_shape=[
            shaped((rows, width), F32), shaped((8, PAIR), F32), shaped((chunks, up_part, chunk), BF16),
            shaped((chunks, down_part, width), BF16), shaped((count, up_part, wide), BF16),
        ],
        in_specs=smem_spec(2) + vmem_spec(7) + any_spec(7),
        out_specs=any_spec(1) + vmem_spec(1) + any_spec(2) + vmem_spec(1),
        scratch_shapes=[
            vf(rows, width), vm(width, width), vm(rows, width), vm(rows, width), vf(rows, width),
            vm(chunks, up_part, chunk), vm(chunks, down_part, width),
            vm(width, 3 * width), vm(rows, 3 * width), vm(rows, width), vm(rows, width), vm(rows, width),
            vm(rows, 3 * width), vm(rows, PAIR), vf(rows, PAIR), vf(rows, PAIR),
        ]
        + scatter_scratch(count, up_part, wide)
        + [
            vm(count, up_part, wide),
            vm(2, up_part // 2, chunk), vm(2, up_part // 2, chunk), vm(up_part, chunk), vm(up_part, chunk),
            vm(2, down_part // 2, width), vm(2, down_part // 2, width), vm(down_part, width), vm(down_part, width),
        ]
        + [vm(chunks, up_part, chunk)] * 3
        + [vm(chunks, down_part, width)] * 3
        + [vm(count, up_part, wide)] * 3
        + [vf(8, width), vf(shards, 8, PAIR), vf(shards, 8, PAIR), vf(8, PAIR), vf(reps, 8, PAIR)]
        + dma((count + 1, 5), (count + 1, 5), (1, 5), (1, 5), (1, 5), (1, 5), (2 * chunks + count + 1, 3),
              (2 * chunks + count + 1, 3),
              (shards - 1,), (shards - 1,), (reps - 1,), (reps - 1,), (7,), (rows // 256 + 2,)),
        compiler_params=pltpu.CompilerParams(
            vmem_limit_bytes=VMEM_LIMIT, collective_id=3, has_side_effects=True
        ),
    )(seq_lens, pass_idx, rows_in, log_rows, mlp_gain_grad, up_done, down_done, up_half, down_half,
      hidden_grad, out_w, attended, normed, joined, qkv_w, inputs)


def place_kernel(
    small_sum, outputs_in, grad_input_in, up_in, down_in, attn_in,
    table_out, attn_gain_out, mlp_gain_out, outputs_out, grad_input_out, qkv_out, out_out, up_out, down_out,
    outputs, grad_input, up_total, down_total, attn_total, qkv, out, up, down, loads, saves,
):
    slices, part, chunk = up_in.shape
    width = outputs.shape[1]
    shards = width // part
    lanes = chunk // shards
    take = [
        pltpu.make_async_copy(source, target, loads.at[index])
        for index, (source, target) in enumerate((
            (grad_input_in, grad_input), (up_in, up_total), (attn_in, attn_total), (down_in, down_total),
            (outputs_in, outputs),
        ))
    ]
    give = [
        pltpu.make_async_copy(source, target, saves.at[index])
        for index, (source, target) in enumerate((
            (grad_input, grad_input_out), (up, up_out), (qkv, qkv_out), (out, out_out), (down, down_out),
            (outputs, outputs_out),
        ))
    ]
    for copy in take:
        copy.start()
    table_out[...] = small_sum[0 : table_out.shape[0], 0:part]
    attn_gain_out[...] = small_sum[5:6, 0:part]
    mlp_gain_out[...] = small_sum[6:7, 0:part]
    take[0].wait()
    give[0].start()
    take[1].wait()
    for index in range(slices):
        for shard in range(shards):
            up[:, (slices * shard + index) * lanes : (slices * shard + index + 1) * lanes] = up_total[
                index, :, shard * lanes : (shard + 1) * lanes
            ].astype(F32)
    give[1].start()
    take[2].wait()
    for pair in range(width // PAIR):
        for plane in range(3):
            start = plane * width + pair * PAIR
            source = (3 * (pair % 2) + plane) * PAIR
            qkv[:, start : start + PAIR] = attn_total[1 + pair // 2, :, source : source + PAIR].astype(F32)
    out[...] = attn_total[0].astype(F32)
    give[2].start()
    give[3].start()
    take[3].wait()
    count = down_total.shape[1]
    for index in range(slices):
        down[index * count : (index + 1) * count, :] = down_total[index].astype(F32)
    give[4].start()
    take[4].wait()
    give[5].start()
    for copy in give:
        copy.wait()


def finish_places(passes, small_sum, outputs, grad_input, up_total, down_total, attn_total):
    rows, width = outputs.shape
    slices, part, chunk = up_total.shape
    down_rows = slices * down_total.shape[1]
    vf = lambda *shape: pltpu.VMEM(shape, F32)
    like = lambda ref: pltpu.VMEM(ref.shape, ref.dtype)
    return pl.pallas_call(
        place_kernel,
        out_shape=[
            shaped((passes, part), F32), shaped((1, part), F32), shaped((1, part), F32), shaped((rows, width), BF16),
            shaped((rows, width), F32), shaped((part, 3 * width), F32), shaped((part, width), F32),
            shaped((part, slices * chunk), F32), shaped((down_rows, width), F32),
        ],
        in_specs=vmem_spec(1) + any_spec(5),
        out_specs=vmem_spec(3) + any_spec(6),
        scratch_shapes=[
            like(outputs), like(grad_input), like(up_total), like(down_total), like(attn_total),
            vf(part, 3 * width), vf(part, width), vf(part, slices * chunk), vf(down_rows, width),
        ]
        + dma((5,), (6,)),
        compiler_params=pltpu.CompilerParams(vmem_limit_bytes=VMEM_LIMIT),
    )(small_sum, outputs, grad_input, up_total, down_total, attn_total)


def direct(reps, inputs, seq_lens, pass_idx, pass_table, gain_attn, w_qkv, w_out, gain_mlp, w_up, w_down, cotangent):
    slices = 3
    (
        rows_in, log_rows, mlp_gain_grad, up_half, down_half,
        normed, joined, attended, qkv_w, out_w, outputs, hidden_grad, up_done, down_done,
    ) = fore_comm(
        slices, seq_lens, pass_idx, pass_table, gain_attn[None], gain_mlp[None], inputs[0], cotangent[0], w_qkv, w_out,
        w_up, w_down,
    )
    grad_input, small_sum, up_total, down_total, attn_total = back_comm(
        reps, seq_lens, pass_idx, rows_in, log_rows, mlp_gain_grad, up_done, down_done, up_half, down_half,
        hidden_grad, out_w, attended, normed, joined, qkv_w, inputs[0],
    )
    table, attn_gain, mlp_gain, outputs, grad_input, qkv, out, up, down = finish_places(
        pass_table.shape[0], small_sum, outputs, grad_input, up_total, down_total, attn_total
    )
    return (outputs[None], grad_input[None], table, attn_gain[0], qkv, out, mlp_gain[0], up, down)


def solution(mesh):
    shards, reps = mesh.shape["shard"], mesh.shape["rep"]
    run = functools.partial(direct, reps) if (shards, reps) == (8, 4) else body
    part = P(("shard", "rep"), None, None)
    return jax.shard_map(
        run,
        mesh=mesh,
        in_specs=(
            part, P(("shard", "rep")), P(("shard", "rep")), P(None, "shard"), P("shard"), P("shard", None),
            P("shard", None), P("shard"), P("shard", None), P("shard", None), part,
        ),
        out_specs=(
            part, part, P(None, "shard"), P("shard"), P("shard", None), P("shard", None), P("shard"),
            P("shard", None), P("shard", None),
        ),
        check_vma=False,
    )
```
